32 devices in a mesh: grp: 2 (over x), seq: 16 (over z, y, core).
Axes of the slice: x: 2, y: 2, z: 4, core: 2. Of those that a mesh axis runs over, the one named last changes fastest.
Arguments:
- alignment: bfloat16 [64, 128, 768], P(('grp', 'seq')), parts along dimension 0, may hold values from -20 to 20
- protein_id: int32 [256], P('grp'), parts along dimension 0, may hold values from 0 to 3, never falling along the last dimension, each value on 1 to 64 neighbouring positions
- row_depth: int32 [8], P('grp'), parts along dimension 0, may hold values from 8 to 32, as said below
- row_gain: float32 [768], replicated, may hold values from 0.1 to 1.9
- row_query: bfloat16 [768, 768], replicated, may hold values from -40 to 40
- row_key: bfloat16 [768, 768], replicated, may hold values from -0.21875 to 0.21875
- row_value: bfloat16 [768, 768], replicated, may hold values from -0.21875 to 0.21875
- row_output: bfloat16 [768, 768], replicated, may hold values from -0.21875 to 0.21875
- column_gain: float32 [768], replicated, may hold values from 0.1 to 1.9
- column_query: bfloat16 [768, 768], replicated, may hold values from -40 to 40
- column_key: bfloat16 [768, 768], replicated, may hold values from -0.21875 to 0.21875
- column_value: bfloat16 [768, 768], replicated, may hold values from -0.21875 to 0.21875
- column_output: bfloat16 [768, 768], replicated, may hold values from -0.21875 to 0.21875
Outputs:
- layer_out: bfloat16 [64, 128, 768], P(('grp', 'seq')), parts along dimension 0
The draws below stay inside these ranges and needn't reach their ends.
There are 2 independent parts, one for each index of `grp`. The reference program is written for one: setup_inputs(seed, part) draws one part's arguments, and reference() takes and returns one part's arrays. A program takes and returns all parts, laid end to end along the dimension named above; an argument that names none is the same for every part. Nothing has to cross between parts.
Inputs may be any that keep to these rules, and one draw needn't show every extreme that they name: `row_depth`: row 0 is real for every protein; one protein of each pack has all 32 rows real. `protein_id`: proteins occupy contiguous column ranges in order, each 1 to 64 columns.
All inputs are finite; a program needn't handle non-finite values.
Results may differ from the reference program's by a relative error of at most 0.011.
Values may be sent and summed in bfloat16 or wider, within the bound.
No kernel may reach another device: no remote copies, remote signals or barrier semaphores. Data moves between devices by JAX's collectives and lax.ppermute only.
A program may use at most 64 MiB of HBM per device.

```python
import math
import jax
import jax.numpy as jnp
import numpy as np
from jax import lax

D = 768
H = 12
HD = 64
C = 128
PROT = 4
R = 32


def draw_alignment(key, part):
    base = jax.random.normal(jax.random.fold_in(key, 11), (R, C, D), jnp.float32)
    return jnp.clip(base, -20.0, 20.0).astype(jnp.bfloat16)


def draw_row_depth(key, part):
    lowest = max(1, R // 4)
    depths = jax.random.randint(jax.random.fold_in(key, 21), (PROT,), lowest, R + 1, jnp.int32)
    full_one = jax.random.randint(jax.random.fold_in(key, 22), (), 0, PROT, jnp.int32)
    return jnp.where(jnp.arange(PROT, dtype=jnp.int32) == full_one, R, depths).astype(jnp.int32)


def query_weights(key):
    sampled = jax.random.normal(jax.random.fold_in(key, 1), (D, D), jnp.float32) / math.sqrt(D)
    return jnp.clip(sampled, -40.0, 40.0).astype(jnp.bfloat16)


def draw_row_query(key, part):
    return query_weights(jax.random.fold_in(key, 31))


def draw_column_query(key, part):
    return query_weights(jax.random.fold_in(key, 41))


def split_up(amount, total, limit, slope):
    portions = [(1 << 20) // math.isqrt(rank ** slope) + 1 for rank in range(2, amount + 1)]
    surplus, given = total - limit - (amount - 1), [1] * (amount - 1)
    while surplus > 0:
        candidates = [i for i in range(amount - 1) if given[i] < limit]
        mass, left = sum([portions[i] for i in candidates]), surplus
        for i in candidates:
            more = min(limit - given[i], max(1, left * portions[i] // mass), surplus)
            given[i] = given[i] + more
            surplus = surplus - more
    return np.array([limit] + given)


def uneven(rng, number_of, total, most, slope):
    if number_of == 2:
        one = jax.random.randint(rng, (), max(1, total - most), min(most, total - 1) + 1)
        return jnp.stack([one, total - one])
    lengths = jnp.asarray(split_up(number_of, total, most, slope), jnp.int32)
    pairs = (number_of - 1) // 2
    donor, sink = lengths[1:1 + 2 * pairs:2], lengths[2:2 + 2 * pairs:2]
    slack = jnp.minimum(donor - 1, most - sink)
    moved = jax.random.randint(jax.random.fold_in(rng, 1), (pairs,), 0, 1 << 20) % (slack + 1)
    lengths = lengths.at[1:1 + 2 * pairs:2].set(donor - moved).at[2:2 + 2 * pairs:2].set(sink + moved)
    return lengths[jax.random.permutation(jax.random.fold_in(rng, 2), number_of)]


def noise(rng, extent, deviation, limit, kind=jnp.bfloat16):
    return jnp.clip(deviation * jax.random.normal(rng, extent, jnp.float32), -limit, limit).astype(kind)


def setup_inputs(seed: int = 0, part: int = 0) -> dict:
    splits = jax.random.split(jax.random.key(seed), 14)
    part_splits = jax.random.split(jax.random.fold_in(splits[13], part), 14)
    alignment = draw_alignment(jax.random.fold_in(jax.random.fold_in(splits[13], part), 71), part)
    protein_id = jnp.searchsorted(jnp.cumsum(uneven(part_splits[1], PROT, C, C // 2, 0)), jnp.arange(C), side="right").astype(jnp.int32)
    row_depth = draw_row_depth(jax.random.fold_in(jax.random.fold_in(splits[13], part), 71), part)
    row_gain = jnp.clip(1.0 + 0.18 * jax.random.normal(splits[3], (D,), jnp.float32), 0.1, 1.9)
    row_query = draw_row_query(jax.random.fold_in(splits[13], 71), part)
    row_key = noise(splits[5], (D, D), D ** -0.5, 0.21875)
    row_value = noise(splits[6], (D, D), D ** -0.5, 0.21875)
    row_output = noise(splits[7], (D, D), D ** -0.5, 0.21875)
    column_gain = jnp.clip(1.0 + 0.18 * jax.random.normal(splits[8], (D,), jnp.float32), 0.1, 1.9)
    column_query = draw_column_query(jax.random.fold_in(splits[13], 71), part)
    column_key = noise(splits[10], (D, D), D ** -0.5, 0.21875)
    column_value = noise(splits[11], (D, D), D ** -0.5, 0.21875)
    column_output = noise(splits[12], (D, D), D ** -0.5, 0.21875)
    return dict(alignment=alignment, protein_id=protein_id, row_depth=row_depth, row_gain=row_gain, row_query=row_query, row_key=row_key, row_value=row_value, row_output=row_output, column_gain=column_gain, column_query=column_query, column_key=column_key, column_value=column_value, column_output=column_output)


def layer_norm(values, gain):
    full = values.astype(jnp.float32)
    middle = lax.optimization_barrier(jnp.mean(full, axis=-1, keepdims=True))
    spread = lax.optimization_barrier(jnp.mean((full - middle) ** 2, axis=-1, keepdims=True))
    return ((full - middle) * lax.rsqrt(spread + 1e-05) * gain.astype(jnp.float32)).astype(jnp.bfloat16)

def project(normed, weight):
    shape = normed.shape
    flattened = normed.reshape(-1, shape[-1])
    return jnp.dot(flattened, weight, preferred_element_type=jnp.float32).astype(jnp.bfloat16).reshape(shape[:-1] + (weight.shape[1],))

def column_depth(protein_id, row_depth):
    onehot = protein_id[:, None] == jnp.arange(row_depth.shape[0], dtype=jnp.int32)[None, :]
    return lax.optimization_barrier(jnp.sum(jnp.where(onehot, row_depth[None, :], 0), axis=1)).astype(jnp.int32)

def reference(alignment, protein_id, row_depth, row_gain, row_query, row_key, row_value, row_output, column_gain, column_query, column_key, column_value, column_output):
    depth_col = column_depth(protein_id, row_depth)
    valid = jnp.arange(R, dtype=jnp.int32)[:, None] < depth_col[None, :]
    mask_bf = valid.astype(jnp.bfloat16)[:, :, None]
    normed_row = layer_norm(alignment, row_gain)
    query_a = project(normed_row, row_query) * mask_bf
    key_a = project(normed_row, row_key) * mask_bf
    value_a = project(normed_row, row_value)
    query_h = query_a.reshape(R, C, H, HD).transpose(2, 0, 1, 3)
    key_h = key_a.reshape(R, C, H, HD).transpose(2, 0, 1, 3)
    value_h = value_a.reshape(R, C, H, HD).transpose(2, 0, 1, 3)
    same_prot = protein_id[:, None] == protein_id[None, :]
    scale = 1.0 / (math.sqrt(HD) * math.sqrt(R))

    def one_head(operands):
        query_one, key_one, value_one = operands
        tied = jnp.einsum('rie,rje->ij', query_one.astype(jnp.float32), key_one.astype(jnp.float32)) * scale
        tied = jnp.where(same_prot, tied, -1000000000.0)
        weights = jax.nn.softmax(tied, axis=-1).astype(jnp.bfloat16)
        mixed = jnp.einsum('ij,rje->rie', weights.astype(jnp.float32), value_one.astype(jnp.float32))
        return mixed.astype(jnp.bfloat16)
    row_mixed = lax.map(one_head, (query_h, key_h, value_h))
    row_mixed = row_mixed.transpose(1, 2, 0, 3).reshape(R, C, D)
    after_row = (alignment.astype(jnp.float32) + jnp.dot(row_mixed.reshape(-1, D), row_output, preferred_element_type=jnp.float32).reshape(R, C, D)).astype(jnp.bfloat16)
    normed_col = layer_norm(after_row, column_gain)
    query_b = project(normed_col, column_query)
    key_b = project(normed_col, column_key)
    value_b = project(normed_col, column_value)
    block = math.gcd(C, 16)
    count = C // block

    def regroup(values):
        return values.reshape(R, count, block, H, HD).transpose(1, 2, 3, 0, 4)
    key_valid = valid.transpose(1, 0).reshape(count, block, R)

    def one_block(operands):
        query_one, key_one, value_one, valid_one = operands
        scores = jnp.einsum('chre,chse->chrs', query_one.astype(jnp.float32), key_one.astype(jnp.float32)) / math.sqrt(HD)
        scores = jnp.where(valid_one[:, None, None, :], scores, -1000000000.0)
        weights = jax.nn.softmax(scores, axis=-1).astype(jnp.bfloat16)
        return jnp.einsum('chrs,chse->chre', weights.astype(jnp.float32), value_one.astype(jnp.float32)).astype(jnp.bfloat16)
    col_mixed = lax.map(one_block, (regroup(query_b), regroup(key_b), regroup(value_b), key_valid))
    col_mixed = col_mixed.transpose(3, 0, 1, 2, 4).reshape(R, C, D)
    layer_out = after_row.astype(jnp.float32) + jnp.dot(col_mixed.reshape(-1, D), column_output, preferred_element_type=jnp.float32).reshape(R, C, D)
    return layer_out.astype(jnp.bfloat16)
```

```python
import math

import jax
import jax.numpy as jnp
from jax import lax
from jax.sharding import PartitionSpec as P

H = 12


def layer_norm(values, gain):
    full = values.astype(jnp.float32)
    middle = jnp.mean(full, axis=-1, keepdims=True)
    spread = jnp.mean((full - middle) ** 2, axis=-1, keepdims=True)
    return ((full - middle) * lax.rsqrt(spread + 1e-05) * gain).astype(jnp.bfloat16)


def project(normed, weight):
    shape = normed.shape
    flattened = normed.reshape(-1, shape[-1])
    return (
        jnp.dot(flattened, weight, preferred_element_type=jnp.float32)
        .astype(jnp.bfloat16)
        .reshape(shape[:-1] + (weight.shape[1],))
    )


def column_depth(protein_id, row_depth):
    onehot = protein_id[:, None] == jnp.arange(row_depth.shape[0], dtype=jnp.int32)[None, :]
    return jnp.sum(jnp.where(onehot, row_depth[None, :], 0), axis=1)


def per_device(
    alignment,
    protein_id,
    row_depth,
    row_gain,
    row_query,
    row_key,
    row_value,
    row_output,
    column_gain,
    column_query,
    column_key,
    column_value,
    column_output,
):
    rows_dev, columns, width = alignment.shape
    devices = lax.axis_size("seq")
    position = lax.axis_index("seq")
    total_rows = rows_dev * devices
    head_count = H
    head_size = width // head_count
    tile_cols = columns // devices
    depth_col = column_depth(protein_id, row_depth)
    row_ids = position * rows_dev + jnp.arange(rows_dev, dtype=jnp.int32)
    valid = row_ids[:, None] < depth_col[None, :]
    mask_bf = valid.astype(jnp.bfloat16)[:, :, None]
    normed_row = layer_norm(alignment, row_gain)
    query_a = (project(normed_row, row_query) * mask_bf).reshape(
        rows_dev, columns, head_count, head_size
    )
    key_a = (project(normed_row, row_key) * mask_bf).reshape(
        rows_dev, columns, head_count, head_size
    )
    value_a = project(normed_row, row_value).reshape(rows_dev, columns, head_count, head_size)
    scale = 1.0 / (math.sqrt(head_size) * math.sqrt(total_rows))
    fold = columns // 2
    partial = jnp.einsum("rihe,rjhe->ihj", query_a, key_a, preferred_element_type=jnp.float32)
    same = protein_id[:, None] == protein_id[None, :]
    folded = jnp.where(same[:, None, :fold], partial[..., :fold], partial[..., fold:])
    blocks = lax.all_to_all(
        folded.reshape(devices, tile_cols, head_count * fold),
        "seq",
        split_axis=0,
        concat_axis=0,
        tiled=True,
    )
    tied = jnp.sum(blocks, axis=0).reshape(tile_cols, head_count, fold) * scale
    same_tile = lax.dynamic_slice_in_dim(same, position * tile_cols, tile_cols, 0)
    same_folded = same_tile[:, :fold] | same_tile[:, fold:]
    tied = jnp.where(same_folded[:, None, :], tied, -1000000000.0)
    row_weights = jax.nn.softmax(tied, axis=-1).astype(jnp.bfloat16)
    gathered = lax.all_to_all(
        jnp.broadcast_to(
            row_weights.reshape(1, tile_cols, head_count * fold),
            (devices, tile_cols, head_count * fold),
        ),
        "seq",
        split_axis=0,
        concat_axis=0,
        tiled=True,
    ).reshape(columns, head_count, fold)
    weights = jnp.where(
        same[:, None, :], jnp.concatenate([gathered, gathered], axis=-1), jnp.bfloat16(0)
    )
    row_mixed = (
        jnp.einsum("ihj,rjhe->rihe", weights, value_a, preferred_element_type=jnp.float32)
        .astype(jnp.bfloat16)
        .reshape(rows_dev, columns, width)
    )
    after_row = (
        alignment.astype(jnp.float32)
        + jnp.dot(
            row_mixed.reshape(-1, width), row_output, preferred_element_type=jnp.float32
        ).reshape(rows_dev, columns, width)
    ).astype(jnp.bfloat16)
    normed_col = layer_norm(after_row, column_gain)
    moved = lax.all_to_all(normed_col, "seq", split_axis=1, concat_axis=0, tiled=True)
    query_b = project(moved, column_query)
    key_b = project(moved, column_key)
    value_b = project(moved, column_value)
    query_b = query_b.reshape(total_rows, tile_cols, head_count, head_size)
    key_b = key_b.reshape(total_rows, tile_cols, head_count, head_size)
    value_b = value_b.reshape(total_rows, tile_cols, head_count, head_size)
    depth_tile = lax.dynamic_slice_in_dim(depth_col, position * tile_cols, tile_cols, 0)
    key_valid = jnp.arange(total_rows, dtype=jnp.int32)[None, :] < depth_tile[:, None]
    col_scores = jnp.einsum(
        "rche,sche->chrs", query_b, key_b, preferred_element_type=jnp.float32
    ) / math.sqrt(head_size)
    col_scores = jnp.where(key_valid[:, None, None, :], col_scores, -1000000000.0)
    col_weights = jax.nn.softmax(col_scores, axis=-1).astype(jnp.bfloat16)
    col_mixed = jnp.einsum(
        "chrs,sche->rche", col_weights, value_b, preferred_element_type=jnp.float32
    ).astype(jnp.bfloat16)
    col_mixed = col_mixed.reshape(total_rows, tile_cols, width)
    returned = lax.all_to_all(col_mixed, "seq", split_axis=0, concat_axis=1, tiled=True)
    layer_out = after_row.astype(jnp.float32) + jnp.dot(
        returned.reshape(-1, width), column_output, preferred_element_type=jnp.float32
    ).reshape(rows_dev, columns, width)
    return layer_out.astype(jnp.bfloat16)


def solution(mesh):
    return jax.shard_map(
        per_device,
        mesh=mesh,
        in_specs=(
            P(("grp", "seq"), None, None),
            P("grp"),
            P("grp"),
            P(),
            P(),
            P(),
            P(),
            P(),
            P(),
            P(),
            P(),
            P(),
            P(),
        ),
        out_specs=P(("grp", "seq"), None, None),
        check_vma=False,
    )
```

```python
import functools
import math

import jax
import jax.numpy as jnp
from jax import lax
from jax.experimental import pallas as pl
from jax.experimental.pallas import tpu as pltpu
from jax.sharding import PartitionSpec as P

H = 12
EPS = 1e-05
NEG = -1000000000.0
F32 = jnp.float32
BF16 = jnp.bfloat16
LIMIT = 48 << 20


def call(kernel, out_shape, ins, outs, scratch, cost, name):
    spaces = {"v": pltpu.VMEM, "s": pltpu.SMEM, "a": pl.ANY}
    return pl.pallas_call(
        kernel,
        out_shape=out_shape,
        in_specs=[pl.BlockSpec(memory_space=spaces[c]) for c in ins],
        out_specs=[pl.BlockSpec(memory_space=spaces[c]) for c in outs],
        scratch_shapes=scratch,
        compiler_params=pltpu.CompilerParams(vmem_limit_bytes=LIMIT),
        cost_estimate=pl.CostEstimate(flops=cost[0], bytes_accessed=cost[1], transcendentals=cost[2]),
        name=name,
    )


def norm(full, gain):
    middle = jnp.mean(full, axis=-1, keepdims=True)
    spread = jnp.mean((full - middle) ** 2, axis=-1, keepdims=True)
    return (full - middle) * lax.rsqrt(spread + EPS) * gain


def dot(a, b):
    return jnp.dot(a, b, preferred_element_type=F32)


def dot_t(a, b):
    return lax.dot_general(a, b, (((1,), (1,)), ((), ())), preferred_element_type=F32)


def iota(shape, dim):
    return lax.broadcasted_iota(jnp.int32, shape, dim)


def to_column(row, size):
    eye = iota((size, size), 0) == iota((size, size), 1)
    return jnp.sum(jnp.where(eye, jnp.broadcast_to(row, (size, size)), 0.0), axis=1, keepdims=True)


def half_masks(width):
    low = (iota((1, width), 1) % 128) < 64
    return jnp.where(low, 1.0, 0.0), jnp.where(low, 0.0, 1.0)


def row_scores_kernel(
    depth_ref, place_ref, x_ref, gain_ref, prot_ref, wq_ref, wk_ref, part_ref, normed_ref, same_ref
):
    columns = prot_ref.shape[1]
    tokens, width = x_ref.shape
    rows = tokens // columns
    normed = norm(x_ref[...].astype(F32), gain_ref[...]).astype(BF16)
    normed_ref[...] = normed
    prot = prot_ref[...].astype(F32)
    depth = jnp.zeros((1, columns), F32)
    for p in range(depth_ref.shape[0]):
        depth = jnp.where(prot == float(p), depth_ref[p].astype(F32), depth)
    prot_col = to_column(prot, columns)
    depth_col = to_column(depth, columns)
    same = jnp.broadcast_to(prot_col, (columns, columns)) == jnp.broadcast_to(prot, (columns, columns))
    same_f = jnp.where(same, 1.0, 0.0)
    same_ref[...] = same_f
    low = iota((columns, columns), 1) < 64
    first = jnp.where(low, same_f, pltpu.roll(same_f, 64, 1)) > 0.5
    valid = [
        jnp.where((place_ref[0] * rows + r).astype(F32) < depth_col, 1.0, 0.0) for r in range(rows)
    ]
    valid = jnp.concatenate(valid, axis=0)
    even, odd = half_masks(256)
    for n in range(width // 256):
        cols = slice(256 * n, 256 * n + 256)
        query = dot(normed, wq_ref[:, cols]).astype(BF16).astype(F32) * valid
        key = (dot(normed, wk_ref[:, cols]) * valid).astype(BF16)
        query_even, query_odd = (query * even).astype(BF16), (query * odd).astype(BF16)
        for q in range(2):
            lanes = slice(128 * q, 128 * q + 128)

            def side(array, lanes=lanes):
                return jnp.concatenate(
                    [array[r * columns : (r + 1) * columns, lanes] for r in range(rows)], axis=1
                )

            both = jnp.concatenate([side(query_even), side(query_odd)], axis=0)
            logits = dot_t(both, side(key))
            one, two = logits[:columns], logits[columns:]
            folded = jnp.where(
                low,
                jnp.where(first, one, pltpu.roll(one, 64, 1)),
                jnp.where(first, pltpu.roll(two, 64, 1), two),
            )
            part_ref[:, 256 * n + 128 * q : 256 * n + 128 * q + 128] = folded


def project_kernel(x_ref, w_ref, out_ref):
    out_ref[...] = dot(x_ref[...], w_ref[...]).astype(BF16)


def row_softmax_kernel(scale, place_ref, blocks_ref, same_ref, out_ref, mask_ref):
    devices, tile, width = blocks_ref.shape
    same = same_ref[...]
    mask_ref[...] = jnp.maximum(same, pltpu.roll(same, 64, 1))
    live = mask_ref[pl.ds(place_ref[0] * tile, tile), :] > 0.5
    low = iota((tile, 128), 1) < 64
    total = blocks_ref[0]
    for d in range(1, devices):
        total = total + blocks_ref[d]
    pieces = []
    for p in range(width // 128):
        tied = jnp.where(live, total[:, 128 * p : 128 * p + 128] * scale, NEG)
        top_low = jnp.max(jnp.where(low, tied, 2 * NEG), axis=1, keepdims=True)
        top_high = jnp.max(jnp.where(low, 2 * NEG, tied), axis=1, keepdims=True)
        value = jnp.exp(tied - jnp.where(low, top_low, top_high))
        sum_low = jnp.sum(jnp.where(low, value, 0.0), axis=1, keepdims=True)
        sum_high = jnp.sum(jnp.where(low, 0.0, value), axis=1, keepdims=True)
        pieces.append(value / jnp.where(low, sum_low, sum_high))
    out_ref[...] = jnp.broadcast_to(
        jnp.concatenate(pieces, axis=1).astype(BF16)[None], (devices, tile, width)
    )


def row_output_kernel(
    folded_ref, same_ref, value_ref, x_ref, w_ref, gain_ref, after_ref, normed_ref, mixed_ref
):
    columns = same_ref.shape[0]
    tokens, width = x_ref.shape
    rows = tokens // columns
    folded = folded_ref[...].reshape(columns, width).astype(F32)
    same = same_ref[...] > 0.5
    low = iota((columns, columns), 1) < 64
    even, odd = half_masks(128 * rows)
    even, odd = even.astype(BF16), odd.astype(BF16)
    for p in range(width // 128):
        lanes = slice(128 * p, 128 * p + 128)
        piece = folded[:, lanes]
        turned = pltpu.roll(piece, 64, 1)
        one = jnp.where(same, jnp.where(low, piece, turned), 0.0)
        two = jnp.where(same, jnp.where(low, turned, piece), 0.0)
        weights = jnp.concatenate([one, two], axis=1).astype(BF16)
        value = jnp.concatenate(
            [value_ref[r * columns : (r + 1) * columns, lanes] for r in range(rows)], axis=1
        )
        value = jnp.concatenate([value * even, value * odd], axis=0)
        mixed = dot(weights, value).astype(BF16)
        for r in range(rows):
            mixed_ref[r * columns : (r + 1) * columns, lanes] = mixed[:, 128 * r : 128 * r + 128]
    after = (x_ref[...].astype(F32) + dot(mixed_ref[...], w_ref[...])).astype(BF16)
    after_ref[...] = after
    normed = norm(after.astype(F32), gain_ref[...])
    if len(normed_ref.shape) == 2:
        normed_ref[...] = normed.astype(BF16)
    else:
        devices, _, tile, _ = normed_ref.shape
        for d in range(devices):
            for r in range(rows):
                start = r * columns + d * tile
                normed_ref[d, r] = normed[start : start + tile].astype(BF16)


def column_kernel(scale, tile, depth_ref, prot_ref, place_ref, x_ref, wq_ref, wk_ref, wv_ref, out_ref):
    tokens, width = x_ref.shape
    x = x_ref[...]
    lane = iota((1, tokens), 1)
    depth = jnp.zeros((1, tokens), jnp.int32)
    for c in range(tile):
        depth = jnp.where(lane % tile == c, depth_ref[prot_ref[place_ref[0] * tile + c]], depth)
    live = (iota((tokens, tokens), 0) % tile == iota((tokens, tokens), 1) % tile) & (
        iota((tokens, tokens), 1) // tile < depth
    )
    even, odd = half_masks(256)
    for n in range(width // 256):
        cols = slice(256 * n, 256 * n + 256)
        query = dot(x, wq_ref[:, cols]).astype(BF16).astype(F32)
        key = dot(x, wk_ref[:, cols]).astype(BF16)
        value = dot(x, wv_ref[:, cols])
        query_sides = [(query * side).astype(BF16) for side in (even, odd)]
        value_sides = [(value * side).astype(BF16) for side in (even, odd)]
        for q in range(2):
            lanes = slice(128 * q, 128 * q + 128)
            mixed = jnp.zeros((tokens, 128), F32)
            for s in range(2):
                scores = dot_t(query_sides[s][:, lanes], key[:, lanes]) * scale
                scores = jnp.where(live, scores, NEG)
                top = jnp.max(scores, axis=1, keepdims=True)
                weight = jnp.exp(scores - top)
                weight = weight / jnp.sum(weight, axis=1, keepdims=True)
                mixed = mixed + dot(weight.astype(BF16), value_sides[s][:, lanes])
            out_ref[:, 256 * n + 128 * q : 256 * n + 128 * q + 128] = mixed.astype(BF16)


def column_output_kernel(x_ref, w_ref, after_ref, out_ref, total_ref):
    rows, columns, width = out_ref.shape
    if len(x_ref.shape) == 2:
        total = dot(x_ref[...], w_ref[...]) + after_ref[...].astype(F32)
        out_ref[...] = total.astype(BF16).reshape(rows, columns, width)
    else:
        devices, _, tile, _ = x_ref.shape
        total = dot(x_ref[...].reshape(rows * columns, width), w_ref[...])
        for d in range(devices):
            for r in range(rows):
                start, block = r * columns + d * tile, (d * rows + r) * tile
                total_ref[start : start + tile] = total[block : block + tile]
        total = total_ref[...] + after_ref[...].astype(F32)
        out_ref[...] = total.astype(BF16).reshape(rows, columns, width)


def exchange(array):
    return lax.all_to_all(array, "seq", split_axis=0, concat_axis=0, tiled=True)


def per_device(
    alignment,
    protein_id,
    row_depth,
    row_gain,
    row_query,
    row_key,
    row_value,
    row_output,
    column_gain,
    column_query,
    column_key,
    column_value,
    column_output,
):
    rows, columns, width = alignment.shape
    devices = lax.axis_size("seq")
    place = lax.axis_index("seq").astype(jnp.int32)[None]
    total_rows = rows * devices
    head_size = width // H
    tile = columns // devices
    tokens = rows * columns
    blocked = tile % 8 == 0
    x = alignment.reshape(tokens, width)
    shape = jax.ShapeDtypeStruct
    square = 2 * tokens * width * width

    partial, normed, same = call(
        row_scores_kernel,
        (shape((columns, width), F32), shape((tokens, width), BF16), shape((columns, columns), F32)),
        "ssvvvvv",
        "vvv",
        [],
        (2 * square, 4 * width * width, tokens),
        "row_scores",
    )(row_depth, place, x, row_gain[None], protein_id[None], row_query, row_key)
    blocks = exchange(partial.reshape(devices, tile, width))
    (value,) = call(
        project_kernel, (shape((tokens, width), BF16),), "vv", "v", [], (square, 2 * width * width, 0), "row_value"
    )(normed, row_value)
    (weights,) = call(
        functools.partial(row_softmax_kernel, 1.0 / (math.sqrt(head_size) * math.sqrt(total_rows))),
        (shape((devices, tile, width), BF16),),
        "svv",
        "v",
        [pltpu.VMEM((columns, columns), F32)],
        (columns * width, 6 * columns * width, tile * width),
        "row_softmax",
    )(place, blocks, same)
    folded = exchange(weights)
    normed_shape = (devices, rows, tile, width) if blocked else (tokens, width)
    after, normed = call(
        row_output_kernel,
        (shape((tokens, width), BF16), shape(normed_shape, BF16)),
        "vvvvvv",
        "vv",
        [pltpu.VMEM((tokens, width), BF16)],
        (square, 2 * width * width, tokens),
        "row_output",
    )(folded, same, value, x, row_output, column_gain[None])
    if not blocked:
        normed = normed.reshape(rows, devices, tile, width).transpose(1, 0, 2, 3)
    moved = exchange(normed).reshape(tokens, width)
    (mixed,) = call(
        functools.partial(column_kernel, 1.0 / math.sqrt(head_size), tile),
        (shape((tokens, width), BF16),),
        "sssvvvv",
        "v",
        [],
        (4 * square, 6 * width * width, H * tokens * tokens),
        "column_attention",
    )(row_depth, protein_id, place, moved, column_query, column_key, column_value)
    returned = exchange(mixed.reshape(devices, rows, tile, width))
    if not blocked:
        returned = returned.transpose(1, 0, 2, 3).reshape(tokens, width)
    (out,) = call(
        column_output_kernel,
        (shape((rows, columns, width), BF16),),
        "vvv",
        "v",
        [pltpu.VMEM((tokens, width), F32)],
        (square, 2 * width * width, 0),
        "column_output",
    )(returned, column_output, after)
    return out


def solution(mesh):
    return jax.shard_map(
        per_device,
        mesh=mesh,
        in_specs=(P(("grp", "seq"), None, None), P("grp"), P("grp")) + (P(),) * 10,
        out_specs=P(("grp", "seq"), None, None),
        check_vma=False,
    )
```

```python
import functools
import math

import jax
import jax.numpy as jnp
from jax import lax
from jax.experimental import pallas as pl
from jax.experimental.pallas import tpu as pltpu
from jax.sharding import PartitionSpec as P

H = 12
EPS = 1e-05
NEG = -1000000000.0
F32 = jnp.float32
BF16 = jnp.bfloat16
LIMIT = 20 << 20
LARGE = 56 << 20
PLANE = 4


def call(kernel, out_shape, ins, outs, scratch, cost, name, limit=LIMIT):
    spaces = {"v": pltpu.VMEM, "s": pltpu.SMEM, "a": pl.ANY}
    return pl.pallas_call(
        kernel,
        out_shape=out_shape,
        in_specs=[pl.BlockSpec(memory_space=spaces[c]) for c in ins],
        out_specs=[pl.BlockSpec(memory_space=spaces[c]) for c in outs],
        scratch_shapes=scratch,
        compiler_params=pltpu.CompilerParams(vmem_limit_bytes=limit),
        cost_estimate=pl.CostEstimate(flops=cost[0], bytes_accessed=cost[1], transcendentals=cost[2]),
        name=name,
    )


def norm(full, gain):
    middle = jnp.mean(full, axis=-1, keepdims=True)
    spread = jnp.mean((full - middle) ** 2, axis=-1, keepdims=True)
    return (full - middle) * lax.rsqrt(spread + EPS) * gain


def dot(a, b):
    return jnp.dot(a, b, preferred_element_type=F32)


def dot_t(a, b):
    return lax.dot_general(a, b, (((1,), (1,)), ((), ())), preferred_element_type=F32)


def iota(shape, dim):
    return lax.broadcasted_iota(jnp.int32, shape, dim)


def to_column(row, size):
    eye = iota((size, size), 0) == iota((size, size), 1)
    return jnp.sum(jnp.where(eye, jnp.broadcast_to(row, (size, size)), 0.0), axis=1, keepdims=True)


def half_masks(width):
    low = (iota((1, width), 1) % 128) < 64
    return jnp.where(low, 1.0, 0.0), jnp.where(low, 0.0, 1.0)


def row_scores_kernel(
    depth_hbm,
    place_ref,
    x_hbm,
    gain_hbm,
    prot_hbm,
    wq_hbm,
    wk_hbm,
    keep_ref,
    send_ref,
    normed_ref,
    same_ref,
    depth_ref,
    x_ref,
    gain_ref,
    prot_ref,
    wq_ref,
    wk_ref,
    sems,
):
    columns = prot_ref.shape[0]
    tokens, width = x_ref.shape
    rows = tokens // columns
    pairs = [(x_hbm, x_ref), (gain_hbm, gain_ref), (prot_hbm, prot_ref), (depth_hbm, depth_ref)]
    for n in range(width // 256):
        for source, target in ((wq_hbm, wq_ref), (wk_hbm, wk_ref)):
            pairs.append((source.at[:, 256 * n : 256 * n + 256], target.at[:, 256 * n : 256 * n + 256]))
    copies = [pltpu.make_async_copy(a, b, sems.at[i]) for i, (a, b) in enumerate(pairs)]
    for copy in copies:
        copy.start()
    for copy in copies[:2]:
        copy.wait()
    normed = norm(x_ref[...].astype(F32), gain_ref[...].reshape(1, width)).astype(BF16)
    normed_ref[...] = normed
    for copy in copies[2:4]:
        copy.wait()
    prot = prot_ref[...].reshape(1, columns).astype(F32)
    depth = jnp.zeros((1, columns), F32)
    for p in range(depth_ref.shape[0]):
        depth = jnp.where(prot == float(p), depth_ref[p].astype(F32), depth)
    prot_col = to_column(prot, columns)
    depth_col = to_column(depth, columns)
    same = jnp.broadcast_to(prot_col, (columns, columns)) == jnp.broadcast_to(prot, (columns, columns))
    same_f = jnp.where(same, 1.0, 0.0)
    same_ref[...] = same_f
    low = iota((columns, columns), 1) < 64
    first = jnp.where(low, same_f, pltpu.roll(same_f, 64, 1)) > 0.5
    valid = [
        jnp.where((place_ref[0] * rows + r).astype(F32) < depth_col, 1.0, 0.0) for r in range(rows)
    ]
    valid = jnp.concatenate(valid, axis=0)
    even, odd = half_masks(256)
    quarter = columns // PLANE
    core = (place_ref[0] % 2) == 0
    for n in range(width // 256):
        cols = slice(256 * n, 256 * n + 256)
        copies[4 + 2 * n].wait()
        query = dot(normed, wq_ref[:, cols]).astype(BF16).astype(F32) * valid
        copies[5 + 2 * n].wait()
        key = (dot(normed, wk_ref[:, cols]) * valid).astype(BF16)
        query_even, query_odd = (query * even).astype(BF16), (query * odd).astype(BF16)
        for q in range(2):
            lanes = slice(128 * q, 128 * q + 128)

            def side(array, lanes=lanes):
                return jnp.concatenate(
                    [array[r * columns : (r + 1) * columns, lanes] for r in range(rows)], axis=1
                )

            both = jnp.concatenate([side(query_even), side(query_odd)], axis=0)
            logits = dot_t(both, side(key))
            one, two = logits[:columns], logits[columns:]
            folded = jnp.where(
                low,
                jnp.where(first, one, pltpu.roll(one, 64, 1)),
                jnp.where(first, pltpu.roll(two, 64, 1), two),
            )
            out = slice(256 * n + 128 * q, 256 * n + 128 * q + 128)
            for y in range(PLANE // 2):
                start = 2 * y * quarter
                left, right = folded[start : start + quarter], folded[start + quarter : start + 2 * quarter]
                keep_ref[y, :, out] = jnp.where(core, left, right)
                send_ref[y, :, out] = jnp.where(core, right, left)


def core_sum_kernel(place_ref, mine_ref, other_ref, keep_ref, send_ref):
    row = (place_ref[0] // 2) % 2
    keep_ref[...] = mine_ref[row] + other_ref[row]
    send_ref[...] = mine_ref[1 - row] + other_ref[1 - row]


def add_kernel(*refs):
    total = refs[0][...] + refs[1][...]
    if len(refs) == 5:
        total = total + (refs[2][...] + refs[3][...])
    refs[-1][...] = total


def project_kernel(x_ref, w_ref, out_ref):
    out_ref[...] = dot(x_ref[...], w_ref[...]).astype(BF16)


def row_softmax_kernel(scale, place_ref, *refs):
    part_refs, (same_ref, out_ref, mask_ref) = refs[:-3], refs[-3:]
    tile, width = out_ref.shape
    same = same_ref[...]
    mask_ref[...] = jnp.maximum(same, pltpu.roll(same, 64, 1))
    live = mask_ref[pl.ds((place_ref[0] % PLANE) * tile, tile), :] > 0.5
    low = iota((tile, 128), 1) < 64
    for p in range(width // 128):
        lanes = slice(128 * p, 128 * p + 128)
        parts = [part[:, lanes] for part in part_refs]
        while len(parts) > 1:
            parts = [a + b for a, b in zip(parts[::2], parts[1::2])]
        tied = jnp.where(live, parts[0] * scale, NEG)
        top_low = jnp.max(jnp.where(low, tied, 2 * NEG), axis=1, keepdims=True)
        top_high = jnp.max(jnp.where(low, 2 * NEG, tied), axis=1, keepdims=True)
        value = jnp.exp(tied - jnp.where(low, top_low, top_high))
        sum_low = jnp.sum(jnp.where(low, value, 0.0), axis=1, keepdims=True)
        sum_high = jnp.sum(jnp.where(low, 0.0, value), axis=1, keepdims=True)
        out_ref[:, lanes] = (value / jnp.where(low, sum_low, sum_high)).astype(BF16)


def row_output_kernel(
    place_ref,
    piece0_ref,
    piece1_ref,
    piece2_ref,
    piece3_ref,
    same_ref,
    value_ref,
    x_ref,
    w_ref,
    gain_ref,
    after_ref,
    normed_ref,
    mixed_ref,
    folded_ref,
):
    columns = same_ref.shape[0]
    tokens, width = x_ref.shape
    rows = tokens // columns
    mine = place_ref[0] % PLANE
    quarter = columns // PLANE
    spot = [mine, mine + 1 - 2 * (mine % 2), (mine + 2) % 4]
    spot.append(spot[1] + spot[2] - mine)
    for where, piece in zip(spot, (piece0_ref, piece1_ref, piece2_ref, piece3_ref)):
        folded_ref[pl.ds(pl.multiple_of(where * quarter, quarter), quarter), :] = piece[...].astype(F32)
    same = same_ref[...] > 0.5
    low = iota((columns, columns), 1) < 64
    even, odd = half_masks(128 * rows)
    even, odd = even.astype(BF16), odd.astype(BF16)
    for p in range(width // 128):
        lanes = slice(128 * p, 128 * p + 128)
        piece = folded_ref[:, lanes]
        turned = pltpu.roll(piece, 64, 1)
        one = jnp.where(same, jnp.where(low, piece, turned), 0.0)
        two = jnp.where(same, jnp.where(low, turned, piece), 0.0)
        weights = jnp.concatenate([one, two], axis=1).astype(BF16)
        value = jnp.concatenate(
            [value_ref[r * columns : (r + 1) * columns, lanes] for r in range(rows)], axis=1
        )
        value = jnp.concatenate([value * even, value * odd], axis=0)
        mixed = dot(weights, value).astype(BF16)
        for r in range(rows):
            mixed_ref[r * columns : (r + 1) * columns, lanes] = mixed[:, 128 * r : 128 * r + 128]
    after = (x_ref[...].astype(F32) + dot(mixed_ref[...], w_ref[...])).astype(BF16)
    after_ref[...] = after
    normed = norm(after.astype(F32), gain_ref[...])
    if len(normed_ref.shape) == 2:
        normed_ref[...] = normed.astype(BF16)
    else:
        devices, _, tile, _ = normed_ref.shape
        for d in range(devices):
            for r in range(rows):
                start = r * columns + d * tile
                normed_ref[d, r] = normed[start : start + tile].astype(BF16)


def column_kernel(scale, tile, depth_ref, prot_ref, place_ref, x_ref, wq_ref, wk_ref, wv_ref, out_ref):
    tokens, width = x_ref.shape
    x = x_ref[...]
    lane = iota((1, tokens), 1)
    depth = jnp.zeros((1, tokens), jnp.int32)
    for c in range(tile):
        depth = jnp.where(lane % tile == c, depth_ref[prot_ref[place_ref[0] * tile + c]], depth)
    live = (iota((tokens, tokens), 0) % tile == iota((tokens, tokens), 1) % tile) & (
        iota((tokens, tokens), 1) // tile < depth
    )
    even, odd = half_masks(256)
    for n in range(width // 256):
        cols = slice(256 * n, 256 * n + 256)
        query = dot(x, wq_ref[:, cols]).astype(BF16).astype(F32)
        key = dot(x, wk_ref[:, cols]).astype(BF16)
        value = dot(x, wv_ref[:, cols])
        query_sides = [(query * side).astype(BF16) for side in (even, odd)]
        value_sides = [(value * side).astype(BF16) for side in (even, odd)]
        for q in range(2):
            lanes = slice(128 * q, 128 * q + 128)
            mixed = jnp.zeros((tokens, 128), F32)
            for s in range(2):
                scores = dot_t(query_sides[s][:, lanes], key[:, lanes]) * scale
                scores = jnp.where(live, scores, NEG)
                top = jnp.max(scores, axis=1, keepdims=True)
                weight = jnp.exp(scores - top)
                weight = weight / jnp.sum(weight, axis=1, keepdims=True)
                mixed = mixed + dot(weight.astype(BF16), value_sides[s][:, lanes])
            out_ref[:, 256 * n + 128 * q : 256 * n + 128 * q + 128] = mixed.astype(BF16)


def column_output_kernel(x_ref, w_ref, after_ref, out_ref, total_ref):
    rows, columns, width = out_ref.shape
    if len(x_ref.shape) == 2:
        total = dot(x_ref[...], w_ref[...]) + after_ref[...].astype(F32)
        out_ref[...] = total.astype(BF16).reshape(rows, columns, width)
    else:
        devices, _, tile, _ = x_ref.shape
        total = dot(x_ref[...].reshape(rows * columns, width), w_ref[...])
        for d in range(devices):
            for r in range(rows):
                start, block = r * columns + d * tile, (d * rows + r) * tile
                total_ref[start : start + tile] = total[block : block + tile]
        total = total_ref[...] + after_ref[...].astype(F32)
        out_ref[...] = total.astype(BF16).reshape(rows, columns, width)


def swap(array, offset):
    devices = lax.axis_size("seq")
    return lax.ppermute(array, "seq", [(i, i ^ offset) for i in range(devices)])


def exchange(array):
    return lax.all_to_all(array, "seq", split_axis=0, concat_axis=0, tiled=True)


def per_device(
    alignment,
    protein_id,
    row_depth,
    row_gain,
    row_query,
    row_key,
    row_value,
    row_output,
    column_gain,
    column_query,
    column_key,
    column_value,
    column_output,
):
    rows, columns, width = alignment.shape
    devices = lax.axis_size("seq")
    place = lax.axis_index("seq").astype(jnp.int32)[None]
    total_rows = rows * devices
    head_size = width // H
    tile = columns // devices
    tokens = rows * columns
    blocked = tile % 8 == 0
    x = alignment.reshape(tokens, width)
    shape = jax.ShapeDtypeStruct
    square = 2 * tokens * width * width

    quarter = columns // PLANE
    half = shape((PLANE // 2, quarter, width), F32)
    part = shape((quarter, width), F32)
    keep, send, normed, same = call(
        row_scores_kernel,
        (half, half, shape((tokens, width), BF16), shape((columns, columns), F32)),
        "asaaaaa",
        "vvvv",
        [
            pltpu.SMEM(row_depth.shape, jnp.int32),
            pltpu.VMEM((tokens, width), BF16),
            pltpu.VMEM((width,), F32),
            pltpu.VMEM((columns,), jnp.int32),
            pltpu.VMEM((width, width), BF16),
            pltpu.VMEM((width, width), BF16),
            pltpu.SemaphoreType.DMA((4 + 2 * (width // 256),)),
        ],
        (2 * square, 4 * width * width, tokens),
        "row_scores",
        LARGE,
    )(row_depth, place, x, row_gain, protein_id, row_query, row_key)
    (value,) = call(
        project_kernel, (shape((tokens, width), BF16),), "vv", "v", [], (square, 2 * width * width, 0), "row_value"
    )(normed, row_value)
    keep, send = call(
        core_sum_kernel, (part, part), "svv", "vv", [], (columns * width, 6 * columns * width, 0), "core_sum"
    )(place, keep, swap(send, 1))
    parts = [keep, swap(send, 2)]
    stride, planes = PLANE, devices // PLANE
    while planes > 1:
        ways = 4 if planes % 4 == 0 else 2
        (total,) = call(
            add_kernel, (part,), "v" * len(parts), "v", [], (columns * width, 6 * columns * width, 0), "add"
        )(*parts)
        parts = [total] + [swap(total, stride * w) for w in range(1, ways)]
        stride, planes = stride * ways, planes // ways
    (weights,) = call(
        functools.partial(row_softmax_kernel, 1.0 / (math.sqrt(head_size) * math.sqrt(total_rows))),
        (shape((quarter, width), BF16),),
        "s" + "v" * len(parts) + "v",
        "v",
        [pltpu.VMEM((columns, columns), F32)],
        (columns * width, 6 * columns * width, quarter * width),
        "row_softmax",
    )(place, *parts, same)
    across = swap(weights, 2)
    pieces = (weights, swap(weights, 1), across, swap(across, 1))
    normed_shape = (devices, rows, tile, width) if blocked else (tokens, width)
    after, normed = call(
        row_output_kernel,
        (shape((tokens, width), BF16), shape(normed_shape, BF16)),
        "s" + "v" * 9,
        "vv",
        [pltpu.VMEM((tokens, width), BF16), pltpu.VMEM((columns, width), F32)],
        (square, 2 * width * width, tokens),
        "row_output",
    )(place, *pieces, same, value, x, row_output, column_gain[None])
    if not blocked:
        normed = normed.reshape(rows, devices, tile, width).transpose(1, 0, 2, 3)
    moved = exchange(normed).reshape(tokens, width)
    (mixed,) = call(
        functools.partial(column_kernel, 1.0 / math.sqrt(head_size), tile),
        (shape((tokens, width), BF16),),
        "sssvvvv",
        "v",
        [],
        (4 * square, 6 * width * width, H * tokens * tokens),
        "column_attention",
    )(row_depth, protein_id, place, moved, column_query, column_key, column_value)
    returned = exchange(mixed.reshape(devices, rows, tile, width))
    if not blocked:
        returned = returned.transpose(1, 0, 2, 3).reshape(tokens, width)
    (out,) = call(
        column_output_kernel,
        (shape((rows, columns, width), BF16),),
        "vvv",
        "v",
        [pltpu.VMEM((tokens, width), F32)],
        (square, 2 * width * width, 0),
        "column_output",
    )(returned, column_output, after)
    return out


def solution(mesh):
    return jax.shard_map(
        per_device,
        mesh=mesh,
        in_specs=(P(("grp", "seq"), None, None), P("grp"), P("grp")) + (P(),) * 10,
        out_specs=P(("grp", "seq"), None, None),
        check_vma=False,
    )
```

```python
import functools
import math

import jax
import jax.numpy as jnp
from jax import lax
from jax.experimental import pallas as pl
from jax.experimental.pallas import tpu as pltpu
from jax.sharding import PartitionSpec as P

H = 12
EPS = 1e-05
NEG = -1000000000.0
F32 = jnp.float32
BF16 = jnp.bfloat16
LIMIT = 20 << 20
PLANE = 4


def call(kernel, out_shape, ins, outs, scratch, cost, name):
    spaces = {"v": pltpu.VMEM, "s": pltpu.SMEM, "h": pltpu.HBM}
    return pl.pallas_call(
        kernel,
        out_shape=out_shape,
        in_specs=[pl.BlockSpec(memory_space=spaces[c]) for c in ins],
        out_specs=[pl.BlockSpec(memory_space=spaces[c]) for c in outs],
        scratch_shapes=scratch,
        compiler_params=pltpu.CompilerParams(vmem_limit_bytes=LIMIT),
        cost_estimate=pl.CostEstimate(flops=cost[0], bytes_accessed=cost[1], transcendentals=cost[2]),
        name=name,
    )


def norm(full, gain):
    middle = jnp.mean(full, axis=-1, keepdims=True)
    spread = jnp.mean((full - middle) ** 2, axis=-1, keepdims=True)
    return (full - middle) * lax.rsqrt(spread + EPS) * gain


def dot(a, b):
    return jnp.dot(a, b, preferred_element_type=F32)


def dot_t(a, b):
    return lax.dot_general(a, b, (((1,), (1,)), ((), ())), preferred_element_type=F32)


def iota(shape, dim):
    return lax.broadcasted_iota(jnp.int32, shape, dim)


def to_column(row, size):
    eye = iota((size, size), 0) == iota((size, size), 1)
    return jnp.sum(jnp.where(eye, jnp.broadcast_to(row, (size, size)), 0.0), axis=1, keepdims=True)


def half_masks(width):
    low = (iota((1, width), 1) % 128) < 64
    return jnp.where(low, 1.0, 0.0), jnp.where(low, 0.0, 1.0)


def row_scores_kernel(
    depth_hbm,
    place_ref,
    x_hbm,
    gain_hbm,
    prot_hbm,
    wq_hbm,
    wk_hbm,
    keep_ref,
    send_ref,
    normed_ref,
    same_ref,
    depth_ref,
    x_ref,
    gain_ref,
    prot_ref,
    wq_ref,
    wk_ref,
    sems,
):
    columns = prot_ref.shape[0]
    tokens, width = x_ref.shape
    rows = tokens // columns
    pairs = [(x_hbm, x_ref), (gain_hbm, gain_ref), (prot_hbm, prot_ref), (depth_hbm, depth_ref)]
    for n in range(width // 256):
        for source, target in ((wq_hbm, wq_ref), (wk_hbm, wk_ref)):
            pairs.append((source.at[256 * n : 256 * n + 256], target.at[256 * n : 256 * n + 256]))
    copies = [pltpu.make_async_copy(a, b, sems.at[i]) for i, (a, b) in enumerate(pairs)]
    for copy in copies:
        copy.start()
    for copy in copies[:2]:
        copy.wait()
    normed = norm(x_ref[...].astype(F32), gain_ref[...].reshape(1, width)).astype(BF16)
    normed_ref[...] = normed
    for copy in copies[2:4]:
        copy.wait()
    prot = prot_ref[...].reshape(1, columns).astype(F32)
    depth = jnp.zeros((1, columns), F32)
    for p in range(depth_ref.shape[0]):
        depth = jnp.where(prot == float(p), depth_ref[p].astype(F32), depth)
    prot_col = to_column(prot, columns)
    depth_col = to_column(depth, columns)
    same = jnp.broadcast_to(prot_col, (columns, columns)) == jnp.broadcast_to(prot, (columns, columns))
    same_f = jnp.where(same, 1.0, 0.0)
    same_ref[...] = same_f
    low = iota((columns, columns), 1) < 64
    first = jnp.where(low, same_f, pltpu.roll(same_f, 64, 1)) > 0.5
    valid = [
        jnp.where((place_ref[0] * rows + r).astype(F32) < depth_col, 1.0, 0.0) for r in range(rows)
    ]
    valid = jnp.concatenate(valid, axis=0)
    even, odd = half_masks(256)
    quarter = columns // PLANE
    core = (place_ref[0] % 2) == 0
    for copy in copies[4:]:
        copy.wait()
    for n in range(width // 256):
        cols = slice(256 * n, 256 * n + 256)
        query = dot(normed, wq_ref[:, cols]).astype(BF16).astype(F32) * valid
        key = (dot(normed, wk_ref[:, cols]) * valid).astype(BF16)
        query_even, query_odd = (query * even).astype(BF16), (query * odd).astype(BF16)
        for q in range(2):
            lanes = slice(128 * q, 128 * q + 128)

            def side(array, lanes=lanes):
                return jnp.concatenate(
                    [array[r * columns : (r + 1) * columns, lanes] for r in range(rows)], axis=1
                )

            both = jnp.concatenate([side(query_even), side(query_odd)], axis=0)
            logits = dot_t(both, side(key))
            one, two = logits[:columns], logits[columns:]
            folded = jnp.where(
                low,
                jnp.where(first, one, pltpu.roll(one, 64, 1)),
                jnp.where(first, pltpu.roll(two, 64, 1), two),
            )
            out = slice(256 * n + 128 * q, 256 * n + 128 * q + 128)
            for y in range(PLANE // 2):
                start = 2 * y * quarter
                left, right = folded[start : start + quarter], folded[start + quarter : start + 2 * quarter]
                keep_ref[y, :, out] = jnp.where(core, left, right)
                send_ref[y, :, out] = jnp.where(core, right, left)


def core_sum_kernel(place_ref, mine_ref, other_ref, keep_ref, send_ref):
    row = (place_ref[0] // 2) % 2
    keep_ref[...] = mine_ref[row] + other_ref[row]
    send_ref[...] = mine_ref[1 - row] + other_ref[1 - row]


def add_kernel(*refs):
    total = refs[0][...] + refs[1][...]
    if len(refs) == 5:
        total = total + (refs[2][...] + refs[3][...])
    refs[-1][...] = total


def project_kernel(x_ref, w_ref, out_ref):
    out_ref[...] = dot(x_ref[...], w_ref[...]).astype(BF16)


def row_softmax_kernel(scale, place_ref, *refs):
    part_refs, (same_ref, out_ref, mask_ref) = refs[:-3], refs[-3:]
    tile, width = out_ref.shape
    same = same_ref[...]
    mask_ref[...] = jnp.maximum(same, pltpu.roll(same, 64, 1))
    live = mask_ref[pl.ds((place_ref[0] % PLANE) * tile, tile), :] > 0.5
    low = iota((tile, 128), 1) < 64
    for p in range(width // 128):
        lanes = slice(128 * p, 128 * p + 128)
        parts = [part[:, lanes] for part in part_refs]
        while len(parts) > 1:
            parts = [a + b for a, b in zip(parts[::2], parts[1::2])]
        tied = jnp.where(live, parts[0] * scale, NEG)
        top_low = jnp.max(jnp.where(low, tied, 2 * NEG), axis=1, keepdims=True)
        top_high = jnp.max(jnp.where(low, 2 * NEG, tied), axis=1, keepdims=True)
        value = jnp.exp(tied - jnp.where(low, top_low, top_high))
        sum_low = jnp.sum(jnp.where(low, value, 0.0), axis=1, keepdims=True)
        sum_high = jnp.sum(jnp.where(low, 0.0, value), axis=1, keepdims=True)
        out_ref[:, lanes] = (value / jnp.where(low, sum_low, sum_high)).astype(BF16)


def row_output_kernel(
    place_ref,
    piece0_ref,
    piece1_ref,
    piece2_ref,
    piece3_ref,
    same_ref,
    value_ref,
    x_ref,
    w_ref,
    gain_ref,
    after_ref,
    normed_ref,
    mixed_ref,
    folded_ref,
):
    columns = same_ref.shape[0]
    tokens, width = x_ref.shape
    rows = tokens // columns
    mine = place_ref[0] % PLANE
    quarter = columns // PLANE
    spot = [mine, mine + 1 - 2 * (mine % 2), (mine + 2) % 4]
    spot.append(spot[1] + spot[2] - mine)
    for where, piece in zip(spot, (piece0_ref, piece1_ref, piece2_ref, piece3_ref)):
        folded_ref[pl.ds(pl.multiple_of(where * quarter, quarter), quarter), :] = piece[...].astype(F32)
    same = same_ref[...] > 0.5
    low = iota((columns, columns), 1) < 64
    even, odd = half_masks(128 * rows)
    even, odd = even.astype(BF16), odd.astype(BF16)
    for p in range(width // 128):
        lanes = slice(128 * p, 128 * p + 128)
        piece = folded_ref[:, lanes]
        turned = pltpu.roll(piece, 64, 1)
        one = jnp.where(same, jnp.where(low, piece, turned), 0.0)
        two = jnp.where(same, jnp.where(low, turned, piece), 0.0)
        weights = jnp.concatenate([one, two], axis=1).astype(BF16)
        value = jnp.concatenate(
            [value_ref[r * columns : (r + 1) * columns, lanes] for r in range(rows)], axis=1
        )
        value = jnp.concatenate([value * even, value * odd], axis=0)
        mixed = dot(weights, value).astype(BF16)
        for r in range(rows):
            mixed_ref[r * columns : (r + 1) * columns, lanes] = mixed[:, 128 * r : 128 * r + 128]
    after = (x_ref[...].astype(F32) + dot(mixed_ref[...], w_ref[...])).astype(BF16)
    after_ref[...] = after
    normed = norm(after.astype(F32), gain_ref[...])
    if len(normed_ref.shape) == 2:
        normed_ref[...] = normed.astype(BF16)
    else:
        devices, _, tile, _ = normed_ref.shape
        for d in range(devices):
            for r in range(rows):
                start = r * columns + d * tile
                normed_ref[d, r] = normed[start : start + tile].astype(BF16)


def column_kernel(
    scale, tile, depth_ref, prot_ref, place_ref, x_ref, wq_ref, wk_ref, wv_ref, out_ref, mixed_ref
):
    tokens, width = x_ref.shape
    rows = tokens // tile
    chunk = max(128, rows)
    groups = chunk // rows
    x = x_ref[...]
    here, there = iota((tokens, tokens), 0), iota((tokens, tokens), 1)
    if tile > 1:
        sort = jnp.where(there == (here % rows) * tile + here // rows, 1.0, 0.0).astype(BF16)
        x = dot(sort, x).astype(BF16)
    same = jnp.where(iota((256, 256), 0) == iota((256, 256), 1), 1.0, 0.0).astype(BF16)
    group = (iota((1, 2 * chunk), 1) % chunk) // rows
    mine = [jnp.where(group == g, 1.0, 0.0).astype(BF16) for g in range(groups)]
    lives = []
    for start in range(0, tokens, chunk):
        depth = jnp.zeros((1, 2 * chunk), jnp.int32)
        for g in range(groups):
            column = place_ref[0] * tile + start // rows + g
            depth = jnp.where(group == g, depth_ref[prot_ref[column]], depth)
        lives.append(iota((rows, 2 * chunk), 0) < depth)
    even, odd = half_masks(256)
    even, odd = even * scale, odd * scale
    packs, values = [], []
    for n in range(width // 256):
        cols = slice(256 * n, 256 * n + 256)
        query = dot(x, wq_ref[:, cols]).astype(BF16).astype(F32)
        key = dot(x, wk_ref[:, cols]).astype(BF16)
        sides = [(query * side).astype(BF16) for side in (even, odd)]
        for q in range(2):
            lanes = slice(128 * q, 128 * q + 128)
            for j, live in enumerate(lives):
                part = slice(j * chunk, j * chunk + chunk)
                both = jnp.concatenate([side[part, lanes] for side in sides], axis=0)
                scores = dot_t(key[part, lanes], both)
                packed = scores[:rows]
                for g in range(1, groups):
                    packed = jnp.where(group == g, scores[g * rows : (g + 1) * rows], packed)
                packs.append(jnp.where(live, packed, NEG))
        values.append(dot_t(same, dot(x, wv_ref[:, cols]).astype(BF16)).astype(BF16))
    packs = [jnp.exp(packed - jnp.max(packed, axis=0, keepdims=True)) for packed in packs]
    packs = [
        (packed * (1.0 / jnp.sum(packed, axis=0, keepdims=True))).astype(BF16) for packed in packs
    ]
    for n, value in enumerate(values):
        for q in range(2):
            for j in range(len(lives)):
                part = slice(j * chunk, j * chunk + chunk)
                weight = packs[(2 * n + q) * len(lives) + j]
                spread = jnp.concatenate([weight * m for m in mine], axis=0)
                for s in range(2):
                    first = 128 * q + 64 * s
                    mixed = dot(value[first : first + 64, part], spread[:, s * chunk : (s + 1) * chunk])
                    mixed_ref[256 * n + first : 256 * n + first + 64, part] = mixed.astype(BF16)
    back = jnp.where(there == (here % tile) * rows + here // tile, 1.0, 0.0).astype(BF16)
    out_ref[...] = dot_t(back, mixed_ref[...]).astype(BF16)


def column_output_kernel(x_ref, w_ref, after_ref, out_ref, total_ref):
    rows, columns, width = out_ref.shape
    if len(x_ref.shape) == 2:
        total = dot(x_ref[...], w_ref[...]) + after_ref[...].astype(F32)
        out_ref[...] = total.astype(BF16).reshape(rows, columns, width)
    else:
        devices, _, tile, _ = x_ref.shape
        total = dot(x_ref[...].reshape(rows * columns, width), w_ref[...])
        for d in range(devices):
            for r in range(rows):
                start, block = r * columns + d * tile, (d * rows + r) * tile
                total_ref[start : start + tile] = total[block : block + tile]
        total = total_ref[...] + after_ref[...].astype(F32)
        out_ref[...] = total.astype(BF16).reshape(rows, columns, width)


def hbm(array):
    return pltpu.with_memory_space_constraint(array, pltpu.HBM)


def swap(array, offset):
    devices = lax.axis_size("seq")
    return lax.ppermute(array, "seq", [(i, i ^ offset) for i in range(devices)])


def exchange(array):
    return lax.all_to_all(array, "seq", split_axis=0, concat_axis=0, tiled=True)


def per_device(
    alignment,
    protein_id,
    row_depth,
    row_gain,
    row_query,
    row_key,
    row_value,
    row_output,
    column_gain,
    column_query,
    column_key,
    column_value,
    column_output,
):
    rows, columns, width = alignment.shape
    devices = lax.axis_size("seq")
    place = lax.axis_index("seq").astype(jnp.int32)[None]
    total_rows = rows * devices
    head_size = width // H
    tile = columns // devices
    tokens = rows * columns
    blocked = tile % 8 == 0
    x = alignment.reshape(tokens, width)
    shape = jax.ShapeDtypeStruct
    square = 2 * tokens * width * width

    quarter = columns // PLANE
    half = shape((PLANE // 2, quarter, width), F32)
    part = shape((quarter, width), F32)
    keep, send, normed, same = call(
        row_scores_kernel,
        (half, half, shape((tokens, width), BF16), shape((columns, columns), F32)),
        "hshhhhh",
        "vvvv",
        [
            pltpu.SMEM(row_depth.shape, jnp.int32),
            pltpu.VMEM((tokens, width), BF16),
            pltpu.VMEM((width,), F32),
            pltpu.VMEM((columns,), jnp.int32),
            pltpu.VMEM((width, width), BF16),
            pltpu.VMEM((width, width), BF16),
            pltpu.SemaphoreType.DMA((4 + 2 * (width // 256),)),
        ],
        (2 * square, 4 * width * width, tokens),
        "row_scores",
    )(hbm(row_depth), place, hbm(x), hbm(row_gain), hbm(protein_id), hbm(row_query), hbm(row_key))
    column_value, normed = lax.optimization_barrier((column_value, normed))
    (value,) = call(
        project_kernel, (shape((tokens, width), BF16),), "vv", "v", [], (square, 2 * width * width, 0), "row_value"
    )(normed, row_value)
    keep, send = call(
        core_sum_kernel, (part, part), "svv", "vv", [], (columns * width, 6 * columns * width, 0), "core_sum"
    )(place, keep, swap(send, 1))
    parts = [keep, swap(send, 2)]
    stride, planes = PLANE, devices // PLANE
    while planes > 1:
        ways = 4 if planes % 4 == 0 else 2
        (total,) = call(
            add_kernel, (part,), "v" * len(parts), "v", [], (columns * width, 6 * columns * width, 0), "add"
        )(*parts)
        parts = [total] + [swap(total, stride * w) for w in range(1, ways)]
        stride, planes = stride * ways, planes // ways
    (weights,) = call(
        functools.partial(row_softmax_kernel, 1.0 / (math.sqrt(head_size) * math.sqrt(total_rows))),
        (shape((quarter, width), BF16),),
        "s" + "v" * len(parts) + "v",
        "v",
        [pltpu.VMEM((columns, columns), F32)],
        (columns * width, 6 * columns * width, quarter * width),
        "row_softmax",
    )(place, *parts, same)
    across = swap(weights, 2)
    pieces = (weights, swap(weights, 1), across, swap(across, 1))
    normed_shape = (devices, rows, tile, width) if blocked else (tokens, width)
    after, normed = call(
        row_output_kernel,
        (shape((tokens, width), BF16), shape(normed_shape, BF16)),
        "s" + "v" * 9,
        "vv",
        [pltpu.VMEM((tokens, width), BF16), pltpu.VMEM((columns, width), F32)],
        (square, 2 * width * width, tokens),
        "row_output",
    )(place, *pieces, same, value, x, row_output, column_gain[None])
    if not blocked:
        normed = normed.reshape(rows, devices, tile, width).transpose(1, 0, 2, 3)
    moved = exchange(normed).reshape(tokens, width)
    (mixed,) = call(
        functools.partial(column_kernel, 1.0 / math.sqrt(head_size), tile),
        (shape((tokens, width), BF16),),
        "sssvvvv",
        "v",
        [pltpu.VMEM((width, tokens), BF16)],
        (4 * square, 6 * width * width, H * tokens * tokens),
        "column_attention",
    )(row_depth, protein_id, place, moved, column_query, column_key, column_value)
    returned = exchange(mixed.reshape(devices, rows, tile, width))
    if not blocked:
        returned = returned.transpose(1, 0, 2, 3).reshape(tokens, width)
    (out,) = call(
        column_output_kernel,
        (shape((rows, columns, width), BF16),),
        "vvv",
        "v",
        [pltpu.VMEM((tokens, width), F32)],
        (square, 2 * width * width, 0),
        "column_output",
    )(returned, column_output, after)
    return out


def solution(mesh):
    return jax.shard_map(
        per_device,
        mesh=mesh,
        in_specs=(P(("grp", "seq"), None, None), P("grp"), P("grp")) + (P(),) * 10,
        out_specs=P(("grp", "seq"), None, None),
        check_vma=False,
    )
```

```python
import functools
import math

import jax
import jax.numpy as jnp
from jax import lax
from jax.experimental import pallas as pl
from jax.experimental.pallas import tpu as pltpu
from jax.sharding import PartitionSpec as P

H = 12
EPS = 1e-05
NEG = -1000000000.0
F32 = jnp.float32
BF16 = jnp.bfloat16
LIMIT = 20 << 20
PLANE = 4


def call(kernel, out_shape, ins, outs, scratch, cost, name):
    spaces = {"v": pltpu.VMEM, "s": pltpu.SMEM, "h": pltpu.HBM, "a": pl.ANY}
    return pl.pallas_call(
        kernel,
        out_shape=out_shape,
        in_specs=[pl.BlockSpec(memory_space=spaces[c]) for c in ins],
        out_specs=[pl.BlockSpec(memory_space=spaces[c]) for c in outs],
        scratch_shapes=scratch,
        compiler_params=pltpu.CompilerParams(vmem_limit_bytes=LIMIT),
        cost_estimate=pl.CostEstimate(flops=cost[0], bytes_accessed=cost[1], transcendentals=cost[2]),
        name=name,
    )


def norm(full, gain):
    middle = jnp.mean(full, axis=-1, keepdims=True)
    spread = jnp.mean((full - middle) ** 2, axis=-1, keepdims=True)
    return (full - middle) * lax.rsqrt(spread + EPS) * gain


def dot(a, b):
    return jnp.dot(a, b, preferred_element_type=F32)


def dot_t(a, b):
    return lax.dot_general(a, b, (((1,), (1,)), ((), ())), preferred_element_type=F32)


def iota(shape, dim):
    return lax.broadcasted_iota(jnp.int32, shape, dim)


def flat(ref):
    return jnp.concatenate([ref[p] for p in range(ref.shape[0])], axis=1)


def to_column(row, size):
    eye = iota((size, size), 0) == iota((size, size), 1)
    return jnp.sum(jnp.where(eye, jnp.broadcast_to(row, (size, size)), 0.0), axis=1, keepdims=True)


def half_masks(width):
    low = (iota((1, width), 1) % 128) < 64
    return jnp.where(low, 1.0, 0.0), jnp.where(low, 0.0, 1.0)


def row_scores_kernel(
    depth_hbm,
    place_ref,
    x_hbm,
    gain_hbm,
    prot_hbm,
    wq_hbm,
    wk_hbm,
    keep_ref,
    send_ref,
    normed_ref,
    same_ref,
    depth_ref,
    x_ref,
    gain_ref,
    prot_ref,
    wq_ref,
    wk_ref,
    sems,
):
    columns = prot_ref.shape[0]
    tokens, width = x_ref.shape
    rows = tokens // columns
    pairs = [(x_hbm, x_ref), (gain_hbm, gain_ref), (prot_hbm, prot_ref), (depth_hbm, depth_ref)]
    for n in range(width // 256):
        for source, target in ((wq_hbm, wq_ref), (wk_hbm, wk_ref)):
            pairs.append((source.at[256 * n : 256 * n + 256], target.at[256 * n : 256 * n + 256]))
    copies = [pltpu.make_async_copy(a, b, sems.at[i]) for i, (a, b) in enumerate(pairs)]
    for copy in copies:
        copy.start()
    for copy in copies[:2]:
        copy.wait()
    normed = norm(x_ref[...].astype(F32), gain_ref[...].reshape(1, width)).astype(BF16)
    normed_ref[...] = normed
    for copy in copies[2:4]:
        copy.wait()
    prot = prot_ref[...].reshape(1, columns).astype(F32)
    depth = jnp.zeros((1, columns), F32)
    for p in range(depth_ref.shape[0]):
        depth = jnp.where(prot == float(p), depth_ref[p].astype(F32), depth)
    prot_col = to_column(prot, columns)
    depth_col = to_column(depth, columns)
    same = jnp.broadcast_to(prot_col, (columns, columns)) == jnp.broadcast_to(prot, (columns, columns))
    same_f = jnp.where(same, 1.0, 0.0)
    same_ref[...] = same_f
    low = iota((columns, columns), 1) < 64
    first = jnp.where(low, same_f, pltpu.roll(same_f, 64, 1)) > 0.5
    valid = [
        jnp.where((place_ref[0] * rows + r).astype(F32) < depth_col, 1.0, 0.0) for r in range(rows)
    ]
    valid = jnp.concatenate(valid, axis=0)
    even, odd = half_masks(256)
    quarter = columns // PLANE
    core = (place_ref[0] % 2) == 0
    for copy in copies[4:]:
        copy.wait()
    for n in range(width // 256):
        cols = slice(256 * n, 256 * n + 256)
        query = dot(normed, wq_ref[:, cols]).astype(BF16).astype(F32) * valid
        key = (dot(normed, wk_ref[:, cols]) * valid).astype(BF16)
        query_even, query_odd = (query * even).astype(BF16), (query * odd).astype(BF16)
        for q in range(2):
            lanes = slice(128 * q, 128 * q + 128)

            def side(array, lanes=lanes):
                return jnp.concatenate(
                    [array[r * columns : (r + 1) * columns, lanes] for r in range(rows)], axis=1
                )

            both = jnp.concatenate([side(query_even), side(query_odd)], axis=0)
            logits = dot_t(both, side(key))
            one, two = logits[:columns], logits[columns:]
            folded = jnp.where(
                low,
                jnp.where(first, one, pltpu.roll(one, 64, 1)),
                jnp.where(first, pltpu.roll(two, 64, 1), two),
            )
            out = slice(256 * n + 128 * q, 256 * n + 128 * q + 128)
            for y in range(PLANE // 2):
                start = 2 * y * quarter
                left, right = folded[start : start + quarter], folded[start + quarter : start + 2 * quarter]
                keep_ref[y, :, out] = jnp.where(core, left, right)
                send_ref[y, :, out] = jnp.where(core, right, left)


def core_sum_kernel(place_ref, mine_ref, other_ref, keep_ref, send_ref):
    row = (place_ref[0] // 2) % 2
    keep_ref[...] = mine_ref[row] + other_ref[row]
    send_ref[...] = mine_ref[1 - row] + other_ref[1 - row]


def add_kernel(*refs):
    total = refs[0][...] + refs[1][...]
    if len(refs) == 5:
        total = total + (refs[2][...] + refs[3][...])
    refs[-1][...] = total


def row_value_kernel(columns, place_ref, x_ref, w_ref, mine_ref, other_ref, out_ref, spread_ref):
    core = place_ref[0] % 2
    out_ref[...] = dot(x_ref[...], w_ref[...]).astype(BF16)
    rows = x_ref.shape[0] // columns
    quarter = columns // PLANE
    for source, index in ((mine_ref, core), (other_ref, 1 - core)):
        for r in range(rows):
            for y in range(2):
                start = pl.multiple_of(r * columns + y * columns // 2 + quarter * core, quarter)
                piece = source[pl.ds(start, quarter), :].astype(F32)
                target = pl.ds(2 * rows * quarter * y + index * rows + r, quarter, stride=2 * rows)
                for p in range(piece.shape[1] // 128):
                    spread_ref[p, target, :] = piece[:, 128 * p : 128 * p + 128]


def row_softmax_kernel(scale, place_ref, *refs):
    part_refs, (same_ref, out_ref, mask_ref) = refs[:-3], refs[-3:]
    tile, width = out_ref.shape
    same = same_ref[...]
    mask_ref[...] = jnp.maximum(same, pltpu.roll(same, 64, 1))
    live = mask_ref[pl.ds((place_ref[0] % PLANE) * tile, tile), :] > 0.5
    low = iota((tile, 128), 1) < 64
    for p in range(width // 128):
        lanes = slice(128 * p, 128 * p + 128)
        parts = [part[:, lanes] for part in part_refs]
        while len(parts) > 1:
            parts = [a + b for a, b in zip(parts[::2], parts[1::2])]
        tied = jnp.where(live, parts[0] * scale, NEG)
        top_low = jnp.max(jnp.where(low, tied, 2 * NEG), axis=1, keepdims=True)
        top_high = jnp.max(jnp.where(low, 2 * NEG, tied), axis=1, keepdims=True)
        value = jnp.exp(tied - jnp.where(low, top_low, top_high))
        sum_low = jnp.sum(jnp.where(low, value, 0.0), axis=1, keepdims=True)
        sum_high = jnp.sum(jnp.where(low, 0.0, value), axis=1, keepdims=True)
        out_ref[:, lanes] = (value / jnp.where(low, sum_low, sum_high)).astype(BF16)


def row_output_kernel(
    place_ref,
    mine_ref,
    across_ref,
    same_ref,
    value_ref,
    other_ref,
    x_ref,
    w_ref,
    gain_ref,
    after_ref,
    *refs,
):
    outs, (mixed_ref, folded_ref, normed_ref) = refs[:-3], refs[-3:]
    columns = same_ref.shape[0]
    tokens, width = after_ref.shape
    rows = tokens // columns
    quarter, local = columns // PLANE, columns // 2
    place = place_ref[0]
    core, line, plane = place % 2, (place // 2) % 2, place // PLANE
    folded_ref[pl.ds(pl.multiple_of(line * quarter, quarter), quarter), :] = mine_ref[...].astype(F32)
    folded_ref[pl.ds(pl.multiple_of((1 - line) * quarter, quarter), quarter), :] = across_ref[...].astype(F32)
    same = [
        same_ref[pl.ds(pl.multiple_of(y * local + core * quarter, quarter), quarter), :] for y in range(2)
    ]
    same = jnp.concatenate(same, axis=0) > 0.5
    low = iota((local, columns), 1) < 64
    even, odd = half_masks(256 * rows)
    even, odd = even.astype(BF16), odd.astype(BF16)
    spots = [core * rows + r for r in range(rows)] + [(1 - core) * rows + r for r in range(rows)]
    for p in range(width // 128):
        lanes = slice(128 * p, 128 * p + 128)
        piece = folded_ref[:, lanes]
        turned = pltpu.roll(piece, 64, 1)
        one = jnp.where(same, jnp.where(low, piece, turned), 0.0)
        two = jnp.where(same, jnp.where(low, turned, piece), 0.0)
        weights = jnp.concatenate([one, two], axis=1).astype(BF16)
        value = jnp.concatenate(
            [
                source[r * columns : (r + 1) * columns, lanes]
                for source in (value_ref, other_ref)
                for r in range(rows)
            ],
            axis=1,
        )
        value = jnp.concatenate([value * even, value * odd], axis=0)
        mixed = dot(weights, value)
        for i, spot in enumerate(spots):
            mixed_ref[p, pl.ds(spot, local, stride=2 * rows), :] = mixed[:, 128 * i : 128 * i + 128]
    after = (flat(x_ref) + dot(flat(mixed_ref).astype(BF16), w_ref[...])).astype(BF16)
    after_ref[...] = after
    normed_ref[...] = norm(after.astype(F32), gain_ref[...])
    size = tokens // len(outs)
    for s, out in enumerate(outs):
        start = pl.multiple_of(((plane + s) % len(outs)) * size, size)
        out[...] = normed_ref[pl.ds(start, size), :].astype(BF16)


def column_kernel(scale, planes, columns, depth_ref, prot_ref, place_ref, wq_ref, wk_ref, wv_ref, *refs):
    ins, (keep_ref, send_ref, all_ref, mixed_ref) = refs[: 2 * planes], refs[2 * planes :]
    size, width = ins[0].shape
    wide = width // 2
    slots, local = 2 * planes, columns // 2
    own = local // planes
    rows = size // own
    block = 4 if own % 4 == 0 else own
    piece = block * rows
    chunk = slots * piece
    chunks = own // block
    fold = piece // 8
    pair = 8 // rows
    place = place_ref[0]
    core, line, plane = place % 2, (place // 2) % 2, place // PLANE
    for g in range(chunks):
        for i, source in enumerate(ins):
            all_ref[g * chunk + i * piece : g * chunk + (i + 1) * piece, :] = source[g * piece : (g + 1) * piece, :]
    x = all_ref[...]
    heads = pl.ds(pl.multiple_of(core * wide, 128), wide)
    even, odd = half_masks(wide)
    query = dot(x, wq_ref[:, heads]).astype(BF16).astype(F32) * scale
    key = dot(x, wk_ref[:, heads]).astype(BF16)
    value = dot(x, wv_ref[:, heads]).astype(BF16)
    sides = [(query * side).astype(BF16) for side in (even, odd)]
    unit = jnp.where(iota((128, 128), 0) == iota((128, 128), 1), 1.0, 0.0).astype(BF16)
    lane = (iota((8, 2 * chunk), 1) % piece) // rows
    level = iota((8, 2 * chunk), 0)
    fits = level // rows == lane % pair
    mine = [jnp.where(lane // pair == v, 1.0, 0.0)[None] for v in range(fold)]
    lives = []
    for g in range(chunks):
        depth = jnp.zeros((8, 2 * chunk), jnp.int32)
        for c in range(block):
            index = plane * own + g * block + c
            column = index % (local // 2) + (local // 2) * line + local * (index // (local // 2))
            depth = jnp.where(lane == c, depth_ref[prot_ref[column]], depth)
        live = []
        for i in range(slots):
            away = ((plane + planes - i % planes) % planes) * 2 + (core if i < planes else 1 - core)
            live.append((fits & (level % rows + away * rows < depth))[None])
        lives.append(jnp.concatenate([jnp.where(l, 1.0, 0.0) for l in live], axis=0) > 0.5)
    packs, values = [], []
    for q in range(wide // 128):
        lanes = slice(128 * q, 128 * q + 128)
        for g in range(chunks):
            part = slice(g * chunk, g * chunk + chunk)
            both = jnp.concatenate([side[part, lanes] for side in sides], axis=0)
            scores = dot_t(key[part, lanes], both).reshape(slots, fold, 8, 2 * chunk)
            packed = scores[:, 0]
            for v in range(1, fold):
                packed = jnp.where(mine[v] > 0.5, scores[:, v], packed)
            packs.append(jnp.where(lives[g], packed, NEG))
        values.append(dot_t(unit, value[:, lanes]).astype(BF16))
    packs = [jnp.exp(packed - jnp.max(packed, axis=(0, 1), keepdims=True)) for packed in packs]
    packs = [packed * (1.0 / jnp.sum(packed, axis=(0, 1), keepdims=True)) for packed in packs]
    for q, value in enumerate(values):
        for g in range(chunks):
            part = slice(g * chunk, g * chunk + chunk)
            weight = packs[q * chunks + g]
            spread = jnp.stack([weight * m for m in mine], axis=1).reshape(chunk, 2 * chunk).astype(BF16)
            for s in range(2):
                mixed = dot(value[64 * s : 64 * s + 64, part], spread[:, s * chunk : (s + 1) * chunk])
                mixed_ref[128 * q + 64 * s : 128 * q + 64 * s + 64, part] = mixed.astype(BF16)
    turn = jnp.where(iota((chunk, chunk), 0) == iota((chunk, chunk), 1), 1.0, 0.0).astype(BF16)
    for g in range(chunks):
        mixed = dot_t(turn, mixed_ref[:, g * chunk : (g + 1) * chunk])
        for i in range(slots):
            target = keep_ref if i < planes else send_ref
            target[i % planes, g * piece : (g + 1) * piece, :] = mixed[i * piece : (i + 1) * piece].astype(BF16)


def join_kernel(place_ref, keep_ref, other_ref, *outs):
    wide = keep_ref.shape[2]
    core = place_ref[0] % 2

    def write(left, right):
        for s, out in enumerate(outs):
            out[:, :wide] = left[s]
            out[:, wide:] = right[s]

    @pl.when(core == 0)
    def _():
        write(keep_ref, other_ref)

    @pl.when(core == 1)
    def _():
        write(other_ref, keep_ref)


def column_output_kernel(place_ref, w_ref, after_ref, *refs):
    ins, (keep_ref, send_ref, total_ref) = refs[:-3], refs[-3:]
    rows, local, _ = keep_ref.shape
    core, plane = place_ref[0] % 2, place_ref[0] // PLANE
    size = ins[0].shape[0]
    total = dot(jnp.concatenate([source[...] for source in ins], axis=0), w_ref[...])
    for s in range(len(ins)):
        start = pl.multiple_of(((plane + s) % len(ins)) * size, size)
        for p in range(total.shape[1] // 128):
            total_ref[p, pl.ds(start, size), :] = total[s * size : (s + 1) * size, 128 * p : 128 * p + 128]
    for p in range(total.shape[1] // 128):
        lanes = slice(128 * p, 128 * p + 128)
        total_ref[p] = total_ref[p] + after_ref[:, lanes].astype(F32)
        for r in range(rows):
            for target, index in ((keep_ref, core), (send_ref, 1 - core)):
                row = total_ref[p, pl.ds(index * rows + r, local, stride=2 * rows), :]
                target[r, :, lanes] = row.astype(BF16)


def assemble_kernel(place_ref, mine_ref, other_ref, out_ref, sems):
    core = place_ref[0] % 2
    local = mine_ref.shape[1]
    quarter = local // 2
    copies = []
    for source, index in ((mine_ref, core), (other_ref, 1 - core)):
        for y in range(2):
            start = pl.multiple_of(y * local + index * quarter, quarter)
            copies.append(
                pltpu.make_async_copy(
                    source.at[:, y * quarter : (y + 1) * quarter, :],
                    out_ref.at[:, pl.ds(start, quarter), :],
                    sems.at[len(copies)],
                )
            )
    for copy in copies:
        copy.start()
    for copy in copies:
        copy.wait()


def hbm(array):
    return pltpu.with_memory_space_constraint(array, pltpu.HBM)


def swap(array, offset):
    devices = lax.axis_size("seq")
    return lax.ppermute(array, "seq", [(i, i ^ offset) for i in range(devices)])


def spin_pairs(step):
    planes = lax.axis_size("seq") // PLANE
    pairs = []
    for z in range(planes):
        for y in range(2):
            for k in range(2):
                pairs.append((z * PLANE + 2 * y + k, (z + step) % planes * PLANE + 2 * k + y))
    return pairs


def spin(array, step):
    return lax.ppermute(array, "seq", spin_pairs(step))


def spin_back(array, step):
    return lax.ppermute(array, "seq", [(b, a) for a, b in spin_pairs(step)])


def per_device(
    alignment,
    protein_id,
    row_depth,
    row_gain,
    row_query,
    row_key,
    row_value,
    row_output,
    column_gain,
    column_query,
    column_key,
    column_value,
    column_output,
):
    rows, columns, width = alignment.shape
    devices = lax.axis_size("seq")
    place = lax.axis_index("seq").astype(jnp.int32)[None]
    total_rows = rows * devices
    head_size = width // H
    tokens = rows * columns
    planes, local = devices // PLANE, columns // 2
    size = tokens // planes
    x = alignment.reshape(tokens, width)
    shape = jax.ShapeDtypeStruct
    square = 2 * tokens * width * width

    quarter = columns // PLANE
    half = shape((PLANE // 2, quarter, width), F32)
    part = shape((quarter, width), F32)
    keep, send, normed, same = call(
        row_scores_kernel,
        (half, half, shape((tokens, width), BF16), shape((columns, columns), F32)),
        "hshhhhh",
        "vvvv",
        [
            pltpu.SMEM(row_depth.shape, jnp.int32),
            pltpu.VMEM((tokens, width), BF16),
            pltpu.VMEM((width,), F32),
            pltpu.VMEM((columns,), jnp.int32),
            pltpu.VMEM((width, width), BF16),
            pltpu.VMEM((width, width), BF16),
            pltpu.SemaphoreType.DMA((4 + 2 * (width // 256),)),
        ],
        (2 * square, 4 * width * width, tokens),
        "row_scores",
    )(hbm(row_depth), place, hbm(x), hbm(row_gain), hbm(protein_id), hbm(row_query), hbm(row_key))
    column_query, column_key, column_value, late, normed = lax.optimization_barrier(
        (column_query, column_key, column_value, x, normed)
    )
    sibling = swap(late, 1)
    value, spread = call(
        functools.partial(row_value_kernel, columns),
        (shape((tokens, width), BF16), shape((width // 128, tokens, 128), F32)),
        "svvvv",
        "vv",
        [],
        (square, 2 * width * width, 0),
        "row_value",
    )(place, normed, row_value, late, sibling)
    value_other = swap(value, 1)
    keep, send = call(
        core_sum_kernel, (part, part), "svv", "vv", [], (columns * width, 6 * columns * width, 0), "core_sum"
    )(place, keep, swap(send, 1))
    parts = [keep, swap(send, 2)]
    stride, left = PLANE, planes
    while left > 1:
        ways = 4 if left % 4 == 0 else 2
        (total,) = call(
            add_kernel, (part,), "v" * len(parts), "v", [], (columns * width, 6 * columns * width, 0), "add"
        )(*parts)
        parts = [total] + [swap(total, stride * w) for w in range(1, ways)]
        stride, left = stride * ways, left // ways
    (weights,) = call(
        functools.partial(row_softmax_kernel, 1.0 / (math.sqrt(head_size) * math.sqrt(total_rows))),
        (shape((quarter, width), BF16),),
        "s" + "v" * len(parts) + "v",
        "v",
        [pltpu.VMEM((columns, columns), F32)],
        (columns * width, 6 * columns * width, quarter * width),
        "row_softmax",
    )(place, *parts, same)
    across = swap(weights, 2)
    after, *blocks = call(
        row_output_kernel,
        (shape((tokens, width), BF16),) + (shape((size, width), BF16),) * planes,
        "s" + "v" * 8,
        "v" * (1 + planes),
        [
            pltpu.VMEM((width // 128, tokens, 128), F32),
            pltpu.VMEM((local, width), F32),
            pltpu.VMEM((tokens, width), F32),
        ],
        (square, 2 * width * width, tokens),
        "row_output",
    )(place, weights, across, same, value, value_other, spread, row_output, column_gain[None])
    moved = [spin(block, s) for s, block in enumerate(blocks)]
    moved += [swap(block, 1) for block in moved]
    wide = width // 2
    halves = shape((planes, size, wide), BF16)
    keep, send = call(
        functools.partial(column_kernel, 1.0 / math.sqrt(head_size), planes, columns),
        (halves, halves),
        "sss" + "v" * (3 + 2 * planes),
        "vv",
        [pltpu.VMEM((2 * tokens, width), BF16), pltpu.VMEM((wide, 2 * tokens), BF16)],
        (4 * square, 6 * width * width, H * tokens * tokens // 4),
        "column_attention",
    )(row_depth, protein_id, place, column_query, column_key, column_value, *moved)
    joined = call(
        join_kernel,
        (shape((size, width), BF16),) * planes,
        "svv",
        "v" * planes,
        [],
        (tokens * width, 4 * tokens * width, 0),
        "join",
    )(place, keep, swap(send, 1))
    returned = [spin_back(block, s) for s, block in enumerate(joined)]
    half = shape((rows, local, width), BF16)
    keep, send = call(
        column_output_kernel,
        (half, half),
        "svv" + "v" * planes,
        "vv",
        [pltpu.VMEM((width // 128, tokens, 128), F32)],
        (square, 2 * width * width, 0),
        "column_output",
    )(place, column_output, after, *returned)
    (out,) = call(
        assemble_kernel,
        (shape((rows, columns, width), BF16),),
        "svv",
        "a",
        [pltpu.SemaphoreType.DMA((4,))],
        (tokens * width, 4 * tokens * width, 0),
        "assemble",
    )(place, keep, swap(send, 1))
    return out


def solution(mesh):
    return jax.shard_map(
        per_device,
        mesh=mesh,
        in_specs=(P(("grp", "seq"), None, None), P("grp"), P("grp")) + (P(),) * 10,
        out_specs=P(("grp", "seq"), None, None),
        check_vma=False,
    )
```

```python
import functools
import math

import jax
import jax.numpy as jnp
from jax import lax
from jax.experimental import pallas as pl
from jax.experimental.pallas import tpu as pltpu
from jax.sharding import PartitionSpec as P

H = 12
EPS = 1e-05
NEG = -1000000000.0
F32 = jnp.float32
BF16 = jnp.bfloat16
LIMIT = 20 << 20
PLANE = 4


def call(kernel, out_shape, ins, outs, scratch, cost, name):
    spaces = {"v": pltpu.VMEM, "s": pltpu.SMEM, "h": pltpu.HBM, "a": pl.ANY}
    return pl.pallas_call(
        kernel,
        out_shape=out_shape,
        in_specs=[pl.BlockSpec(memory_space=spaces[c]) for c in ins],
        out_specs=[pl.BlockSpec(memory_space=spaces[c]) for c in outs],
        scratch_shapes=scratch,
        compiler_params=pltpu.CompilerParams(vmem_limit_bytes=LIMIT),
        cost_estimate=pl.CostEstimate(flops=cost[0], bytes_accessed=cost[1], transcendentals=cost[2]),
        name=name,
    )


def norm(full, gain):
    middle = jnp.mean(full, axis=-1, keepdims=True)
    spread = jnp.mean((full - middle) ** 2, axis=-1, keepdims=True)
    return (full - middle) * lax.rsqrt(spread + EPS) * gain


def dot(a, b):
    return jnp.dot(a, b, preferred_element_type=F32)


def dot_t(a, b):
    return lax.dot_general(a, b, (((1,), (1,)), ((), ())), preferred_element_type=F32)


def iota(shape, dim):
    return lax.broadcasted_iota(jnp.int32, shape, dim)


def flat(ref):
    return jnp.concatenate([ref[p] for p in range(ref.shape[0])], axis=1)


def to_column(row, size):
    eye = iota((size, size), 0) == iota((size, size), 1)
    return jnp.sum(jnp.where(eye, jnp.broadcast_to(row, (size, size)), 0.0), axis=1, keepdims=True)


def half_masks(width):
    low = (iota((1, width), 1) % 128) < 64
    return jnp.where(low, 1.0, 0.0), jnp.where(low, 0.0, 1.0)


def row_scores_kernel(
    depth_hbm,
    place_ref,
    x_hbm,
    gain_hbm,
    prot_hbm,
    wq_hbm,
    wk_hbm,
    keep_ref,
    send_ref,
    normed_ref,
    same_ref,
    depth_ref,
    x_ref,
    gain_ref,
    prot_ref,
    wq_ref,
    wk_ref,
    sems,
):
    columns = prot_ref.shape[0]
    tokens, width = x_ref.shape
    rows = tokens // columns
    pairs = [(x_hbm, x_ref), (gain_hbm, gain_ref), (prot_hbm, prot_ref), (depth_hbm, depth_ref)]
    for n in range(width // 256):
        for source, target in ((wq_hbm, wq_ref), (wk_hbm, wk_ref)):
            pairs.append((source.at[256 * n : 256 * n + 256], target.at[256 * n : 256 * n + 256]))
    copies = [pltpu.make_async_copy(a, b, sems.at[i]) for i, (a, b) in enumerate(pairs)]
    for copy in copies:
        copy.start()
    for copy in copies[:2]:
        copy.wait()
    normed = norm(x_ref[...].astype(F32), gain_ref[...].reshape(1, width)).astype(BF16)
    normed_ref[...] = normed
    for copy in copies[2:4]:
        copy.wait()
    prot = prot_ref[...].reshape(1, columns).astype(F32)
    depth = jnp.zeros((1, columns), F32)
    for p in range(depth_ref.shape[0]):
        depth = jnp.where(prot == float(p), depth_ref[p].astype(F32), depth)
    prot_col = to_column(prot, columns)
    depth_col = to_column(depth, columns)
    same = jnp.broadcast_to(prot_col, (columns, columns)) == jnp.broadcast_to(prot, (columns, columns))
    same_f = jnp.where(same, 1.0, 0.0)
    same_ref[...] = same_f
    low = iota((columns, columns), 1) < 64
    first = jnp.where(low, same_f, pltpu.roll(same_f, 64, 1)) > 0.5
    valid = [
        jnp.where((place_ref[0] * rows + r).astype(F32) < depth_col, 1.0, 0.0) for r in range(rows)
    ]
    valid = jnp.concatenate(valid, axis=0)
    even, odd = half_masks(256)
    quarter = columns // PLANE
    core = (place_ref[0] % 2) == 0
    own = keep_ref.shape[1]
    for copy in copies[4:]:
        copy.wait()
    for n in range(width // 256):
        cols = slice(256 * n, 256 * n + 256)
        query = dot(normed, wq_ref[:, cols]).astype(BF16).astype(F32) * valid
        key = (dot(normed, wk_ref[:, cols]) * valid).astype(BF16)
        query_even, query_odd = (query * even).astype(BF16), (query * odd).astype(BF16)
        for q in range(2):
            lanes = slice(128 * q, 128 * q + 128)

            def side(array, lanes=lanes):
                return jnp.concatenate(
                    [array[r * columns : (r + 1) * columns, lanes] for r in range(rows)], axis=1
                )

            both = jnp.concatenate([side(query_even), side(query_odd)], axis=0)
            logits = dot_t(both, side(key))
            one, two = logits[:columns], logits[columns:]
            folded = jnp.where(
                low,
                jnp.where(first, one, pltpu.roll(one, 64, 1)),
                jnp.where(first, pltpu.roll(two, 64, 1), two),
            )
            out = slice(256 * n + 128 * q, 256 * n + 128 * q + 128)
            for y in range(PLANE // 2):
                start = 2 * y * quarter
                left, right = folded[start : start + quarter], folded[start + quarter : start + 2 * quarter]
                for target, value in ((keep_ref, jnp.where(core, left, right)), (send_ref, jnp.where(core, right, left))):
                    for i in range(quarter // own):
                        target[y * (quarter // own) + i, :, out] = value[i * own : (i + 1) * own]


def core_sum_kernel(place_ref, mine_ref, other_ref, *outs):
    plane, planes = place_ref[0] // PLANE, len(outs)
    for s, out in enumerate(outs):
        index = (plane + s) % planes
        out[...] = mine_ref[index] + other_ref[index]


def add_kernel(*refs):
    parts = [ref[...] for ref in refs[:-1]]
    while len(parts) > 1:
        parts = [a + b for a, b in zip(parts[::2], parts[1::2])]
    refs[-1][...] = parts[0]


def row_value_kernel(
    columns, place_ref, x_ref, w_ref, gain_ref, mine_ref, other_ref, out_ref, next_ref, spread_ref
):
    core = place_ref[0] % 2
    out_ref[...] = dot(x_ref[...], w_ref[...]).astype(BF16)
    normed = norm(other_ref[...].astype(F32), gain_ref[...]).astype(BF16)
    next_ref[...] = dot(normed, w_ref[...]).astype(BF16)
    rows = x_ref.shape[0] // columns
    quarter = columns // PLANE
    for source, index in ((mine_ref, core), (other_ref, 1 - core)):
        for r in range(rows):
            for y in range(2):
                start = pl.multiple_of(r * columns + y * columns // 2 + quarter * core, quarter)
                piece = source[pl.ds(start, quarter), :].astype(F32)
                target = pl.ds(2 * rows * quarter * y + index * rows + r, quarter, stride=2 * rows)
                for p in range(piece.shape[1] // 128):
                    spread_ref[p, target, :] = piece[:, 128 * p : 128 * p + 128]


def row_softmax_kernel(scale, place_ref, mine_ref, other_ref, same_ref, out_ref, mask_ref):
    own, width = out_ref.shape
    columns = same_ref.shape[0]
    quarter, local = columns // PLANE, columns // 2
    line, plane = (place_ref[0] // 2) % 2, place_ref[0] // PLANE
    same = same_ref[...]
    mask = jnp.maximum(same, pltpu.roll(same, 64, 1))
    for i in range(columns // own):
        mask_ref[i] = mask[i * own : (i + 1) * own]
    first = plane * own
    live = mask_ref[(first % quarter + quarter * line + local * (first // quarter)) // own] > 0.5
    low = iota((own, 128), 1) < 64
    for p in range(width // 128):
        lanes = slice(128 * p, 128 * p + 128)
        tied = jnp.where(live, (mine_ref[:, lanes] + other_ref[:, lanes]) * scale, NEG)
        top_low = jnp.max(jnp.where(low, tied, 2 * NEG), axis=1, keepdims=True)
        top_high = jnp.max(jnp.where(low, 2 * NEG, tied), axis=1, keepdims=True)
        value = jnp.exp(tied - jnp.where(low, top_low, top_high))
        sum_low = jnp.sum(jnp.where(low, value, 0.0), axis=1, keepdims=True)
        sum_high = jnp.sum(jnp.where(low, 0.0, value), axis=1, keepdims=True)
        out_ref[:, lanes] = (value / jnp.where(low, sum_low, sum_high)).astype(BF16)


def row_output_kernel(
    steps,
    place_ref,
    same_ref,
    value_ref,
    other_ref,
    x_ref,
    w_ref,
    gain_ref,
    *refs,
):
    planes = (len(refs) - 4) // 2
    pieces, after_ref, outs = refs[:planes], refs[planes], refs[planes + 1 : -3]
    mixed_ref, folded_ref, normed_ref = refs[-3:]
    columns = same_ref.shape[0]
    tokens, width = after_ref.shape
    rows = tokens // columns
    quarter, local = columns // PLANE, columns // 2
    place = place_ref[0]
    core, plane = place % 2, place // PLANE
    own = local // planes
    for s, piece in zip(steps, pieces):
        folded_ref[(plane + planes - s) % planes] = piece[...].astype(F32)
    same = [
        same_ref[pl.ds(pl.multiple_of(y * local + core * quarter, quarter), quarter), :] for y in range(2)
    ]
    same = jnp.concatenate(same, axis=0) > 0.5
    low = iota((local, columns), 1) < 64
    even, odd = half_masks(256 * rows)
    even, odd = even.astype(BF16), odd.astype(BF16)
    spots = [core * rows + r for r in range(rows)] + [(1 - core) * rows + r for r in range(rows)]
    for p in range(width // 128):
        lanes = slice(128 * p, 128 * p + 128)
        piece = folded_ref[:, :, lanes].reshape(local, 128)
        turned = pltpu.roll(piece, 64, 1)
        one = jnp.where(same, jnp.where(low, piece, turned), 0.0)
        two = jnp.where(same, jnp.where(low, turned, piece), 0.0)
        weights = jnp.concatenate([one, two], axis=1).astype(BF16)
        value = jnp.concatenate(
            [
                source[r * columns : (r + 1) * columns, lanes]
                for source in (value_ref, other_ref)
                for r in range(rows)
            ],
            axis=1,
        )
        value = jnp.concatenate([value * even, value * odd], axis=0)
        mixed = dot(weights, value)
        for i, spot in enumerate(spots):
            mixed_ref[p, pl.ds(spot, local, stride=2 * rows), :] = mixed[:, 128 * i : 128 * i + 128]
    after = (flat(x_ref) + dot(flat(mixed_ref).astype(BF16), w_ref[...])).astype(BF16)
    after_ref[...] = after
    normed_ref[...] = norm(after.astype(F32), gain_ref[...])
    size = tokens // len(outs)
    for s, out in enumerate(outs):
        start = pl.multiple_of(((plane + s) % len(outs)) * size, size)
        out[...] = normed_ref[pl.ds(start, size), :].astype(BF16)


def column_kernel(scale, steps, columns, depth_ref, prot_ref, place_ref, wq_ref, wk_ref, wv_ref, *refs):
    planes = len(steps)
    ins, (keep_ref, send_ref, all_ref, mixed_ref) = refs[: 2 * planes], refs[2 * planes :]
    size, width = ins[0].shape
    wide = width // 2
    slots, local = 2 * planes, columns // 2
    own = local // planes
    rows = size // own
    block = 4 if own % 4 == 0 else own
    piece = block * rows
    chunk = slots * piece
    chunks = own // block
    fold = piece // 8
    pair = 8 // rows
    place = place_ref[0]
    core, line, plane = place % 2, (place // 2) % 2, place // PLANE
    for g in range(chunks):
        for i, source in enumerate(ins):
            all_ref[g * chunk + i * piece : g * chunk + (i + 1) * piece, :] = source[g * piece : (g + 1) * piece, :]
    x = all_ref[...]
    heads = pl.ds(pl.multiple_of(core * wide, 128), wide)
    even, odd = half_masks(wide)
    query = dot(x, wq_ref[:, heads]).astype(BF16).astype(F32) * scale
    key = dot(x, wk_ref[:, heads]).astype(BF16)
    value = dot(x, wv_ref[:, heads]).astype(BF16)
    sides = [(query * side).astype(BF16) for side in (even, odd)]
    unit = jnp.where(iota((128, 128), 0) == iota((128, 128), 1), 1.0, 0.0).astype(BF16)
    lane = (iota((8, 2 * chunk), 1) % piece) // rows
    level = iota((8, 2 * chunk), 0)
    fits = level // rows == lane % pair
    mine = [jnp.where(lane // pair == v, 1.0, 0.0)[None] for v in range(fold)]
    lives = []
    for g in range(chunks):
        depth = jnp.zeros((8, 2 * chunk), jnp.int32)
        for c in range(block):
            index = plane * own + g * block + c
            column = index % (local // 2) + (local // 2) * line + local * (index // (local // 2))
            depth = jnp.where(lane == c, depth_ref[prot_ref[column]], depth)
        live = []
        for i in range(slots):
            away = ((plane + planes - steps[i % planes]) % planes) * 2 + (core if i < planes else 1 - core)
            live.append((fits & (level % rows + away * rows < depth))[None])
        lives.append(jnp.concatenate([jnp.where(l, 1.0, 0.0) for l in live], axis=0) > 0.5)
    packs, values = [], []
    for q in range(wide // 128):
        lanes = slice(128 * q, 128 * q + 128)
        for g in range(chunks):
            part = slice(g * chunk, g * chunk + chunk)
            both = jnp.concatenate([side[part, lanes] for side in sides], axis=0)
            scores = dot_t(key[part, lanes], both).reshape(slots, fold, 8, 2 * chunk)
            packed = scores[:, 0]
            for v in range(1, fold):
                packed = jnp.where(mine[v] > 0.5, scores[:, v], packed)
            packs.append(jnp.where(lives[g], packed, NEG))
        values.append(dot_t(unit, value[:, lanes]).astype(BF16))
    packs = [jnp.exp(packed - jnp.max(packed, axis=(0, 1), keepdims=True)) for packed in packs]
    packs = [packed * (1.0 / jnp.sum(packed, axis=(0, 1), keepdims=True)) for packed in packs]
    for q, value in enumerate(values):
        for g in range(chunks):
            part = slice(g * chunk, g * chunk + chunk)
            weight = packs[q * chunks + g]
            spread = jnp.stack([weight * m for m in mine], axis=1).reshape(chunk, 2 * chunk).astype(BF16)
            for s in range(2):
                mixed = dot(value[64 * s : 64 * s + 64, part], spread[:, s * chunk : (s + 1) * chunk])
                mixed_ref[128 * q + 64 * s : 128 * q + 64 * s + 64, part] = mixed.astype(BF16)
    turn = jnp.where(iota((chunk, chunk), 0) == iota((chunk, chunk), 1), 1.0, 0.0).astype(BF16)
    for g in range(chunks):
        mixed = dot_t(turn, mixed_ref[:, g * chunk : (g + 1) * chunk])
        for i in range(slots):
            target = keep_ref if i < planes else send_ref
            target[i % planes, g * piece : (g + 1) * piece, :] = mixed[i * piece : (i + 1) * piece].astype(BF16)


def join_kernel(place_ref, keep_ref, other_ref, *outs):
    wide = keep_ref.shape[2]
    core = place_ref[0] % 2

    def write(left, right):
        for s, out in enumerate(outs):
            out[:, :wide] = left[s]
            out[:, wide:] = right[s]

    @pl.when(core == 0)
    def _():
        write(keep_ref, other_ref)

    @pl.when(core == 1)
    def _():
        write(other_ref, keep_ref)


def column_output_kernel(steps, place_ref, w_ref, after_ref, *refs):
    ins, (keep_ref, send_ref, total_ref) = refs[:-3], refs[-3:]
    rows, local, _ = keep_ref.shape
    core, plane = place_ref[0] % 2, place_ref[0] // PLANE
    size = ins[0].shape[0]
    total = dot(jnp.concatenate([source[...] for source in ins], axis=0), w_ref[...])
    for i, s in enumerate(steps):
        start = pl.multiple_of(((plane + s) % len(ins)) * size, size)
        for p in range(total.shape[1] // 128):
            total_ref[p, pl.ds(start, size), :] = total[i * size : (i + 1) * size, 128 * p : 128 * p + 128]
    for p in range(total.shape[1] // 128):
        lanes = slice(128 * p, 128 * p + 128)
        total_ref[p] = total_ref[p] + after_ref[:, lanes].astype(F32)
        for r in range(rows):
            for target, index in ((keep_ref, core), (send_ref, 1 - core)):
                row = total_ref[p, pl.ds(index * rows + r, local, stride=2 * rows), :]
                target[r, :, lanes] = row.astype(BF16)


def assemble_kernel(place_ref, mine_ref, other_ref, out_ref, sems):
    core = place_ref[0] % 2
    local = mine_ref.shape[1]
    quarter = local // 2
    copies = []
    for source, index in ((mine_ref, core), (other_ref, 1 - core)):
        for y in range(2):
            start = pl.multiple_of(y * local + index * quarter, quarter)
            copies.append(
                pltpu.make_async_copy(
                    source.at[:, y * quarter : (y + 1) * quarter, :],
                    out_ref.at[:, pl.ds(start, quarter), :],
                    sems.at[len(copies)],
                )
            )
    for copy in copies:
        copy.start()
    for copy in copies:
        copy.wait()


def hbm(array):
    return pltpu.with_memory_space_constraint(array, pltpu.HBM)


def swap(array, offset):
    devices = lax.axis_size("seq")
    return lax.ppermute(array, "seq", [(i, i ^ offset) for i in range(devices)])


def spin_pairs(step):
    planes = lax.axis_size("seq") // PLANE
    pairs = []
    for z in range(planes):
        for y in range(2):
            for k in range(2):
                pairs.append((z * PLANE + 2 * y + k, (z + step) % planes * PLANE + 2 * k + y))
    return pairs


def far_first(planes):
    return sorted(range(planes), key=lambda s: (-min(s, planes - s), s))


def spin(array, step):
    return lax.ppermute(array, "seq", spin_pairs(step))


def spin_back(array, step):
    return lax.ppermute(array, "seq", [(b, a) for a, b in spin_pairs(step)])


def per_device(
    alignment,
    protein_id,
    row_depth,
    row_gain,
    row_query,
    row_key,
    row_value,
    row_output,
    column_gain,
    column_query,
    column_key,
    column_value,
    column_output,
):
    rows, columns, width = alignment.shape
    devices = lax.axis_size("seq")
    place = lax.axis_index("seq").astype(jnp.int32)[None]
    total_rows = rows * devices
    head_size = width // H
    tokens = rows * columns
    planes, local = devices // PLANE, columns // 2
    size = tokens // planes
    sum_steps = move_steps = back_steps = far_first(planes)
    share_steps = far_first(planes)
    share_steps = share_steps[1:] + share_steps[:1]
    x = alignment.reshape(tokens, width)
    shape = jax.ShapeDtypeStruct
    square = 2 * tokens * width * width

    half = shape((planes, local // planes, width), F32)
    part = shape((local // planes, width), F32)
    keep, send, normed, same = call(
        row_scores_kernel,
        (half, half, shape((tokens, width), BF16), shape((columns, columns), F32)),
        "hshhhhh",
        "vvvv",
        [
            pltpu.SMEM(row_depth.shape, jnp.int32),
            pltpu.VMEM((tokens, width), BF16),
            pltpu.VMEM((width,), F32),
            pltpu.VMEM((columns,), jnp.int32),
            pltpu.VMEM((width, width), BF16),
            pltpu.VMEM((width, width), BF16),
            pltpu.SemaphoreType.DMA((4 + 2 * (width // 256),)),
        ],
        (2 * square, 4 * width * width, tokens),
        "row_scores",
    )(hbm(row_depth), place, hbm(x), hbm(row_gain), hbm(protein_id), hbm(row_query), hbm(row_key))
    column_query, column_key, column_value, late, normed = lax.optimization_barrier(
        (column_query, column_key, column_value, x, normed)
    )
    other = swap(send, 1)
    sibling = swap(late, 1)
    pieces = call(
        core_sum_kernel,
        (part,) * planes,
        "svv",
        "v" * planes,
        [],
        (columns * width, 6 * columns * width, 0),
        "core_sum",
    )(place, keep, other)
    (total,) = call(
        add_kernel, (part,), "v" * planes, "v", [], (columns * width, 2 * columns * width, 0), "add"
    )(*[spin(pieces[s], s) for s in sum_steps])
    value, value_other, spread = call(
        functools.partial(row_value_kernel, columns),
        (shape((tokens, width), BF16),) * 2 + (shape((width // 128, tokens, 128), F32),),
        "svvvvv",
        "vvv",
        [],
        (2 * square, 2 * width * width, 0),
        "row_value",
    )(place, normed, row_value, row_gain[None], late, sibling)
    (weights,) = call(
        functools.partial(row_softmax_kernel, 1.0 / (math.sqrt(head_size) * math.sqrt(total_rows))),
        (shape((local // planes, width), BF16),),
        "svvv",
        "v",
        [pltpu.VMEM((columns * planes // local, local // planes, columns), F32)],
        (columns * width, 2 * columns * width, columns * width // 8),
        "row_softmax",
    )(place, total, swap(total, 1), same)
    shared = [spin(weights, s) for s in share_steps]
    after, *blocks = call(
        functools.partial(row_output_kernel, share_steps),
        (shape((tokens, width), BF16),) + (shape((size, width), BF16),) * planes,
        "s" + "v" * (6 + planes),
        "v" * (1 + planes),
        [
            pltpu.VMEM((width // 128, tokens, 128), F32),
            pltpu.VMEM((planes, local // planes, width), F32),
            pltpu.VMEM((tokens, width), F32),
        ],
        (square, 2 * width * width, tokens),
        "row_output",
    )(place, same, value, value_other, spread, row_output, column_gain[None], *shared)
    moved = [spin(blocks[s], s) for s in move_steps]
    moved += [swap(block, 1) for block in moved]
    wide = width // 2
    halves = shape((planes, size, wide), BF16)
    keep, send = call(
        functools.partial(column_kernel, 1.0 / math.sqrt(head_size), move_steps, columns),
        (halves, halves),
        "sss" + "v" * (3 + 2 * planes),
        "vv",
        [pltpu.VMEM((2 * tokens, width), BF16), pltpu.VMEM((wide, 2 * tokens), BF16)],
        (4 * square, 6 * width * width, H * tokens * tokens // 4),
        "column_attention",
    )(row_depth, protein_id, place, column_query, column_key, column_value, *moved)
    joined = call(
        join_kernel,
        (shape((size, width), BF16),) * planes,
        "svv",
        "v" * planes,
        [],
        (tokens * width, 4 * tokens * width, 0),
        "join",
    )(place, keep, swap(send, 1))
    returned = [spin_back(joined[move_steps.index(s)], s) for s in back_steps]
    half = shape((rows, local, width), BF16)
    keep, send = call(
        functools.partial(column_output_kernel, back_steps),
        (half, half),
        "svv" + "v" * planes,
        "vv",
        [pltpu.VMEM((width // 128, tokens, 128), F32)],
        (square, 2 * width * width, 0),
        "column_output",
    )(place, column_output, after, *returned)
    (out,) = call(
        assemble_kernel,
        (shape((rows, columns, width), BF16),),
        "svv",
        "a",
        [pltpu.SemaphoreType.DMA((4,))],
        (tokens * width, 4 * tokens * width, 0),
        "assemble",
    )(place, keep, swap(send, 1))
    return out


def solution(mesh):
    return jax.shard_map(
        per_device,
        mesh=mesh,
        in_specs=(P(("grp", "seq"), None, None), P("grp"), P("grp")) + (P(),) * 10,
        out_specs=P(("grp", "seq"), None, None),
        check_vma=False,
    )
```

```python
import functools
import math

import jax
import jax.numpy as jnp
from jax import lax
from jax.experimental import pallas as pl
from jax.experimental.pallas import tpu as pltpu
from jax.sharding import PartitionSpec as P

H = 12
EPS = 1e-05
NEG = -1000000000.0
F32 = jnp.float32
BF16 = jnp.bfloat16
LIMIT = 20 << 20
PLANE = 4


def call(kernel, out_shape, ins, outs, scratch, cost, name):
    spaces = {"v": pltpu.VMEM, "s": pltpu.SMEM, "h": pltpu.HBM, "a": pl.ANY}
    return pl.pallas_call(
        kernel,
        out_shape=out_shape,
        in_specs=[pl.BlockSpec(memory_space=spaces[c]) for c in ins],
        out_specs=[pl.BlockSpec(memory_space=spaces[c]) for c in outs],
        scratch_shapes=scratch,
        compiler_params=pltpu.CompilerParams(vmem_limit_bytes=LIMIT),
        cost_estimate=pl.CostEstimate(flops=cost[0], bytes_accessed=cost[1], transcendentals=cost[2]),
        name=name,
    )


def norm(full, gain):
    middle = jnp.mean(full, axis=-1, keepdims=True)
    spread = jnp.mean((full - middle) ** 2, axis=-1, keepdims=True)
    return (full - middle) * lax.rsqrt(spread + EPS) * gain


def dot(a, b):
    return jnp.dot(a, b, preferred_element_type=F32)


def dot_t(a, b):
    return lax.dot_general(a, b, (((1,), (1,)), ((), ())), preferred_element_type=F32)


def iota(shape, dim):
    return lax.broadcasted_iota(jnp.int32, shape, dim)


def flat(ref):
    return jnp.concatenate([ref[p] for p in range(ref.shape[0])], axis=1)


def to_column(row, size):
    eye = iota((size, size), 0) == iota((size, size), 1)
    return jnp.sum(jnp.where(eye, jnp.broadcast_to(row, (size, size)), 0.0), axis=1, keepdims=True)


def half_masks(width):
    low = (iota((1, width), 1) % 128) < 64
    return jnp.where(low, 1.0, 0.0), jnp.where(low, 0.0, 1.0)


def own_columns(array, core, quarter):
    pieces = []
    for y in range(PLANE // 2):
        left, right = (array[(2 * y + k) * quarter : (2 * y + k + 1) * quarter] for k in range(2))
        pieces.append(jnp.where(core, left, right))
    return jnp.concatenate(pieces, axis=0)


def query_tokens(normed_ref, place_ref, columns):
    quarter = columns // PLANE
    core = place_ref[0] % 2
    pieces = []
    for start in range(0, normed_ref.shape[0], columns // 2):
        pieces.append(normed_ref[pl.ds(pl.multiple_of(start + core * quarter, quarter), quarter), :])
    return jnp.concatenate(pieces, axis=0)


def row_own_kernel(
    columns,
    place_ref,
    x_hbm,
    gain_hbm,
    wq_hbm,
    wk_hbm,
    normed_ref,
    query_ref,
    key_ref,
    wq_ref,
    wk_ref,
    x_ref,
    gain_ref,
    sems,
):
    tokens, width = x_ref.shape
    pairs = [(x_hbm, x_ref), (gain_hbm, gain_ref)]
    for n in range(width // 256):
        for source, target in ((wq_hbm, wq_ref), (wk_hbm, wk_ref)):
            pairs.append((source.at[256 * n : 256 * n + 256], target.at[256 * n : 256 * n + 256]))
    copies = [pltpu.make_async_copy(a, b, sems.at[i]) for i, (a, b) in enumerate(pairs)]
    for copy in copies:
        copy.start()
    for copy in copies[:2]:
        copy.wait()
    normed_ref[...] = norm(x_ref[...].astype(F32), gain_ref[...].reshape(1, width)).astype(BF16)
    for copy in copies[2:]:
        copy.wait()
    query_ref[...] = dot(query_tokens(normed_ref, place_ref, columns), wq_ref[...]).astype(BF16)
    key_ref[...] = dot(normed_ref[...], wk_ref[...]).astype(BF16)


def row_scores_kernel(
    depth_ref,
    place_ref,
    x_ref,
    gain_ref,
    prot_ref,
    wq_ref,
    wk_ref,
    query_ref,
    key_ref,
    *refs,
):
    outs, (normed_ref, same_ref, part_ref) = refs[:-3], refs[-3:]
    columns = prot_ref.shape[0]
    tokens, width = x_ref.shape
    rows, local, quarter = tokens // columns, columns // 2, columns // PLANE
    planes, own = part_ref.shape[:2]
    place = place_ref[0]
    core = (place % 2) == 0
    normed_ref[...] = norm(x_ref[...].astype(F32), gain_ref[...].reshape(1, width)).astype(BF16)
    prot = prot_ref[...].reshape(1, columns).astype(F32)
    depth = jnp.zeros((1, columns), F32)
    for p in range(depth_ref.shape[0]):
        depth = jnp.where(prot == float(p), depth_ref[p].astype(F32), depth)
    prot_col = to_column(prot, columns)
    depth_col = to_column(depth, columns)
    same = jnp.broadcast_to(prot_col, (columns, columns)) == jnp.broadcast_to(prot, (columns, columns))
    same_f = jnp.where(same, 1.0, 0.0)
    same_ref[...] = same_f
    same_l = own_columns(same_f, core, quarter)
    depth_l = own_columns(depth_col, core, quarter)
    low = iota((local, columns), 1) < 64
    first = jnp.where(low, same_l, pltpu.roll(same_l, 64, 1)) > 0.5
    even, odd = half_masks(256)
    other = place + 1 - 2 * (place % 2)
    ids = [place * rows + r for r in range(rows)] + [other * rows + r for r in range(rows)]
    seen_q = [jnp.where(i.astype(F32) < depth_l, 1.0, 0.0) for i in ids]
    seen_k = [jnp.where(i.astype(F32) < depth_col, 1.0, 0.0) for i in ids]
    tokens_q = query_tokens(normed_ref, place_ref, columns)
    for n in range(width // 256):
        cols = slice(256 * n, 256 * n + 256)
        queries = (query_ref[:, cols].astype(F32), dot(tokens_q, wq_ref[:, cols]).astype(BF16).astype(F32))
        keys = (key_ref[:, cols].astype(F32), dot(normed_ref[...], wk_ref[:, cols]))
        query, key = [], []
        for i in range(2 * rows):
            r = i % rows
            query.append(queries[i // rows][r * local : (r + 1) * local] * seen_q[i])
            key.append((keys[i // rows][r * columns : (r + 1) * columns] * seen_k[i]).astype(BF16))
        query_sides = [[(q * side).astype(BF16) for q in query] for side in (even, odd)]
        for q in range(2):
            lanes = slice(128 * q, 128 * q + 128)
            both = [jnp.concatenate([a[:, lanes] for a in side], axis=1) for side in query_sides]
            both = jnp.concatenate(both, axis=0)
            logits = dot_t(both, jnp.concatenate([a[:, lanes] for a in key], axis=1))
            one, two = logits[:local], logits[local:]
            folded = jnp.where(
                low,
                jnp.where(first, one, pltpu.roll(one, 64, 1)),
                jnp.where(first, pltpu.roll(two, 64, 1), two),
            )
            out = slice(256 * n + 128 * q, 256 * n + 128 * q + 128)
            for i in range(planes):
                part_ref[i, :, out] = folded[i * own : (i + 1) * own]
    plane = place // PLANE
    for s, target in enumerate(outs):
        target[...] = part_ref[(plane + s) % planes]


def add_kernel(*refs):
    parts = [ref[...] for ref in refs[:-1]]
    while len(parts) > 1:
        parts = [a + b for a, b in zip(parts[::2], parts[1::2])]
    refs[-1][...] = parts[0]


def row_value_kernel(
    columns, place_ref, x_ref, y_ref, w_ref, mine_ref, other_ref, out_ref, next_ref, spread_ref
):
    core = place_ref[0] % 2
    out_ref[...] = dot(x_ref[...], w_ref[...]).astype(BF16)
    next_ref[...] = dot(y_ref[...], w_ref[...]).astype(BF16)
    rows = x_ref.shape[0] // columns
    quarter = columns // PLANE
    for source, index in ((mine_ref, core), (other_ref, 1 - core)):
        for r in range(rows):
            for y in range(2):
                start = pl.multiple_of(r * columns + y * columns // 2 + quarter * core, quarter)
                piece = source[pl.ds(start, quarter), :].astype(F32)
                target = pl.ds(2 * rows * quarter * y + index * rows + r, quarter, stride=2 * rows)
                for p in range(piece.shape[1] // 128):
                    spread_ref[p, target, :] = piece[:, 128 * p : 128 * p + 128]


def row_softmax_kernel(scale, place_ref, mine_ref, other_ref, same_ref, out_ref, mask_ref):
    own, width = out_ref.shape
    columns = same_ref.shape[0]
    quarter, local = columns // PLANE, columns // 2
    line, plane = (place_ref[0] // 2) % 2, place_ref[0] // PLANE
    same = same_ref[...]
    mask = jnp.maximum(same, pltpu.roll(same, 64, 1))
    for i in range(columns // own):
        mask_ref[i] = mask[i * own : (i + 1) * own]
    first = plane * own
    live = mask_ref[(first % quarter + quarter * line + local * (first // quarter)) // own] > 0.5
    low = iota((own, 128), 1) < 64
    for p in range(width // 128):
        lanes = slice(128 * p, 128 * p + 128)
        tied = jnp.where(live, (mine_ref[:, lanes] + other_ref[:, lanes]) * scale, NEG)
        top_low = jnp.max(jnp.where(low, tied, 2 * NEG), axis=1, keepdims=True)
        top_high = jnp.max(jnp.where(low, 2 * NEG, tied), axis=1, keepdims=True)
        value = jnp.exp(tied - jnp.where(low, top_low, top_high))
        sum_low = jnp.sum(jnp.where(low, value, 0.0), axis=1, keepdims=True)
        sum_high = jnp.sum(jnp.where(low, 0.0, value), axis=1, keepdims=True)
        out_ref[:, lanes] = (value / jnp.where(low, sum_low, sum_high)).astype(BF16)


def row_output_kernel(
    steps,
    place_ref,
    same_ref,
    value_ref,
    other_ref,
    x_ref,
    w_ref,
    gain_ref,
    *refs,
):
    planes = (len(refs) - 4) // 2
    pieces, after_ref, outs = refs[:planes], refs[planes], refs[planes + 1 : -3]
    mixed_ref, folded_ref, normed_ref = refs[-3:]
    columns = same_ref.shape[0]
    tokens, width = after_ref.shape
    rows = tokens // columns
    quarter, local = columns // PLANE, columns // 2
    place = place_ref[0]
    core, plane = place % 2, place // PLANE
    own = local // planes
    for s, piece in zip(steps, pieces):
        folded_ref[(plane + planes - s) % planes] = piece[...].astype(F32)
    same = [
        same_ref[pl.ds(pl.multiple_of(y * local + core * quarter, quarter), quarter), :] for y in range(2)
    ]
    same = jnp.concatenate(same, axis=0) > 0.5
    low = iota((local, columns), 1) < 64
    even, odd = half_masks(256 * rows)
    even, odd = even.astype(BF16), odd.astype(BF16)
    spots = [core * rows + r for r in range(rows)] + [(1 - core) * rows + r for r in range(rows)]
    for p in range(width // 128):
        lanes = slice(128 * p, 128 * p + 128)
        piece = folded_ref[:, :, lanes].reshape(local, 128)
        turned = pltpu.roll(piece, 64, 1)
        one = jnp.where(same, jnp.where(low, piece, turned), 0.0)
        two = jnp.where(same, jnp.where(low, turned, piece), 0.0)
        weights = jnp.concatenate([one, two], axis=1).astype(BF16)
        value = jnp.concatenate(
            [
                source[r * columns : (r + 1) * columns, lanes]
                for source in (value_ref, other_ref)
                for r in range(rows)
            ],
            axis=1,
        )
        value = jnp.concatenate([value * even, value * odd], axis=0)
        mixed = dot(weights, value)
        for i, spot in enumerate(spots):
            mixed_ref[p, pl.ds(spot, local, stride=2 * rows), :] = mixed[:, 128 * i : 128 * i + 128]
    after = (flat(x_ref) + dot(flat(mixed_ref).astype(BF16), w_ref[...])).astype(BF16)
    after_ref[...] = after
    normed_ref[...] = norm(after.astype(F32), gain_ref[...])
    size = tokens // len(outs)
    for s, out in enumerate(outs):
        start = pl.multiple_of(((plane + s) % len(outs)) * size, size)
        out[...] = normed_ref[pl.ds(start, size), :].astype(BF16)


def pack_kernel(*refs):
    for i, source in enumerate(refs[:-1]):
        refs[-1][i] = source[...]


def block_of(own):
    return 4 if own % 4 == 0 else own


def heads_of(place_ref, wide):
    return pl.ds(pl.multiple_of(place_ref[0] % 2 * wide, 128), wide)


def column_project_kernel(planes, columns, place_ref, wq_ref, wk_ref, wv_ref, *refs):
    ins, (query_ref, key_ref, value_ref, all_ref) = refs[:planes], refs[planes:]
    gather_tokens(ins, columns, all_ref)
    heads = heads_of(place_ref, query_ref.shape[1])
    for w_ref, out in ((wq_ref, query_ref), (wk_ref, key_ref), (wv_ref, value_ref)):
        out[...] = dot(all_ref[...], w_ref[:, heads]).astype(BF16)


def gather_tokens(sources, columns, all_ref):
    planes = len(sources)
    own = columns // 2 // planes
    piece = block_of(own) * sources[0].shape[0] // own
    for g in range(own // block_of(own)):
        for i, source in enumerate(sources):
            start = (g * planes + i) * piece
            all_ref[start : start + piece, :] = source[g * piece : (g + 1) * piece, :]


def column_kernel(
    scale,
    steps,
    columns,
    depth_ref,
    prot_ref,
    place_ref,
    wq_ref,
    wk_ref,
    wv_ref,
    query_ref,
    key_ref,
    value_ref,
    other_ref,
    keep_ref,
    send_ref,
    all_ref,
    mixed_ref,
):
    planes, size, width = other_ref.shape
    wide = width // 2
    slots, local = 2 * planes, columns // 2
    own = local // planes
    rows = size // own
    block = block_of(own)
    piece = block * rows
    chunk = slots * piece
    chunks = own // block
    fold = piece // 8
    pair = 8 // rows
    place = place_ref[0]
    core, line, plane = place % 2, (place // 2) % 2, place // PLANE
    gather_tokens([other_ref.at[i] for i in range(planes)], columns, all_ref)
    heads = heads_of(place_ref, wide)
    full = []
    for mine_ref, w_ref in ((query_ref, wq_ref), (key_ref, wk_ref), (value_ref, wv_ref)):
        other = dot(all_ref[...], w_ref[:, heads]).astype(BF16)
        mine = mine_ref[...]
        parts = []
        for start in range(0, planes * size, chunk // 2):
            parts += [mine[start : start + chunk // 2], other[start : start + chunk // 2]]
        full.append(jnp.concatenate(parts, axis=0))
    query, key, value = full
    query = query.astype(F32) * scale
    even, odd = half_masks(wide)
    sides = [(query * side).astype(BF16) for side in (even, odd)]
    unit = jnp.where(iota((128, 128), 0) == iota((128, 128), 1), 1.0, 0.0).astype(BF16)
    lane = (iota((8, 2 * chunk), 1) % piece) // rows
    level = iota((8, 2 * chunk), 0)
    fits = level // rows == lane % pair
    mine = [jnp.where(lane // pair == v, 1.0, 0.0)[None] for v in range(fold)]
    lives = []
    for g in range(chunks):
        depth = jnp.zeros((8, 2 * chunk), jnp.int32)
        for c in range(block):
            index = plane * own + g * block + c
            column = index % (local // 2) + (local // 2) * line + local * (index // (local // 2))
            depth = jnp.where(lane == c, depth_ref[prot_ref[column]], depth)
        live = []
        for i in range(slots):
            away = ((plane + planes - steps[i % planes]) % planes) * 2 + (core if i < planes else 1 - core)
            live.append((fits & (level % rows + away * rows < depth))[None])
        lives.append(jnp.concatenate([jnp.where(l, 1.0, 0.0) for l in live], axis=0) > 0.5)
    packs, values = [], []
    for q in range(wide // 128):
        lanes = slice(128 * q, 128 * q + 128)
        for g in range(chunks):
            part = slice(g * chunk, g * chunk + chunk)
            both = jnp.concatenate([side[part, lanes] for side in sides], axis=0)
            scores = dot_t(key[part, lanes], both).reshape(slots, fold, 8, 2 * chunk)
            packed = scores[:, 0]
            for v in range(1, fold):
                packed = jnp.where(mine[v] > 0.5, scores[:, v], packed)
            packs.append(jnp.where(lives[g], packed, NEG))
        values.append(dot_t(unit, value[:, lanes]).astype(BF16))
    packs = [jnp.exp(packed - jnp.max(packed, axis=(0, 1), keepdims=True)) for packed in packs]
    packs = [packed * (1.0 / jnp.sum(packed, axis=(0, 1), keepdims=True)) for packed in packs]
    for q, value in enumerate(values):
        for g in range(chunks):
            part = slice(g * chunk, g * chunk + chunk)
            weight = packs[q * chunks + g]
            spread = jnp.stack([weight * m for m in mine], axis=1).reshape(chunk, 2 * chunk).astype(BF16)
            for s in range(2):
                mixed = dot(value[64 * s : 64 * s + 64, part], spread[:, s * chunk : (s + 1) * chunk])
                mixed_ref[128 * q + 64 * s : 128 * q + 64 * s + 64, part] = mixed.astype(BF16)
    turn = jnp.where(iota((chunk, chunk), 0) == iota((chunk, chunk), 1), 1.0, 0.0).astype(BF16)
    for g in range(chunks):
        mixed = dot_t(turn, mixed_ref[:, g * chunk : (g + 1) * chunk])
        for i in range(slots):
            target = keep_ref if i < planes else send_ref
            target[i % planes, g * piece : (g + 1) * piece, :] = mixed[i * piece : (i + 1) * piece].astype(BF16)


def join_kernel(place_ref, keep_ref, other_ref, *outs):
    wide = keep_ref.shape[2]
    core = place_ref[0] % 2

    def write(left, right):
        for s, out in enumerate(outs):
            out[:, :wide] = left[s]
            out[:, wide:] = right[s]

    @pl.when(core == 0)
    def _():
        write(keep_ref, other_ref)

    @pl.when(core == 1)
    def _():
        write(other_ref, keep_ref)


def column_output_kernel(steps, place_ref, w_ref, after_ref, *refs):
    ins, (keep_ref, send_ref, total_ref) = refs[:-3], refs[-3:]
    rows, local, _ = keep_ref.shape
    core, plane = place_ref[0] % 2, place_ref[0] // PLANE
    size = ins[0].shape[0]
    total = dot(jnp.concatenate([source[...] for source in ins], axis=0), w_ref[...])
    for i, s in enumerate(steps):
        start = pl.multiple_of(((plane + s) % len(ins)) * size, size)
        for p in range(total.shape[1] // 128):
            total_ref[p, pl.ds(start, size), :] = total[i * size : (i + 1) * size, 128 * p : 128 * p + 128]
    for p in range(total.shape[1] // 128):
        lanes = slice(128 * p, 128 * p + 128)
        total_ref[p] = total_ref[p] + after_ref[:, lanes].astype(F32)
        for r in range(rows):
            for target, index in ((keep_ref, core), (send_ref, 1 - core)):
                row = total_ref[p, pl.ds(index * rows + r, local, stride=2 * rows), :]
                target[r, :, lanes] = row.astype(BF16)


def assemble_kernel(place_ref, mine_ref, other_ref, out_ref, sems):
    core = place_ref[0] % 2
    local = mine_ref.shape[1]
    quarter = local // 2
    copies = []
    for source, index in ((mine_ref, core), (other_ref, 1 - core)):
        for y in range(2):
            start = pl.multiple_of(y * local + index * quarter, quarter)
            copies.append(
                pltpu.make_async_copy(
                    source.at[:, y * quarter : (y + 1) * quarter, :],
                    out_ref.at[:, pl.ds(start, quarter), :],
                    sems.at[len(copies)],
                )
            )
    for copy in copies:
        copy.start()
    for copy in copies:
        copy.wait()


def hbm(array):
    return pltpu.with_memory_space_constraint(array, pltpu.HBM)


def swap(array, offset):
    devices = lax.axis_size("seq")
    return lax.ppermute(array, "seq", [(i, i ^ offset) for i in range(devices)])


def spin_pairs(step):
    planes = lax.axis_size("seq") // PLANE
    pairs = []
    for z in range(planes):
        for y in range(2):
            for k in range(2):
                pairs.append((z * PLANE + 2 * y + k, (z + step) % planes * PLANE + 2 * k + y))
    return pairs


def far_first(planes):
    return sorted(range(planes), key=lambda s: (-min(s, planes - s), s))


def spin(array, step):
    return lax.ppermute(array, "seq", spin_pairs(step))


def spin_back(array, step):
    return lax.ppermute(array, "seq", [(b, a) for a, b in spin_pairs(step)])


def per_device(
    alignment,
    protein_id,
    row_depth,
    row_gain,
    row_query,
    row_key,
    row_value,
    row_output,
    column_gain,
    column_query,
    column_key,
    column_value,
    column_output,
):
    rows, columns, width = alignment.shape
    devices = lax.axis_size("seq")
    place = lax.axis_index("seq").astype(jnp.int32)[None]
    total_rows = rows * devices
    head_size = width // H
    tokens = rows * columns
    planes, local = devices // PLANE, columns // 2
    size = tokens // planes
    sum_steps = move_steps = back_steps = far_first(planes)
    share_steps = far_first(planes)
    x = alignment.reshape(tokens, width)
    shape = jax.ShapeDtypeStruct
    square = 2 * tokens * width * width

    part = shape((local // planes, width), F32)
    matrix = shape((width, width), BF16)
    sibling = swap(x, 1)
    normed, query, key, row_query, row_key = call(
        functools.partial(row_own_kernel, columns),
        (shape((tokens, width), BF16), shape((tokens // 2, width), BF16), shape((tokens, width), BF16), matrix, matrix),
        "shhhh",
        "vvvvv",
        [
            pltpu.VMEM((tokens, width), BF16),
            pltpu.VMEM((width,), F32),
            pltpu.SemaphoreType.DMA((2 + 2 * (width // 256),)),
        ],
        (3 * square // 2, 4 * width * width, tokens),
        "row_own",
    )(place, hbm(x), hbm(row_gain), hbm(row_query), hbm(row_key))
    *pieces, normed_other, same = call(
        row_scores_kernel,
        (part,) * planes + (shape((tokens, width), BF16), shape((columns, columns), F32)),
        "ss" + "v" * 7,
        "v" * (planes + 2),
        [pltpu.VMEM((planes, local // planes, width), F32)],
        (3 * square // 2, 4 * width * width, tokens),
        "row_scores",
    )(row_depth, place, sibling, row_gain, protein_id, row_query, row_key, query, key)
    column_query, column_key, column_value, late, normed = lax.optimization_barrier(
        (column_query, column_key, column_value, x, normed)
    )
    (total,) = call(
        add_kernel, (part,), "v" * planes, "v", [], (columns * width, 2 * columns * width, 0), "add"
    )(*[spin(pieces[s], s) for s in sum_steps])
    value, value_other, spread = call(
        functools.partial(row_value_kernel, columns),
        (shape((tokens, width), BF16),) * 2 + (shape((width // 128, tokens, 128), F32),),
        "svvvvv",
        "vvv",
        [],
        (2 * square, 2 * width * width, 0),
        "row_value",
    )(place, normed, normed_other, row_value, late, sibling)
    (weights,) = call(
        functools.partial(row_softmax_kernel, 1.0 / (math.sqrt(head_size) * math.sqrt(total_rows))),
        (shape((local // planes, width), BF16),),
        "svvv",
        "v",
        [pltpu.VMEM((columns * planes // local, local // planes, columns), F32)],
        (columns * width, 2 * columns * width, columns * width // 8),
        "row_softmax",
    )(place, total, swap(total, 1), same)
    shared = [spin(weights, s) for s in share_steps]
    after, *blocks = call(
        functools.partial(row_output_kernel, share_steps),
        (shape((tokens, width), BF16),) + (shape((size, width), BF16),) * planes,
        "s" + "v" * (6 + planes),
        "v" * (1 + planes),
        [
            pltpu.VMEM((width // 128, tokens, 128), F32),
            pltpu.VMEM((planes, local // planes, width), F32),
            pltpu.VMEM((tokens, width), F32),
        ],
        (square, 2 * width * width, tokens),
        "row_output",
    )(place, same, value, value_other, spread, row_output, column_gain[None], *shared)
    moved = [spin(blocks[s], s) for s in move_steps]
    wide = width // 2
    (packed,) = call(
        pack_kernel,
        (shape((planes, size, width), BF16),),
        "v" * planes,
        "v",
        [],
        (tokens * width, 4 * tokens * width, 0),
        "pack",
    )(*moved)
    ours = call(
        functools.partial(column_project_kernel, planes, columns),
        (shape((tokens, wide), BF16),) * 3,
        "svvv" + "v" * planes,
        "vvv",
        [pltpu.VMEM((tokens, width), BF16)],
        (3 * square // 2, 3 * width * width, 0),
        "column_project",
    )(place, column_query, column_key, column_value, *moved)
    halves = shape((planes, size, wide), BF16)
    keep, send = call(
        functools.partial(column_kernel, 1.0 / math.sqrt(head_size), move_steps, columns),
        (halves, halves),
        "sss" + "v" * 7,
        "vv",
        [pltpu.VMEM((tokens, width), BF16), pltpu.VMEM((wide, 2 * tokens), BF16)],
        (4 * square, 6 * width * width, H * tokens * tokens // 4),
        "column_attention",
    )(row_depth, protein_id, place, column_query, column_key, column_value, *ours, swap(packed, 1))
    joined = call(
        join_kernel,
        (shape((size, width), BF16),) * planes,
        "svv",
        "v" * planes,
        [],
        (tokens * width, 4 * tokens * width, 0),
        "join",
    )(place, keep, swap(send, 1))
    returned = [spin_back(joined[move_steps.index(s)], s) for s in back_steps]
    half = shape((rows, local, width), BF16)
    keep, send = call(
        functools.partial(column_output_kernel, back_steps),
        (half, half),
        "svv" + "v" * planes,
        "vv",
        [pltpu.VMEM((width // 128, tokens, 128), F32)],
        (square, 2 * width * width, 0),
        "column_output",
    )(place, column_output, after, *returned)
    (out,) = call(
        assemble_kernel,
        (shape((rows, columns, width), BF16),),
        "svv",
        "a",
        [pltpu.SemaphoreType.DMA((4,))],
        (tokens * width, 4 * tokens * width, 0),
        "assemble",
    )(place, keep, swap(send, 1))
    return out


def solution(mesh):
    return jax.shard_map(
        per_device,
        mesh=mesh,
        in_specs=(P(("grp", "seq"), None, None), P("grp"), P("grp")) + (P(),) * 10,
        out_specs=P(("grp", "seq"), None, None),
        check_vma=False,
    )
```

```python
import functools
import math

import jax
import jax.numpy as jnp
from jax import lax
from jax.experimental import pallas as pl
from jax.experimental.pallas import tpu as pltpu
from jax.sharding import PartitionSpec as P

H = 12
EPS = 1e-05
NEG = -1000000000.0
F32 = jnp.float32
BF16 = jnp.bfloat16
LIMIT = 20 << 20
PLANE = 4


def call(kernel, out_shape, ins, outs, scratch, cost, name):
    spaces = {"v": pltpu.VMEM, "s": pltpu.SMEM, "h": pltpu.HBM, "a": pl.ANY}
    return pl.pallas_call(
        kernel,
        out_shape=out_shape,
        in_specs=[pl.BlockSpec(memory_space=spaces[c]) for c in ins],
        out_specs=[pl.BlockSpec(memory_space=spaces[c]) for c in outs],
        scratch_shapes=scratch,
        compiler_params=pltpu.CompilerParams(vmem_limit_bytes=LIMIT),
        cost_estimate=pl.CostEstimate(flops=cost[0], bytes_accessed=cost[1], transcendentals=cost[2]),
        name=name,
    )


def norm(full, gain):
    middle = jnp.mean(full, axis=-1, keepdims=True)
    spread = jnp.mean((full - middle) ** 2, axis=-1, keepdims=True)
    return (full - middle) * lax.rsqrt(spread + EPS) * gain


def dot(a, b):
    return jnp.dot(a, b, preferred_element_type=F32)


def dot_t(a, b):
    return lax.dot_general(a, b, (((1,), (1,)), ((), ())), preferred_element_type=F32)


def iota(shape, dim):
    return lax.broadcasted_iota(jnp.int32, shape, dim)


def flat(ref):
    return jnp.concatenate([ref[p] for p in range(ref.shape[0])], axis=1)


def to_column(row, size):
    eye = iota((size, size), 0) == iota((size, size), 1)
    return jnp.sum(jnp.where(eye, jnp.broadcast_to(row, (size, size)), 0.0), axis=1, keepdims=True)


def half_masks(width):
    low = (iota((1, width), 1) % 128) < 64
    return jnp.where(low, 1.0, 0.0), jnp.where(low, 0.0, 1.0)


def own_columns(array, core, quarter):
    pieces = []
    for y in range(PLANE // 2):
        left, right = (array[(2 * y + k) * quarter : (2 * y + k + 1) * quarter] for k in range(2))
        pieces.append(jnp.where(core, left, right))
    return jnp.concatenate(pieces, axis=0)


def query_tokens(normed_ref, place_ref, columns):
    quarter = columns // PLANE
    core = place_ref[0] % 2
    pieces = []
    for start in range(0, normed_ref.shape[0], columns // 2):
        pieces.append(normed_ref[pl.ds(pl.multiple_of(start + core * quarter, quarter), quarter), :])
    return jnp.concatenate(pieces, axis=0)


def row_own_kernel(
    columns,
    place_ref,
    x_hbm,
    gain_hbm,
    wq_hbm,
    wk_hbm,
    normed_ref,
    query_ref,
    key_ref,
    wq_ref,
    wk_ref,
    x_ref,
    gain_ref,
    sems,
):
    tokens, width = x_ref.shape
    pairs = [(x_hbm, x_ref), (gain_hbm, gain_ref)]
    for n in range(width // 256):
        for source, target in ((wq_hbm, wq_ref), (wk_hbm, wk_ref)):
            pairs.append((source.at[256 * n : 256 * n + 256], target.at[256 * n : 256 * n + 256]))
    copies = [pltpu.make_async_copy(a, b, sems.at[i]) for i, (a, b) in enumerate(pairs)]
    for copy in copies:
        copy.start()
    for copy in copies[:2]:
        copy.wait()
    normed_ref[...] = norm(x_ref[...].astype(F32), gain_ref[...].reshape(1, width)).astype(BF16)
    for copy in copies[2:]:
        copy.wait()
    query_ref[...] = dot(query_tokens(normed_ref, place_ref, columns), wq_ref[...]).astype(BF16)
    key_ref[...] = dot(normed_ref[...], wk_ref[...]).astype(BF16)


def row_scores_kernel(
    depth_ref,
    place_ref,
    x_ref,
    gain_ref,
    prot_ref,
    wq_ref,
    wk_ref,
    query_ref,
    key_ref,
    *refs,
):
    outs, (normed_ref, same_ref, part_ref) = refs[:-3], refs[-3:]
    columns = prot_ref.shape[0]
    tokens, width = x_ref.shape
    rows, local, quarter = tokens // columns, columns // 2, columns // PLANE
    planes, own = part_ref.shape[:2]
    place = place_ref[0]
    core = (place % 2) == 0
    normed_ref[...] = norm(x_ref[...].astype(F32), gain_ref[...].reshape(1, width)).astype(BF16)
    prot = prot_ref[...].reshape(1, columns).astype(F32)
    depth = jnp.zeros((1, columns), F32)
    for p in range(depth_ref.shape[0]):
        depth = jnp.where(prot == float(p), depth_ref[p].astype(F32), depth)
    prot_col = to_column(prot, columns)
    depth_col = to_column(depth, columns)
    same = jnp.broadcast_to(prot_col, (columns, columns)) == jnp.broadcast_to(prot, (columns, columns))
    same_f = jnp.where(same, 1.0, 0.0)
    same_ref[...] = same_f
    same_l = own_columns(same_f, core, quarter)
    depth_l = own_columns(depth_col, core, quarter)
    low = iota((local, columns), 1) < 64
    first = jnp.where(low, same_l, pltpu.roll(same_l, 64, 1)) > 0.5
    even, odd = half_masks(256)
    other = place + 1 - 2 * (place % 2)
    ids = [place * rows + r for r in range(rows)] + [other * rows + r for r in range(rows)]
    seen_q = [jnp.where(i.astype(F32) < depth_l, 1.0, 0.0) for i in ids]
    seen_k = [jnp.where(i.astype(F32) < depth_col, 1.0, 0.0) for i in ids]
    tokens_q = query_tokens(normed_ref, place_ref, columns)
    for n in range(width // 256):
        cols = slice(256 * n, 256 * n + 256)
        queries = (query_ref[:, cols].astype(F32), dot(tokens_q, wq_ref[:, cols]).astype(BF16).astype(F32))
        keys = (key_ref[:, cols].astype(F32), dot(normed_ref[...], wk_ref[:, cols]))
        query, key = [], []
        for i in range(2 * rows):
            r = i % rows
            query.append(queries[i // rows][r * local : (r + 1) * local] * seen_q[i])
            key.append((keys[i // rows][r * columns : (r + 1) * columns] * seen_k[i]).astype(BF16))
        query_sides = [[(q * side).astype(BF16) for q in query] for side in (even, odd)]
        for q in range(2):
            lanes = slice(128 * q, 128 * q + 128)
            both = [jnp.concatenate([a[:, lanes] for a in side], axis=1) for side in query_sides]
            both = jnp.concatenate(both, axis=0)
            logits = dot_t(both, jnp.concatenate([a[:, lanes] for a in key], axis=1))
            one, two = logits[:local], logits[local:]
            folded = jnp.where(
                low,
                jnp.where(first, one, pltpu.roll(one, 64, 1)),
                jnp.where(first, pltpu.roll(two, 64, 1), two),
            )
            out = slice(256 * n + 128 * q, 256 * n + 128 * q + 128)
            for i in range(planes):
                part_ref[i, :, out] = folded[i * own : (i + 1) * own]
    plane = place // PLANE
    for s, target in enumerate(outs):
        target[...] = part_ref[(plane + s) % planes]


def add_kernel(*refs):
    parts = [ref[...] for ref in refs[:-1]]
    while len(parts) > 1:
        parts = [a + b for a, b in zip(parts[::2], parts[1::2])]
    refs[-1][...] = parts[0]


def row_value_kernel(
    columns, place_ref, x_ref, y_ref, w_ref, mine_ref, other_ref, out_ref, next_ref, spread_ref
):
    core = place_ref[0] % 2
    out_ref[...] = dot(x_ref[...], w_ref[...]).astype(BF16)
    next_ref[...] = dot(y_ref[...], w_ref[...]).astype(BF16)
    rows = x_ref.shape[0] // columns
    quarter = columns // PLANE
    for source, index in ((mine_ref, core), (other_ref, 1 - core)):
        for r in range(rows):
            for y in range(2):
                start = pl.multiple_of(r * columns + y * columns // 2 + quarter * core, quarter)
                piece = source[pl.ds(start, quarter), :].astype(F32)
                target = pl.ds(2 * rows * quarter * y + index * rows + r, quarter, stride=2 * rows)
                for p in range(piece.shape[1] // 128):
                    spread_ref[p, target, :] = piece[:, 128 * p : 128 * p + 128]


def row_softmax_kernel(scale, place_ref, mine_ref, other_ref, same_ref, out_ref, mask_ref):
    own, width = out_ref.shape
    columns = same_ref.shape[0]
    quarter, local = columns // PLANE, columns // 2
    core, plane = place_ref[0] % 2, place_ref[0] // PLANE
    same = same_ref[...]
    mask = jnp.maximum(same, pltpu.roll(same, 64, 1))
    for i in range(columns // own):
        mask_ref[i] = mask[i * own : (i + 1) * own]
    first = plane * own
    live = mask_ref[(first % quarter + quarter * core + local * (first // quarter)) // own] > 0.5
    low = iota((own, 128), 1) < 64
    for p in range(width // 128):
        lanes = slice(128 * p, 128 * p + 128)
        tied = jnp.where(live, (mine_ref[:, lanes] + other_ref[:, lanes]) * scale, NEG)
        top_low = jnp.max(jnp.where(low, tied, 2 * NEG), axis=1, keepdims=True)
        top_high = jnp.max(jnp.where(low, 2 * NEG, tied), axis=1, keepdims=True)
        value = jnp.exp(tied - jnp.where(low, top_low, top_high))
        sum_low = jnp.sum(jnp.where(low, value, 0.0), axis=1, keepdims=True)
        sum_high = jnp.sum(jnp.where(low, 0.0, value), axis=1, keepdims=True)
        out_ref[:, lanes] = (value / jnp.where(low, sum_low, sum_high)).astype(BF16)


def row_output_kernel(
    steps,
    place_ref,
    same_ref,
    value_ref,
    other_ref,
    x_ref,
    w_ref,
    gain_ref,
    *refs,
):
    planes = (len(refs) - 4) // 2
    pieces, after_ref, outs = refs[:planes], refs[planes], refs[planes + 1 : -3]
    mixed_ref, folded_ref, normed_ref = refs[-3:]
    columns = same_ref.shape[0]
    tokens, width = after_ref.shape
    rows = tokens // columns
    quarter, local = columns // PLANE, columns // 2
    place = place_ref[0]
    core, plane = place % 2, place // PLANE
    own = local // planes
    for s, piece in zip(steps, pieces):
        folded_ref[(plane + planes - s) % planes] = piece[...].astype(F32)
    same = [
        same_ref[pl.ds(pl.multiple_of(y * local + core * quarter, quarter), quarter), :] for y in range(2)
    ]
    same = jnp.concatenate(same, axis=0) > 0.5
    low = iota((local, columns), 1) < 64
    even, odd = half_masks(256 * rows)
    even, odd = even.astype(BF16), odd.astype(BF16)
    spots = [core * rows + r for r in range(rows)] + [(1 - core) * rows + r for r in range(rows)]
    for p in range(width // 128):
        lanes = slice(128 * p, 128 * p + 128)
        piece = folded_ref[:, :, lanes].reshape(local, 128)
        turned = pltpu.roll(piece, 64, 1)
        one = jnp.where(same, jnp.where(low, piece, turned), 0.0)
        two = jnp.where(same, jnp.where(low, turned, piece), 0.0)
        weights = jnp.concatenate([one, two], axis=1).astype(BF16)
        value = jnp.concatenate(
            [
                source[r * columns : (r + 1) * columns, lanes]
                for source in (value_ref, other_ref)
                for r in range(rows)
            ],
            axis=1,
        )
        value = jnp.concatenate([value * even, value * odd], axis=0)
        mixed = dot(weights, value)
        for i, spot in enumerate(spots):
            mixed_ref[p, pl.ds(spot, local, stride=2 * rows), :] = mixed[:, 128 * i : 128 * i + 128]
    after = (flat(x_ref) + dot(flat(mixed_ref).astype(BF16), w_ref[...])).astype(BF16)
    after_ref[...] = after
    normed_ref[...] = norm(after.astype(F32), gain_ref[...])
    size = tokens // len(outs)
    for s, out in enumerate(outs):
        start = pl.multiple_of(((plane + s) % len(outs)) * size, size)
        out[...] = normed_ref[pl.ds(start, size), :].astype(BF16)


def pack_kernel(*refs):
    for i, source in enumerate(refs[:-1]):
        refs[-1][i] = source[...]


def block_of(own):
    return 4 if own % 4 == 0 else own


def heads_of(place_ref, wide):
    return pl.ds(pl.multiple_of(place_ref[0] % 2 * wide, 128), wide)


def column_project_kernel(planes, columns, place_ref, wq_ref, wk_ref, wv_ref, *refs):
    ins, (query_ref, key_ref, value_ref, all_ref) = refs[:planes], refs[planes:]
    gather_tokens(ins, columns, all_ref)
    heads = heads_of(place_ref, query_ref.shape[1])
    for w_ref, out in ((wq_ref, query_ref), (wk_ref, key_ref), (wv_ref, value_ref)):
        out[...] = dot(all_ref[...], w_ref[:, heads]).astype(BF16)


def gather_tokens(sources, columns, all_ref):
    planes = len(sources)
    own = columns // 2 // planes
    piece = block_of(own) * sources[0].shape[0] // own
    for g in range(own // block_of(own)):
        for i, source in enumerate(sources):
            start = (g * planes + i) * piece
            all_ref[start : start + piece, :] = source[g * piece : (g + 1) * piece, :]


def column_kernel(
    scale,
    steps,
    columns,
    depth_ref,
    prot_ref,
    place_ref,
    wq_ref,
    wk_ref,
    wv_ref,
    query_ref,
    key_ref,
    value_ref,
    other_ref,
    keep_ref,
    send_ref,
    all_ref,
    mixed_ref,
):
    planes, size, width = other_ref.shape
    wide = width // 2
    slots, local = 2 * planes, columns // 2
    own = local // planes
    rows = size // own
    block = block_of(own)
    piece = block * rows
    chunk = slots * piece
    chunks = own // block
    fold = piece // 8
    pair = 8 // rows
    place = place_ref[0]
    core, line, plane = place % 2, (place // 2) % 2, place // PLANE
    gather_tokens([other_ref.at[i] for i in range(planes)], columns, all_ref)
    heads = heads_of(place_ref, wide)
    full = []
    for mine_ref, w_ref in ((query_ref, wq_ref), (key_ref, wk_ref), (value_ref, wv_ref)):
        other = dot(all_ref[...], w_ref[:, heads]).astype(BF16)
        mine = mine_ref[...]
        parts = []
        for start in range(0, planes * size, chunk // 2):
            parts += [mine[start : start + chunk // 2], other[start : start + chunk // 2]]
        full.append(jnp.concatenate(parts, axis=0))
    query, key, value = full
    query = query.astype(F32) * scale
    even, odd = half_masks(wide)
    sides = [(query * side).astype(BF16) for side in (even, odd)]
    unit = jnp.where(iota((128, 128), 0) == iota((128, 128), 1), 1.0, 0.0).astype(BF16)
    lane = (iota((8, 2 * chunk), 1) % piece) // rows
    level = iota((8, 2 * chunk), 0)
    fits = level // rows == lane % pair
    mine = [jnp.where(lane // pair == v, 1.0, 0.0)[None] for v in range(fold)]
    lives = []
    for g in range(chunks):
        depth = jnp.zeros((8, 2 * chunk), jnp.int32)
        for c in range(block):
            index = plane * own + g * block + c
            column = index % (local // 2) + (local // 2) * line + local * (index // (local // 2))
            depth = jnp.where(lane == c, depth_ref[prot_ref[column]], depth)
        live = []
        for i in range(slots):
            away = ((plane + planes - steps[i % planes]) % planes) * 2 + (core if i < planes else 1 - core)
            live.append((fits & (level % rows + away * rows < depth))[None])
        lives.append(jnp.concatenate([jnp.where(l, 1.0, 0.0) for l in live], axis=0) > 0.5)
    packs, values = [], []
    for q in range(wide // 128):
        lanes = slice(128 * q, 128 * q + 128)
        for g in range(chunks):
            part = slice(g * chunk, g * chunk + chunk)
            both = jnp.concatenate([side[part, lanes] for side in sides], axis=0)
            scores = dot_t(key[part, lanes], both).reshape(slots, fold, 8, 2 * chunk)
            packed = scores[:, 0]
            for v in range(1, fold):
                packed = jnp.where(mine[v] > 0.5, scores[:, v], packed)
            packs.append(jnp.where(lives[g], packed, NEG))
        values.append(dot_t(unit, value[:, lanes]).astype(BF16))
    packs = [jnp.exp(packed - jnp.max(packed, axis=(0, 1), keepdims=True)) for packed in packs]
    packs = [packed * (1.0 / jnp.sum(packed, axis=(0, 1), keepdims=True)) for packed in packs]
    for q, value in enumerate(values):
        for g in range(chunks):
            part = slice(g * chunk, g * chunk + chunk)
            weight = packs[q * chunks + g]
            spread = jnp.stack([weight * m for m in mine], axis=1).reshape(chunk, 2 * chunk).astype(BF16)
            for s in range(2):
                mixed = dot(value[64 * s : 64 * s + 64, part], spread[:, s * chunk : (s + 1) * chunk])
                mixed_ref[128 * q + 64 * s : 128 * q + 64 * s + 64, part] = mixed.astype(BF16)
    turn = jnp.where(iota((chunk, chunk), 0) == iota((chunk, chunk), 1), 1.0, 0.0).astype(BF16)
    for g in range(chunks):
        mixed = dot_t(turn, mixed_ref[:, g * chunk : (g + 1) * chunk])
        for i in range(slots):
            target = keep_ref if i < planes else send_ref
            target[i % planes, g * piece : (g + 1) * piece, :] = mixed[i * piece : (i + 1) * piece].astype(BF16)


def join_kernel(place_ref, keep_ref, other_ref, *outs):
    wide = keep_ref.shape[2]
    core = place_ref[0] % 2

    def write(left, right):
        for s, out in enumerate(outs):
            out[:, :wide] = left[s]
            out[:, wide:] = right[s]

    @pl.when(core == 0)
    def _():
        write(keep_ref, other_ref)

    @pl.when(core == 1)
    def _():
        write(other_ref, keep_ref)


def column_output_kernel(steps, place_ref, w_ref, after_ref, *refs):
    ins, (keep_ref, send_ref, total_ref) = refs[:-3], refs[-3:]
    rows, local, _ = keep_ref.shape
    core, plane = place_ref[0] % 2, place_ref[0] // PLANE
    size = ins[0].shape[0]
    total = dot(jnp.concatenate([source[...] for source in ins], axis=0), w_ref[...])
    for i, s in enumerate(steps):
        start = pl.multiple_of(((plane + s) % len(ins)) * size, size)
        for p in range(total.shape[1] // 128):
            total_ref[p, pl.ds(start, size), :] = total[i * size : (i + 1) * size, 128 * p : 128 * p + 128]
    for p in range(total.shape[1] // 128):
        lanes = slice(128 * p, 128 * p + 128)
        total_ref[p] = total_ref[p] + after_ref[:, lanes].astype(F32)
        for r in range(rows):
            for target, index in ((keep_ref, core), (send_ref, 1 - core)):
                row = total_ref[p, pl.ds(index * rows + r, local, stride=2 * rows), :]
                target[r, :, lanes] = row.astype(BF16)


def assemble_kernel(place_ref, mine_ref, other_ref, out_ref, sems):
    core = place_ref[0] % 2
    local = mine_ref.shape[1]
    quarter = local // 2
    copies = []
    for source, index in ((mine_ref, core), (other_ref, 1 - core)):
        for y in range(2):
            start = pl.multiple_of(y * local + index * quarter, quarter)
            copies.append(
                pltpu.make_async_copy(
                    source.at[:, y * quarter : (y + 1) * quarter, :],
                    out_ref.at[:, pl.ds(start, quarter), :],
                    sems.at[len(copies)],
                )
            )
    for copy in copies:
        copy.start()
    for copy in copies:
        copy.wait()


def hbm(array):
    return pltpu.with_memory_space_constraint(array, pltpu.HBM)


def swap(array, offset):
    devices = lax.axis_size("seq")
    return lax.ppermute(array, "seq", [(i, i ^ offset) for i in range(devices)])


def spin_pairs(step):
    planes = lax.axis_size("seq") // PLANE
    pairs = []
    for z in range(planes):
        for y in range(2):
            for k in range(2):
                pairs.append((z * PLANE + 2 * y + k, (z + step) % planes * PLANE + 2 * k + y))
    return pairs


def far_first(planes):
    return sorted(range(planes), key=lambda s: (-min(s, planes - s), s))


def shift(array, step):
    devices = lax.axis_size("seq")
    if step == 0:
        return array
    return lax.ppermute(array, "seq", [(i, (i + PLANE * step) % devices) for i in range(devices)])


def spin(array, step):
    return lax.ppermute(array, "seq", spin_pairs(step))


def spin_back(array, step):
    return lax.ppermute(array, "seq", [(b, a) for a, b in spin_pairs(step)])


def per_device(
    alignment,
    protein_id,
    row_depth,
    row_gain,
    row_query,
    row_key,
    row_value,
    row_output,
    column_gain,
    column_query,
    column_key,
    column_value,
    column_output,
):
    rows, columns, width = alignment.shape
    devices = lax.axis_size("seq")
    place = lax.axis_index("seq").astype(jnp.int32)[None]
    total_rows = rows * devices
    head_size = width // H
    tokens = rows * columns
    planes, local = devices // PLANE, columns // 2
    size = tokens // planes
    sum_steps = move_steps = back_steps = far_first(planes)
    move_steps = move_steps[2:] + move_steps[:2]
    share_steps = far_first(planes)
    x = alignment.reshape(tokens, width)
    shape = jax.ShapeDtypeStruct
    square = 2 * tokens * width * width

    part = shape((local // planes, width), F32)
    matrix = shape((width, width), BF16)
    sibling = swap(x, 1)
    normed, query, key, row_query, row_key = call(
        functools.partial(row_own_kernel, columns),
        (shape((tokens, width), BF16), shape((tokens // 2, width), BF16), shape((tokens, width), BF16), matrix, matrix),
        "shhhh",
        "vvvvv",
        [
            pltpu.VMEM((tokens, width), BF16),
            pltpu.VMEM((width,), F32),
            pltpu.SemaphoreType.DMA((2 + 2 * (width // 256),)),
        ],
        (3 * square // 2, 4 * width * width, tokens),
        "row_own",
    )(place, hbm(x), hbm(row_gain), hbm(row_query), hbm(row_key))
    *pieces, normed_other, same = call(
        row_scores_kernel,
        (part,) * planes + (shape((tokens, width), BF16), shape((columns, columns), F32)),
        "ss" + "v" * 7,
        "v" * (planes + 2),
        [pltpu.VMEM((planes, local // planes, width), F32)],
        (3 * square // 2, 4 * width * width, tokens),
        "row_scores",
    )(row_depth, place, sibling, row_gain, protein_id, row_query, row_key, query, key)
    column_query, column_key, column_value, late, normed = lax.optimization_barrier(
        (column_query, column_key, column_value, x, normed)
    )
    (total,) = call(
        add_kernel, (part,), "v" * planes, "v", [], (columns * width, 2 * columns * width, 0), "add"
    )(*[shift(pieces[s], s) for s in sum_steps])
    value, value_other, spread = call(
        functools.partial(row_value_kernel, columns),
        (shape((tokens, width), BF16),) * 2 + (shape((width // 128, tokens, 128), F32),),
        "svvvvv",
        "vvv",
        [],
        (2 * square, 2 * width * width, 0),
        "row_value",
    )(place, normed, normed_other, row_value, late, sibling)
    (weights,) = call(
        functools.partial(row_softmax_kernel, 1.0 / (math.sqrt(head_size) * math.sqrt(total_rows))),
        (shape((local // planes, width), BF16),),
        "svvv",
        "v",
        [pltpu.VMEM((columns * planes // local, local // planes, columns), F32)],
        (columns * width, 2 * columns * width, columns * width // 8),
        "row_softmax",
    )(place, total, swap(total, 2), same)
    shared = [shift(weights, s) for s in share_steps]
    after, *blocks = call(
        functools.partial(row_output_kernel, share_steps),
        (shape((tokens, width), BF16),) + (shape((size, width), BF16),) * planes,
        "s" + "v" * (6 + planes),
        "v" * (1 + planes),
        [
            pltpu.VMEM((width // 128, tokens, 128), F32),
            pltpu.VMEM((planes, local // planes, width), F32),
            pltpu.VMEM((tokens, width), F32),
        ],
        (square, 2 * width * width, tokens),
        "row_output",
    )(place, same, value, value_other, spread, row_output, column_gain[None], *shared)
    moved = [spin(blocks[s], s) for s in move_steps]
    wide = width // 2
    (packed,) = call(
        pack_kernel,
        (shape((planes, size, width), BF16),),
        "v" * planes,
        "v",
        [],
        (tokens * width, 4 * tokens * width, 0),
        "pack",
    )(*moved)
    ours = call(
        functools.partial(column_project_kernel, planes, columns),
        (shape((tokens, wide), BF16),) * 3,
        "svvv" + "v" * planes,
        "vvv",
        [pltpu.VMEM((tokens, width), BF16)],
        (3 * square // 2, 3 * width * width, 0),
        "column_project",
    )(place, column_query, column_key, column_value, *moved)
    halves = shape((planes, size, wide), BF16)
    keep, send = call(
        functools.partial(column_kernel, 1.0 / math.sqrt(head_size), move_steps, columns),
        (halves, halves),
        "sss" + "v" * 7,
        "vv",
        [pltpu.VMEM((tokens, width), BF16), pltpu.VMEM((wide, 2 * tokens), BF16)],
        (4 * square, 6 * width * width, H * tokens * tokens // 4),
        "column_attention",
    )(row_depth, protein_id, place, column_query, column_key, column_value, *ours, swap(packed, 1))
    joined = call(
        join_kernel,
        (shape((size, width), BF16),) * planes,
        "svv",
        "v" * planes,
        [],
        (tokens * width, 4 * tokens * width, 0),
        "join",
    )(place, keep, swap(send, 1))
    returned = [spin_back(joined[move_steps.index(s)], s) for s in back_steps]
    half = shape((rows, local, width), BF16)
    keep, send = call(
        functools.partial(column_output_kernel, back_steps),
        (half, half),
        "svv" + "v" * planes,
        "vv",
        [pltpu.VMEM((width // 128, tokens, 128), F32)],
        (square, 2 * width * width, 0),
        "column_output",
    )(place, column_output, after, *returned)
    (out,) = call(
        assemble_kernel,
        (shape((rows, columns, width), BF16),),
        "svv",
        "a",
        [pltpu.SemaphoreType.DMA((4,))],
        (tokens * width, 4 * tokens * width, 0),
        "assemble",
    )(place, keep, swap(send, 1))
    return out


def solution(mesh):
    return jax.shard_map(
        per_device,
        mesh=mesh,
        in_specs=(P(("grp", "seq"), None, None), P("grp"), P("grp")) + (P(),) * 10,
        out_specs=P(("grp", "seq"), None, None),
        check_vma=False,
    )
```

```python
import functools
import math

import jax
import jax.numpy as jnp
from jax import lax
from jax.experimental import pallas as pl
from jax.experimental.pallas import tpu as pltpu
from jax.sharding import PartitionSpec as P

H = 12
EPS = 1e-05
NEG = -1000000000.0
F32 = jnp.float32
BF16 = jnp.bfloat16
LIMIT = 20 << 20
PLANE = 4


def call(kernel, out_shape, ins, outs, scratch, cost, name):
    spaces = {"v": pltpu.VMEM, "s": pltpu.SMEM, "h": pltpu.HBM, "a": pl.ANY}
    return pl.pallas_call(
        kernel,
        out_shape=out_shape,
        in_specs=[pl.BlockSpec(memory_space=spaces[c]) for c in ins],
        out_specs=[pl.BlockSpec(memory_space=spaces[c]) for c in outs],
        scratch_shapes=scratch,
        compiler_params=pltpu.CompilerParams(vmem_limit_bytes=LIMIT),
        cost_estimate=pl.CostEstimate(flops=cost[0], bytes_accessed=cost[1], transcendentals=cost[2]),
        name=name,
    )


def norm(full, gain):
    middle = jnp.mean(full, axis=-1, keepdims=True)
    spread = jnp.mean((full - middle) ** 2, axis=-1, keepdims=True)
    return (full - middle) * lax.rsqrt(spread + EPS) * gain


def dot(a, b):
    return jnp.dot(a, b, preferred_element_type=F32)


def dot_t(a, b):
    return lax.dot_general(a, b, (((1,), (1,)), ((), ())), preferred_element_type=F32)


def iota(shape, dim):
    return lax.broadcasted_iota(jnp.int32, shape, dim)


def flat(ref):
    return jnp.concatenate([ref[p] for p in range(ref.shape[0])], axis=1)


def to_column(row, size):
    eye = iota((size, size), 0) == iota((size, size), 1)
    return jnp.sum(jnp.where(eye, jnp.broadcast_to(row, (size, size)), 0.0), axis=1, keepdims=True)


def half_masks(width):
    low = (iota((1, width), 1) % 128) < 64
    return jnp.where(low, 1.0, 0.0), jnp.where(low, 0.0, 1.0)


def own_columns(array, core, quarter):
    pieces = []
    for y in range(PLANE // 2):
        left, right = (array[(2 * y + k) * quarter : (2 * y + k + 1) * quarter] for k in range(2))
        pieces.append(jnp.where(core, left, right))
    return jnp.concatenate(pieces, axis=0)


def query_tokens(normed_ref, place_ref, columns):
    quarter = columns // PLANE
    core = place_ref[0] % 2
    pieces = []
    for start in range(0, normed_ref.shape[0], columns // 2):
        pieces.append(normed_ref[pl.ds(pl.multiple_of(start + core * quarter, quarter), quarter), :])
    return jnp.concatenate(pieces, axis=0)


def row_own_kernel(
    columns,
    place_ref,
    x_hbm,
    gain_hbm,
    wq_hbm,
    wk_hbm,
    depth_hbm,
    prot_hbm,
    normed_ref,
    query_ref,
    key_ref,
    wq_ref,
    wk_ref,
    same_ref,
    seen_ref,
    x_ref,
    gain_ref,
    depth_ref,
    prot_ref,
    sems,
):
    tokens, width = x_ref.shape
    pairs = [(x_hbm, x_ref), (gain_hbm, gain_ref), (depth_hbm, depth_ref), (prot_hbm, prot_ref)]
    for n in range(width // 256):
        for source, target in ((wq_hbm, wq_ref), (wk_hbm, wk_ref)):
            pairs.append((source.at[256 * n : 256 * n + 256], target.at[256 * n : 256 * n + 256]))
    copies = [pltpu.make_async_copy(a, b, sems.at[i]) for i, (a, b) in enumerate(pairs)]
    for copy in copies:
        copy.start()
    for copy in copies[:2]:
        copy.wait()
    normed_ref[...] = norm(x_ref[...].astype(F32), gain_ref[...].reshape(1, width)).astype(BF16)
    for copy in copies[2:4]:
        copy.wait()
    prot = prot_ref[...].reshape(1, columns).astype(F32)
    depth = jnp.zeros((1, columns), F32)
    for p in range(depth_ref.shape[0]):
        depth = jnp.where(prot == float(p), depth_ref[p].astype(F32), depth)
    square = (columns, columns)
    same = jnp.broadcast_to(to_column(prot, columns), square) == jnp.broadcast_to(prot, square)
    same_ref[...] = jnp.where(same, 1.0, 0.0)
    seen_ref[...] = jnp.broadcast_to(to_column(depth, columns), square)
    for copy in copies[4:]:
        copy.wait()
    query_ref[...] = dot(query_tokens(normed_ref, place_ref, columns), wq_ref[...]).astype(BF16)
    key_ref[...] = dot(normed_ref[...], wk_ref[...]).astype(BF16)


def row_scores_kernel(
    place_ref,
    x_ref,
    gain_ref,
    wq_ref,
    wk_ref,
    query_ref,
    key_ref,
    same_ref,
    seen_ref,
    *refs,
):
    outs, (normed_ref, part_ref) = refs[:-2], refs[-2:]
    columns = same_ref.shape[0]
    tokens, width = x_ref.shape
    rows, local, quarter = tokens // columns, columns // 2, columns // PLANE
    planes, own = part_ref.shape[:2]
    place = place_ref[0]
    core = (place % 2) == 0
    normed_ref[...] = norm(x_ref[...].astype(F32), gain_ref[...].reshape(1, width)).astype(BF16)
    same_l = own_columns(same_ref[...], core, quarter)
    seen = seen_ref[...]
    depth_l = own_columns(seen, core, quarter)
    low = iota((local, columns), 1) < 64
    first = jnp.where(low, same_l, pltpu.roll(same_l, 64, 1)) > 0.5
    even, odd = half_masks(256)
    other = place + 1 - 2 * (place % 2)
    ids = [place * rows + r for r in range(rows)] + [other * rows + r for r in range(rows)]
    seen_q = [jnp.where(i.astype(F32) < depth_l, 1.0, 0.0) for i in ids]
    seen_k = [jnp.where(i.astype(F32) < seen, 1.0, 0.0) for i in ids]
    seen_q, seen_k = ([jnp.concatenate([m, m], axis=1) for m in masks] for masks in (seen_q, seen_k))
    tokens_q = query_tokens(normed_ref, place_ref, columns)
    for n in range(width // 256):
        cols = slice(256 * n, 256 * n + 256)
        queries = (query_ref[:, cols].astype(F32), dot(tokens_q, wq_ref[:, cols]).astype(BF16).astype(F32))
        keys = (key_ref[:, cols].astype(F32), dot(normed_ref[...], wk_ref[:, cols]))
        query, key = [], []
        for i in range(2 * rows):
            r = i % rows
            query.append(queries[i // rows][r * local : (r + 1) * local] * seen_q[i])
            key.append((keys[i // rows][r * columns : (r + 1) * columns] * seen_k[i]).astype(BF16))
        query_sides = [[(q * side).astype(BF16) for q in query] for side in (even, odd)]
        for q in range(2):
            lanes = slice(128 * q, 128 * q + 128)
            both = [jnp.concatenate([a[:, lanes] for a in side], axis=1) for side in query_sides]
            both = jnp.concatenate(both, axis=0)
            logits = dot_t(both, jnp.concatenate([a[:, lanes] for a in key], axis=1))
            one, two = logits[:local], logits[local:]
            folded = jnp.where(
                low,
                jnp.where(first, one, pltpu.roll(one, 64, 1)),
                jnp.where(first, pltpu.roll(two, 64, 1), two),
            )
            out = slice(256 * n + 128 * q, 256 * n + 128 * q + 128)
            for i in range(planes):
                part_ref[i, :, out] = folded[i * own : (i + 1) * own]
    plane = place // PLANE
    for s, target in enumerate(outs):
        target[...] = part_ref[(plane + s) % planes]


def add_kernel(*refs):
    parts = [ref[...] for ref in refs[:-1]]
    while len(parts) > 1:
        parts = [a + b for a, b in zip(parts[::2], parts[1::2])]
    refs[-1][...] = parts[0]


def row_value_kernel(
    columns, place_ref, x_ref, y_ref, w_ref, mine_ref, other_ref, out_ref, next_ref, spread_ref
):
    core = place_ref[0] % 2
    out_ref[...] = dot(x_ref[...], w_ref[...]).astype(BF16)
    next_ref[...] = dot(y_ref[...], w_ref[...]).astype(BF16)
    rows = x_ref.shape[0] // columns
    quarter = columns // PLANE
    for source, index in ((mine_ref, core), (other_ref, 1 - core)):
        for r in range(rows):
            for y in range(2):
                start = pl.multiple_of(r * columns + y * columns // 2 + quarter * core, quarter)
                piece = source[pl.ds(start, quarter), :].astype(F32)
                target = pl.ds(2 * rows * quarter * y + index * rows + r, quarter, stride=2 * rows)
                for p in range(piece.shape[1] // 128):
                    spread_ref[p, target, :] = piece[:, 128 * p : 128 * p + 128]


def row_softmax_kernel(scale, place_ref, mine_ref, other_ref, same_ref, out_ref, mask_ref):
    own, width = out_ref.shape
    columns = same_ref.shape[0]
    quarter, local = columns // PLANE, columns // 2
    core, plane = place_ref[0] % 2, place_ref[0] // PLANE
    same = same_ref[...]
    mask = jnp.maximum(same, pltpu.roll(same, 64, 1))
    for i in range(columns // own):
        mask_ref[i] = mask[i * own : (i + 1) * own]
    first = plane * own
    live = mask_ref[(first % quarter + quarter * core + local * (first // quarter)) // own] > 0.5
    low = iota((own, 128), 1) < 64
    for p in range(width // 128):
        lanes = slice(128 * p, 128 * p + 128)
        tied = jnp.where(live, (mine_ref[:, lanes] + other_ref[:, lanes]) * scale, NEG)
        top_low = jnp.max(jnp.where(low, tied, 2 * NEG), axis=1, keepdims=True)
        top_high = jnp.max(jnp.where(low, 2 * NEG, tied), axis=1, keepdims=True)
        value = jnp.exp(tied - jnp.where(low, top_low, top_high))
        sum_low = jnp.sum(jnp.where(low, value, 0.0), axis=1, keepdims=True)
        sum_high = jnp.sum(jnp.where(low, 0.0, value), axis=1, keepdims=True)
        out_ref[:, lanes] = (value / jnp.where(low, sum_low, sum_high)).astype(BF16)


def row_output_kernel(
    steps,
    place_ref,
    same_ref,
    value_ref,
    other_ref,
    x_ref,
    w_ref,
    gain_ref,
    *refs,
):
    planes = (len(refs) - 4) // 2
    pieces, after_ref, outs = refs[:planes], refs[planes], refs[planes + 1 : -3]
    mixed_ref, folded_ref, normed_ref = refs[-3:]
    columns = same_ref.shape[0]
    tokens, width = after_ref.shape
    rows = tokens // columns
    quarter, local = columns // PLANE, columns // 2
    place = place_ref[0]
    core, plane = place % 2, place // PLANE
    own = local // planes
    for s, piece in zip(steps, pieces):
        folded_ref[(plane + planes - s) % planes] = piece[...].astype(F32)
    same = [
        same_ref[pl.ds(pl.multiple_of(y * local + core * quarter, quarter), quarter), :] for y in range(2)
    ]
    same = jnp.concatenate(same, axis=0) > 0.5
    low = iota((local, columns), 1) < 64
    even, odd = half_masks(256 * rows)
    even, odd = even.astype(BF16), odd.astype(BF16)
    spots = [core * rows + r for r in range(rows)] + [(1 - core) * rows + r for r in range(rows)]
    for p in range(width // 128):
        lanes = slice(128 * p, 128 * p + 128)
        piece = folded_ref[:, :, lanes].reshape(local, 128)
        turned = pltpu.roll(piece, 64, 1)
        one = jnp.where(same, jnp.where(low, piece, turned), 0.0)
        two = jnp.where(same, jnp.where(low, turned, piece), 0.0)
        weights = jnp.concatenate([one, two], axis=1).astype(BF16)
        value = jnp.concatenate(
            [
                source[r * columns : (r + 1) * columns, lanes]
                for source in (value_ref, other_ref)
                for r in range(rows)
            ],
            axis=1,
        )
        value = jnp.concatenate([value * even, value * odd], axis=0)
        mixed = dot(weights, value)
        for i, spot in enumerate(spots):
            mixed_ref[p, pl.ds(spot, local, stride=2 * rows), :] = mixed[:, 128 * i : 128 * i + 128]
    after = (flat(x_ref) + dot(flat(mixed_ref).astype(BF16), w_ref[...])).astype(BF16)
    after_ref[...] = after
    normed_ref[...] = norm(after.astype(F32), gain_ref[...])
    size = tokens // len(outs)
    for s, out in enumerate(outs):
        start = pl.multiple_of(((plane + s) % len(outs)) * size, size)
        out[...] = normed_ref[pl.ds(start, size), :].astype(BF16)


def pack_kernel(*refs):
    for i, source in enumerate(refs[:-1]):
        refs[-1][i] = source[...]


def block_of(own):
    return 4 if own % 4 == 0 else own


def heads_of(place_ref, wide):
    return pl.ds(pl.multiple_of(place_ref[0] % 2 * wide, 128), wide)


def column_project_kernel(planes, columns, place_ref, wq_ref, wk_ref, wv_ref, *refs):
    ins, (query_ref, key_ref, value_ref, all_ref) = refs[:planes], refs[planes:]
    gather_tokens(ins, columns, all_ref)
    heads = heads_of(place_ref, query_ref.shape[1])
    for w_ref, out in ((wq_ref, query_ref), (wk_ref, key_ref), (wv_ref, value_ref)):
        out[...] = dot(all_ref[...], w_ref[:, heads]).astype(BF16)


def gather_tokens(sources, columns, all_ref):
    planes = len(sources)
    own = columns // 2 // planes
    piece = block_of(own) * sources[0].shape[0] // own
    for g in range(own // block_of(own)):
        for i, source in enumerate(sources):
            start = (g * planes + i) * piece
            all_ref[start : start + piece, :] = source[g * piece : (g + 1) * piece, :]


def column_kernel(
    scale,
    steps,
    columns,
    depth_ref,
    prot_ref,
    place_ref,
    wq_ref,
    wk_ref,
    wv_ref,
    query_ref,
    key_ref,
    value_ref,
    other_ref,
    keep_ref,
    send_ref,
    all_ref,
    mixed_ref,
):
    planes, size, width = other_ref.shape
    wide = width // 2
    slots, local = 2 * planes, columns // 2
    own = local // planes
    rows = size // own
    block = block_of(own)
    piece = block * rows
    chunk = slots * piece
    chunks = own // block
    fold = piece // 8
    pair = 8 // rows
    place = place_ref[0]
    core, line, plane = place % 2, (place // 2) % 2, place // PLANE
    gather_tokens([other_ref.at[i] for i in range(planes)], columns, all_ref)
    heads = heads_of(place_ref, wide)
    full = []
    for mine_ref, w_ref in ((query_ref, wq_ref), (key_ref, wk_ref), (value_ref, wv_ref)):
        other = dot(all_ref[...], w_ref[:, heads]).astype(BF16)
        mine = mine_ref[...]
        parts = []
        for start in range(0, planes * size, chunk // 2):
            parts += [mine[start : start + chunk // 2], other[start : start + chunk // 2]]
        full.append(jnp.concatenate(parts, axis=0))
    query, key, value = full
    query = query.astype(F32) * scale
    even, odd = half_masks(wide)
    sides = [(query * side).astype(BF16) for side in (even, odd)]
    unit = jnp.where(iota((128, 128), 0) == iota((128, 128), 1), 1.0, 0.0).astype(BF16)
    lane = (iota((8, 2 * chunk), 1) % piece) // rows
    level = iota((8, 2 * chunk), 0)
    fits = level // rows == lane % pair
    mine = [jnp.where(lane // pair == v, 1.0, 0.0)[None] for v in range(fold)]
    lives = []
    for g in range(chunks):
        depth = jnp.zeros((8, 2 * chunk), jnp.int32)
        for c in range(block):
            index = plane * own + g * block + c
            column = index % (local // 2) + (local // 2) * line + local * (index // (local // 2))
            depth = jnp.where(lane == c, depth_ref[prot_ref[column]], depth)
        live = []
        for i in range(slots):
            away = ((plane + planes - steps[i % planes]) % planes) * 2 + (core if i < planes else 1 - core)
            live.append((fits & (level % rows + away * rows < depth))[None])
        lives.append(jnp.concatenate([jnp.where(l, 1.0, 0.0) for l in live], axis=0) > 0.5)
    packs, values = [], []
    for q in range(wide // 128):
        lanes = slice(128 * q, 128 * q + 128)
        for g in range(chunks):
            part = slice(g * chunk, g * chunk + chunk)
            both = jnp.concatenate([side[part, lanes] for side in sides], axis=0)
            scores = dot_t(key[part, lanes], both).reshape(slots, fold, 8, 2 * chunk)
            packed = scores[:, 0]
            for v in range(1, fold):
                packed = jnp.where(mine[v] > 0.5, scores[:, v], packed)
            packs.append(jnp.where(lives[g], packed, NEG))
        values.append(dot_t(unit, value[:, lanes]).astype(BF16))
    packs = [jnp.exp(packed - jnp.max(packed, axis=(0, 1), keepdims=True)) for packed in packs]
    packs = [packed * (1.0 / jnp.sum(packed, axis=(0, 1), keepdims=True)) for packed in packs]
    for q, value in enumerate(values):
        for g in range(chunks):
            part = slice(g * chunk, g * chunk + chunk)
            weight = packs[q * chunks + g]
            spread = jnp.stack([weight * m for m in mine], axis=1).reshape(chunk, 2 * chunk).astype(BF16)
            for s in range(2):
                mixed = dot(value[64 * s : 64 * s + 64, part], spread[:, s * chunk : (s + 1) * chunk])
                mixed_ref[128 * q + 64 * s : 128 * q + 64 * s + 64, part] = mixed.astype(BF16)
    turn = jnp.where(iota((chunk, chunk), 0) == iota((chunk, chunk), 1), 1.0, 0.0).astype(BF16)
    for g in range(chunks):
        mixed = dot_t(turn, mixed_ref[:, g * chunk : (g + 1) * chunk])
        for i in range(slots):
            target = keep_ref if i < planes else send_ref
            target[i % planes, g * piece : (g + 1) * piece, :] = mixed[i * piece : (i + 1) * piece].astype(BF16)


def join_kernel(place_ref, keep_ref, other_ref, *outs):
    wide = keep_ref.shape[2]
    core = place_ref[0] % 2

    def write(left, right):
        for s, out in enumerate(outs):
            out[:, :wide] = left[s]
            out[:, wide:] = right[s]

    @pl.when(core == 0)
    def _():
        write(keep_ref, other_ref)

    @pl.when(core == 1)
    def _():
        write(other_ref, keep_ref)


def column_output_kernel(steps, place_ref, w_ref, after_ref, *refs):
    ins, (keep_ref, send_ref, total_ref) = refs[:-3], refs[-3:]
    rows, local, _ = keep_ref.shape
    core, plane = place_ref[0] % 2, place_ref[0] // PLANE
    size = ins[0].shape[0]
    total = dot(jnp.concatenate([source[...] for source in ins], axis=0), w_ref[...])
    for i, s in enumerate(steps):
        start = pl.multiple_of(((plane + s) % len(ins)) * size, size)
        for p in range(total.shape[1] // 128):
            total_ref[p, pl.ds(start, size), :] = total[i * size : (i + 1) * size, 128 * p : 128 * p + 128]
    for p in range(total.shape[1] // 128):
        lanes = slice(128 * p, 128 * p + 128)
        total_ref[p] = total_ref[p] + after_ref[:, lanes].astype(F32)
        for r in range(rows):
            for target, index in ((keep_ref, core), (send_ref, 1 - core)):
                row = total_ref[p, pl.ds(index * rows + r, local, stride=2 * rows), :]
                target[r, :, lanes] = row.astype(BF16)


def assemble_kernel(place_ref, mine_ref, other_ref, out_ref, sems):
    core = place_ref[0] % 2
    local = mine_ref.shape[1]
    quarter = local // 2
    copies = []
    for source, index in ((mine_ref, core), (other_ref, 1 - core)):
        for y in range(2):
            start = pl.multiple_of(y * local + index * quarter, quarter)
            copies.append(
                pltpu.make_async_copy(
                    source.at[:, y * quarter : (y + 1) * quarter, :],
                    out_ref.at[:, pl.ds(start, quarter), :],
                    sems.at[len(copies)],
                )
            )
    for copy in copies:
        copy.start()
    for copy in copies:
        copy.wait()


def hbm(array):
    return pltpu.with_memory_space_constraint(array, pltpu.HBM)


def swap(array, offset):
    devices = lax.axis_size("seq")
    return lax.ppermute(array, "seq", [(i, i ^ offset) for i in range(devices)])


def spin_pairs(step):
    planes = lax.axis_size("seq") // PLANE
    pairs = []
    for z in range(planes):
        for y in range(2):
            for k in range(2):
                pairs.append((z * PLANE + 2 * y + k, (z + step) % planes * PLANE + 2 * k + y))
    return pairs


def far_first(planes):
    return sorted(range(planes), key=lambda s: (-min(s, planes - s), s))


def shift(array, step):
    devices = lax.axis_size("seq")
    if step == 0:
        return array
    return lax.ppermute(array, "seq", [(i, (i + PLANE * step) % devices) for i in range(devices)])


def spin(array, step):
    return lax.ppermute(array, "seq", spin_pairs(step))


def spin_back(array, step):
    return lax.ppermute(array, "seq", [(b, a) for a, b in spin_pairs(step)])


def per_device(
    alignment,
    protein_id,
    row_depth,
    row_gain,
    row_query,
    row_key,
    row_value,
    row_output,
    column_gain,
    column_query,
    column_key,
    column_value,
    column_output,
):
    rows, columns, width = alignment.shape
    devices = lax.axis_size("seq")
    place = lax.axis_index("seq").astype(jnp.int32)[None]
    total_rows = rows * devices
    head_size = width // H
    tokens = rows * columns
    planes, local = devices // PLANE, columns // 2
    size = tokens // planes
    sum_steps = back_steps = share_steps = far_first(planes)
    move_steps = [s for s in (1, 0) if s < planes] + [s for s in back_steps if s > 1]
    x = alignment.reshape(tokens, width)
    shape = jax.ShapeDtypeStruct
    square = 2 * tokens * width * width

    part = shape((local // planes, width), F32)
    matrix = shape((width, width), BF16)
    sibling = swap(x, 1)
    normed, query, key, row_query, row_key, same, seen = call(
        functools.partial(row_own_kernel, columns),
        (shape((tokens, width), BF16), shape((tokens // 2, width), BF16), shape((tokens, width), BF16), matrix, matrix)
        + (shape((columns, columns), F32),) * 2,
        "shhhhhh",
        "v" * 7,
        [
            pltpu.VMEM((tokens, width), BF16),
            pltpu.VMEM((width,), F32),
            pltpu.SMEM(row_depth.shape, jnp.int32),
            pltpu.VMEM((columns,), jnp.int32),
            pltpu.SemaphoreType.DMA((4 + 2 * (width // 256),)),
        ],
        (3 * square // 2, 4 * width * width, tokens),
        "row_own",
    )(place, hbm(x), hbm(row_gain), hbm(row_query), hbm(row_key), hbm(row_depth), hbm(protein_id))
    *pieces, normed_other = call(
        row_scores_kernel,
        (part,) * planes + (shape((tokens, width), BF16),),
        "s" + "v" * 8,
        "v" * (planes + 1),
        [pltpu.VMEM((planes, local // planes, width), F32)],
        (3 * square // 2, 4 * width * width, tokens),
        "row_scores",
    )(place, sibling, row_gain, row_query, row_key, query, key, same, seen)
    column_query, column_key, column_value, late, normed = lax.optimization_barrier(
        (column_query, column_key, column_value, x, normed)
    )
    (total,) = call(
        add_kernel, (part,), "v" * planes, "v", [], (columns * width, 2 * columns * width, 0), "add"
    )(*[shift(pieces[s], s) for s in sum_steps])
    value, value_other, spread = call(
        functools.partial(row_value_kernel, columns),
        (shape((tokens, width), BF16),) * 2 + (shape((width // 128, tokens, 128), F32),),
        "svvvvv",
        "vvv",
        [],
        (2 * square, 2 * width * width, 0),
        "row_value",
    )(place, normed, normed_other, row_value, late, sibling)
    (weights,) = call(
        functools.partial(row_softmax_kernel, 1.0 / (math.sqrt(head_size) * math.sqrt(total_rows))),
        (shape((local // planes, width), BF16),),
        "svvv",
        "v",
        [pltpu.VMEM((columns * planes // local, local // planes, columns), F32)],
        (columns * width, 2 * columns * width, columns * width // 8),
        "row_softmax",
    )(place, total, swap(total, 2), same)
    shared = [shift(weights, s) for s in share_steps]
    after, *blocks = call(
        functools.partial(row_output_kernel, share_steps),
        (shape((tokens, width), BF16),) + (shape((size, width), BF16),) * planes,
        "s" + "v" * (6 + planes),
        "v" * (1 + planes),
        [
            pltpu.VMEM((width // 128, tokens, 128), F32),
            pltpu.VMEM((planes, local // planes, width), F32),
            pltpu.VMEM((tokens, width), F32),
        ],
        (square, 2 * width * width, tokens),
        "row_output",
    )(place, same, value, value_other, spread, row_output, column_gain[None], *shared)
    moved = [spin(blocks[s], s) for s in move_steps]
    wide = width // 2
    (packed,) = call(
        pack_kernel,
        (shape((planes, size, width), BF16),),
        "v" * planes,
        "v",
        [],
        (tokens * width, 4 * tokens * width, 0),
        "pack",
    )(*moved)
    ours = call(
        functools.partial(column_project_kernel, planes, columns),
        (shape((tokens, wide), BF16),) * 3,
        "svvv" + "v" * planes,
        "vvv",
        [pltpu.VMEM((tokens, width), BF16)],
        (3 * square // 2, 3 * width * width, 0),
        "column_project",
    )(place, column_query, column_key, column_value, *moved)
    halves = shape((planes, size, wide), BF16)
    keep, send = call(
        functools.partial(column_kernel, 1.0 / math.sqrt(head_size), move_steps, columns),
        (halves, halves),
        "sss" + "v" * 7,
        "vv",
        [pltpu.VMEM((tokens, width), BF16), pltpu.VMEM((wide, 2 * tokens), BF16)],
        (4 * square, 6 * width * width, H * tokens * tokens // 4),
        "column_attention",
    )(row_depth, protein_id, place, column_query, column_key, column_value, *ours, swap(packed, 1))
    joined = call(
        join_kernel,
        (shape((size, width), BF16),) * planes,
        "svv",
        "v" * planes,
        [],
        (tokens * width, 4 * tokens * width, 0),
        "join",
    )(place, keep, swap(send, 1))
    returned = [spin_back(joined[move_steps.index(s)], s) for s in back_steps]
    half = shape((rows, local, width), BF16)
    keep, send = call(
        functools.partial(column_output_kernel, back_steps),
        (half, half),
        "svv" + "v" * planes,
        "vv",
        [pltpu.VMEM((width // 128, tokens, 128), F32)],
        (square, 2 * width * width, 0),
        "column_output",
    )(place, column_output, after, *returned)
    (out,) = call(
        assemble_kernel,
        (shape((rows, columns, width), BF16),),
        "svv",
        "a",
        [pltpu.SemaphoreType.DMA((4,))],
        (tokens * width, 4 * tokens * width, 0),
        "assemble",
    )(place, keep, swap(send, 1))
    return out


def solution(mesh):
    return jax.shard_map(
        per_device,
        mesh=mesh,
        in_specs=(P(("grp", "seq"), None, None), P("grp"), P("grp")) + (P(),) * 10,
        out_specs=P(("grp", "seq"), None, None),
        check_vma=False,
    )
```

```python
import functools
import math

import jax
import jax.numpy as jnp
from jax import lax
from jax.experimental import pallas as pl
from jax.experimental.pallas import tpu as pltpu
from jax.sharding import PartitionSpec as P

H = 12
EPS = 1e-05
NEG = -1000000000.0
F32 = jnp.float32
BF16 = jnp.bfloat16
LIMIT = 20 << 20
PLANE = 4


def call(kernel, out_shape, ins, outs, scratch, cost, name):
    spaces = {"v": pltpu.VMEM, "s": pltpu.SMEM, "h": pltpu.HBM, "a": pl.ANY}
    return pl.pallas_call(
        kernel,
        out_shape=out_shape,
        in_specs=[pl.BlockSpec(memory_space=spaces[c]) for c in ins],
        out_specs=[pl.BlockSpec(memory_space=spaces[c]) for c in outs],
        scratch_shapes=scratch,
        compiler_params=pltpu.CompilerParams(vmem_limit_bytes=LIMIT),
        cost_estimate=pl.CostEstimate(flops=cost[0], bytes_accessed=cost[1], transcendentals=cost[2]),
        name=name,
    )


def norm(full, gain):
    middle = jnp.mean(full, axis=-1, keepdims=True)
    spread = jnp.mean((full - middle) ** 2, axis=-1, keepdims=True)
    return (full - middle) * lax.rsqrt(spread + EPS) * gain


def dot(a, b):
    return jnp.dot(a, b, preferred_element_type=F32)


def dot_t(a, b):
    return lax.dot_general(a, b, (((1,), (1,)), ((), ())), preferred_element_type=F32)


def iota(shape, dim):
    return lax.broadcasted_iota(jnp.int32, shape, dim)


def flat(ref):
    return jnp.concatenate([ref[p] for p in range(ref.shape[0])], axis=1)


def to_column(row, size):
    eye = iota((size, size), 0) == iota((size, size), 1)
    return jnp.sum(jnp.where(eye, jnp.broadcast_to(row, (size, size)), 0.0), axis=1, keepdims=True)


def half_masks(width):
    low = (iota((1, width), 1) % 128) < 64
    return jnp.where(low, 1.0, 0.0), jnp.where(low, 0.0, 1.0)


def own_columns(array, core, quarter):
    pieces = []
    for y in range(PLANE // 2):
        left, right = (array[(2 * y + k) * quarter : (2 * y + k + 1) * quarter] for k in range(2))
        pieces.append(jnp.where(core, left, right))
    return jnp.concatenate(pieces, axis=0)


def query_tokens(normed_ref, place_ref, columns):
    quarter = columns // PLANE
    core = place_ref[0] % 2
    pieces = []
    for start in range(0, normed_ref.shape[0], columns // 2):
        pieces.append(normed_ref[pl.ds(pl.multiple_of(start + core * quarter, quarter), quarter), :])
    return jnp.concatenate(pieces, axis=0)


def row_own_kernel(
    columns,
    place_ref,
    x_hbm,
    gain_hbm,
    wq_hbm,
    wk_hbm,
    depth_hbm,
    prot_hbm,
    normed_ref,
    query_ref,
    key_ref,
    wq_ref,
    wk_ref,
    same_ref,
    seen_ref,
    x_ref,
    gain_ref,
    depth_ref,
    prot_ref,
    sems,
):
    tokens, width = x_ref.shape
    pairs = [(x_hbm, x_ref), (gain_hbm, gain_ref), (depth_hbm, depth_ref), (prot_hbm, prot_ref)]
    for n in range(width // 256):
        for source, target in ((wq_hbm, wq_ref), (wk_hbm, wk_ref)):
            pairs.append((source.at[256 * n : 256 * n + 256], target.at[256 * n : 256 * n + 256]))
    copies = [pltpu.make_async_copy(a, b, sems.at[i]) for i, (a, b) in enumerate(pairs)]
    for copy in copies:
        copy.start()
    for copy in copies[:2]:
        copy.wait()
    normed_ref[...] = norm(x_ref[...].astype(F32), gain_ref[...].reshape(1, width)).astype(BF16)
    for copy in copies[2:4]:
        copy.wait()
    prot = prot_ref[...].reshape(1, columns).astype(F32)
    depth = jnp.zeros((1, columns), F32)
    for p in range(depth_ref.shape[0]):
        depth = jnp.where(prot == float(p), depth_ref[p].astype(F32), depth)
    square = (columns, columns)
    same = jnp.broadcast_to(to_column(prot, columns), square) == jnp.broadcast_to(prot, square)
    same_ref[...] = jnp.where(same, 1.0, 0.0)
    seen_ref[...] = jnp.broadcast_to(to_column(depth, columns), square)
    for copy in copies[4:]:
        copy.wait()
    query_ref[...] = dot(query_tokens(normed_ref, place_ref, columns), wq_ref[...]).astype(BF16)
    key_ref[...] = dot(normed_ref[...], wk_ref[...]).astype(BF16)


def row_scores_kernel(
    place_ref,
    x_ref,
    gain_ref,
    wq_ref,
    wk_ref,
    query_ref,
    key_ref,
    same_ref,
    seen_ref,
    *refs,
):
    outs, (normed_ref, part_ref) = refs[:-2], refs[-2:]
    columns = same_ref.shape[0]
    tokens, width = x_ref.shape
    rows, local, quarter = tokens // columns, columns // 2, columns // PLANE
    planes, own = part_ref.shape[:2]
    place = place_ref[0]
    core = (place % 2) == 0
    normed_ref[...] = norm(x_ref[...].astype(F32), gain_ref[...].reshape(1, width)).astype(BF16)
    same_l = own_columns(same_ref[...], core, quarter)
    seen = seen_ref[...]
    depth_l = own_columns(seen, core, quarter)
    low = iota((local, columns), 1) < 64
    first = jnp.where(low, same_l, pltpu.roll(same_l, 64, 1)) > 0.5
    even, odd = half_masks(256)
    other = place + 1 - 2 * (place % 2)
    ids = [place * rows + r for r in range(rows)] + [other * rows + r for r in range(rows)]
    seen_q = [jnp.where(i.astype(F32) < depth_l, 1.0, 0.0) for i in ids]
    seen_k = [jnp.where(i.astype(F32) < seen, 1.0, 0.0) for i in ids]
    seen_q, seen_k = ([jnp.concatenate([m, m], axis=1) for m in masks] for masks in (seen_q, seen_k))
    tokens_q = query_tokens(normed_ref, place_ref, columns)
    for n in range(width // 256):
        cols = slice(256 * n, 256 * n + 256)
        queries = (query_ref[:, cols].astype(F32), dot(tokens_q, wq_ref[:, cols]).astype(BF16).astype(F32))
        keys = (key_ref[:, cols].astype(F32), dot(normed_ref[...], wk_ref[:, cols]))
        query, key = [], []
        for i in range(2 * rows):
            r = i % rows
            query.append(queries[i // rows][r * local : (r + 1) * local] * seen_q[i])
            key.append((keys[i // rows][r * columns : (r + 1) * columns] * seen_k[i]).astype(BF16))
        query_sides = [[(q * side).astype(BF16) for q in query] for side in (even, odd)]
        for q in range(2):
            lanes = slice(128 * q, 128 * q + 128)
            both = [jnp.concatenate([a[:, lanes] for a in side], axis=1) for side in query_sides]
            both = jnp.concatenate(both, axis=0)
            logits = dot_t(both, jnp.concatenate([a[:, lanes] for a in key], axis=1))
            one, two = logits[:local], logits[local:]
            folded = jnp.where(
                low,
                jnp.where(first, one, pltpu.roll(one, 64, 1)),
                jnp.where(first, pltpu.roll(two, 64, 1), two),
            )
            out = slice(256 * n + 128 * q, 256 * n + 128 * q + 128)
            for i in range(planes):
                part_ref[i, :, out] = folded[i * own : (i + 1) * own]
    plane = place // PLANE
    for s, target in enumerate(outs):
        target[...] = part_ref[(plane + s) % planes]


def add_kernel(*refs):
    parts = [ref[...] for ref in refs[:-1]]
    while len(parts) > 1:
        parts = [a + b for a, b in zip(parts[::2], parts[1::2])]
    refs[-1][...] = parts[0]


def row_value_kernel(
    columns, place_ref, x_ref, y_ref, w_ref, mine_ref, other_ref, out_ref, next_ref, spread_ref
):
    core = place_ref[0] % 2
    out_ref[...] = dot(x_ref[...], w_ref[...]).astype(BF16)
    next_ref[...] = dot(y_ref[...], w_ref[...]).astype(BF16)
    rows = x_ref.shape[0] // columns
    quarter = columns // PLANE
    for source, index in ((mine_ref, core), (other_ref, 1 - core)):
        for r in range(rows):
            for y in range(2):
                start = pl.multiple_of(r * columns + y * columns // 2 + quarter * core, quarter)
                piece = source[pl.ds(start, quarter), :].astype(F32)
                target = pl.ds(2 * rows * quarter * y + index * rows + r, quarter, stride=2 * rows)
                for p in range(piece.shape[1] // 128):
                    spread_ref[p, target, :] = piece[:, 128 * p : 128 * p + 128]


def row_softmax_kernel(scale, place_ref, mine_ref, other_ref, same_ref, out_ref, mask_ref):
    own, width = out_ref.shape
    columns = same_ref.shape[0]
    quarter, local = columns // PLANE, columns // 2
    core, plane = place_ref[0] % 2, place_ref[0] // PLANE
    same = same_ref[...]
    mask = jnp.maximum(same, pltpu.roll(same, 64, 1))
    for i in range(columns // own):
        mask_ref[i] = mask[i * own : (i + 1) * own]
    first = plane * own
    live = mask_ref[(first % quarter + quarter * core + local * (first // quarter)) // own] > 0.5
    low = iota((own, 128), 1) < 64
    for p in range(width // 128):
        lanes = slice(128 * p, 128 * p + 128)
        tied = jnp.where(live, (mine_ref[:, lanes] + other_ref[:, lanes]) * scale, NEG)
        top_low = jnp.max(jnp.where(low, tied, 2 * NEG), axis=1, keepdims=True)
        top_high = jnp.max(jnp.where(low, 2 * NEG, tied), axis=1, keepdims=True)
        value = jnp.exp(tied - jnp.where(low, top_low, top_high))
        sum_low = jnp.sum(jnp.where(low, value, 0.0), axis=1, keepdims=True)
        sum_high = jnp.sum(jnp.where(low, 0.0, value), axis=1, keepdims=True)
        out_ref[:, lanes] = (value / jnp.where(low, sum_low, sum_high)).astype(BF16)


def row_output_kernel(
    steps,
    place_ref,
    same_ref,
    value_ref,
    other_ref,
    x_ref,
    w_ref,
    gain_ref,
    *refs,
):
    planes = (len(refs) - 4) // 2
    pieces, after_ref, outs = refs[:planes], refs[planes], refs[planes + 1 : -3]
    mixed_ref, folded_ref, normed_ref = refs[-3:]
    columns = same_ref.shape[0]
    tokens, width = after_ref.shape
    rows = tokens // columns
    quarter, local = columns // PLANE, columns // 2
    place = place_ref[0]
    core, plane = place % 2, place // PLANE
    own = local // planes
    for s, piece in zip(steps, pieces):
        folded_ref[(plane + planes - s) % planes] = piece[...].astype(F32)
    same = [
        same_ref[pl.ds(pl.multiple_of(y * local + core * quarter, quarter), quarter), :] for y in range(2)
    ]
    same = jnp.concatenate(same, axis=0) > 0.5
    low = iota((local, columns), 1) < 64
    even, odd = half_masks(256 * rows)
    even, odd = even.astype(BF16), odd.astype(BF16)
    spots = [core * rows + r for r in range(rows)] + [(1 - core) * rows + r for r in range(rows)]
    for p in range(width // 128):
        lanes = slice(128 * p, 128 * p + 128)
        piece = folded_ref[:, :, lanes].reshape(local, 128)
        turned = pltpu.roll(piece, 64, 1)
        one = jnp.where(same, jnp.where(low, piece, turned), 0.0)
        two = jnp.where(same, jnp.where(low, turned, piece), 0.0)
        weights = jnp.concatenate([one, two], axis=1).astype(BF16)
        value = jnp.concatenate(
            [
                source[r * columns : (r + 1) * columns, lanes]
                for source in (value_ref, other_ref)
                for r in range(rows)
            ],
            axis=1,
        )
        value = jnp.concatenate([value * even, value * odd], axis=0)
        mixed = dot(weights, value)
        for i, spot in enumerate(spots):
            mixed_ref[p, pl.ds(spot, local, stride=2 * rows), :] = mixed[:, 128 * i : 128 * i + 128]
    after = (flat(x_ref) + dot(flat(mixed_ref).astype(BF16), w_ref[...])).astype(BF16)
    after_ref[...] = after
    normed_ref[...] = norm(after.astype(F32), gain_ref[...])
    size = tokens // len(outs)
    for s, out in enumerate(outs):
        start = pl.multiple_of(((plane + s) % len(outs)) * size, size)
        out[...] = normed_ref[pl.ds(start, size), :].astype(BF16)


def pack_kernel(*refs):
    for i, source in enumerate(refs[:-1]):
        refs[-1][i] = source[...]


def block_of(own):
    return 4 if own % 4 == 0 else own


def heads_of(place_ref, wide):
    return pl.ds(pl.multiple_of(place_ref[0] % 2 * wide, 128), wide)


def column_project_kernel(scale, steps, columns, depth_ref, prot_ref, place_ref, wq_ref, wk_ref, wv_ref, *refs):
    planes = len(steps)
    ins, (live_ref, even_ref, odd_ref, key_ref, value_ref, all_ref) = refs[:planes], refs[planes:]
    gather_tokens(ins, columns, all_ref)
    wide = key_ref.shape[1]
    heads = heads_of(place_ref, wide)
    query = dot(all_ref[...], wq_ref[:, heads]).astype(BF16).astype(F32) * scale
    for side, out in zip(half_masks(wide), (even_ref, odd_ref)):
        out[...] = (query * side).astype(BF16)
    for w_ref, out in ((wk_ref, key_ref), (wv_ref, value_ref)):
        out[...] = dot(all_ref[...], w_ref[:, heads]).astype(BF16)
    slots, local = 2 * planes, columns // 2
    own = local // planes
    rows = ins[0].shape[0] // own
    block = block_of(own)
    piece = block * rows
    chunk = slots * piece
    pair = 8 // rows
    place = place_ref[0]
    core, line, plane = place % 2, (place // 2) % 2, place // PLANE
    lane = (iota((8, 2 * chunk), 1) % piece) // rows
    level = iota((8, 2 * chunk), 0)
    fits = level // rows == lane % pair
    for g in range(own // block):
        depth = jnp.zeros((8, 2 * chunk), jnp.int32)
        for c in range(block):
            index = plane * own + g * block + c
            column = index % (local // 2) + (local // 2) * line + local * (index // (local // 2))
            depth = jnp.where(lane == c, depth_ref[prot_ref[column]], depth)
        for i in range(slots):
            away = ((plane + planes - steps[i % planes]) % planes) * 2 + (core if i < planes else 1 - core)
            live_ref[g, i] = jnp.where(fits & (level % rows + away * rows < depth), 1.0, 0.0)


def gather_tokens(sources, columns, all_ref):
    planes = len(sources)
    own = columns // 2 // planes
    piece = block_of(own) * sources[0].shape[0] // own
    for g in range(own // block_of(own)):
        for i, source in enumerate(sources):
            start = (g * planes + i) * piece
            all_ref[start : start + piece, :] = source[g * piece : (g + 1) * piece, :]


def column_kernel(
    scale,
    columns,
    place_ref,
    wq_ref,
    wk_ref,
    wv_ref,
    live_ref,
    even_ref,
    odd_ref,
    key_ref,
    value_ref,
    other_ref,
    keep_ref,
    send_ref,
    all_ref,
    mixed_ref,
):
    planes, size, width = other_ref.shape
    wide = width // 2
    slots, local = 2 * planes, columns // 2
    own = local // planes
    rows = size // own
    block = block_of(own)
    piece = block * rows
    chunk = slots * piece
    chunks = own // block
    fold = piece // 8
    pair = 8 // rows
    gather_tokens([other_ref.at[i] for i in range(planes)], columns, all_ref)
    heads = heads_of(place_ref, wide)
    half = chunk // 2

    def woven(mine, other):
        parts = []
        for start in range(0, planes * size, half):
            parts += [mine[start : start + half], other[start : start + half]]
        return jnp.concatenate(parts, axis=0)

    query = dot(all_ref[...], wq_ref[:, heads]).astype(BF16).astype(F32) * scale
    sides = [
        woven(mine_ref[...], (query * side).astype(BF16))
        for mine_ref, side in zip((even_ref, odd_ref), half_masks(wide))
    ]
    key = woven(key_ref[...], dot(all_ref[...], wk_ref[:, heads]).astype(BF16))
    value = woven(value_ref[...], dot(all_ref[...], wv_ref[:, heads]).astype(BF16))
    unit = jnp.where(iota((128, 128), 0) == iota((128, 128), 1), 1.0, 0.0).astype(BF16)
    lane = (iota((8, 2 * chunk), 1) % piece) // rows
    mine = [jnp.where(lane // pair == v, 1.0, 0.0)[None] for v in range(fold)]
    lives = [live_ref[g] > 0.5 for g in range(chunks)]
    packs, values = [], []
    for q in range(wide // 128):
        lanes = slice(128 * q, 128 * q + 128)
        for g in range(chunks):
            part = slice(g * chunk, g * chunk + chunk)
            both = jnp.concatenate([side[part, lanes] for side in sides], axis=0)
            scores = dot_t(key[part, lanes], both).reshape(slots, fold, 8, 2 * chunk)
            packed = scores[:, 0]
            for v in range(1, fold):
                packed = jnp.where(mine[v] > 0.5, scores[:, v], packed)
            packs.append(jnp.where(lives[g], packed, NEG))
        values.append(dot_t(unit, value[:, lanes]).astype(BF16))
    packs = [jnp.exp(packed - jnp.max(packed, axis=(0, 1), keepdims=True)) for packed in packs]
    packs = [packed * (1.0 / jnp.sum(packed, axis=(0, 1), keepdims=True)) for packed in packs]
    for q, value in enumerate(values):
        for g in range(chunks):
            part = slice(g * chunk, g * chunk + chunk)
            weight = packs[q * chunks + g]
            spread = jnp.stack([weight * m for m in mine], axis=1).reshape(chunk, 2 * chunk).astype(BF16)
            for s in range(2):
                mixed = dot(value[64 * s : 64 * s + 64, part], spread[:, s * chunk : (s + 1) * chunk])
                mixed_ref[128 * q + 64 * s : 128 * q + 64 * s + 64, part] = mixed.astype(BF16)
    turn = jnp.where(iota((chunk, chunk), 0) == iota((chunk, chunk), 1), 1.0, 0.0).astype(BF16)
    for g in range(chunks):
        mixed = dot_t(turn, mixed_ref[:, g * chunk : (g + 1) * chunk])
        for i in range(slots):
            target = keep_ref if i < planes else send_ref
            target[i % planes, g * piece : (g + 1) * piece, :] = mixed[i * piece : (i + 1) * piece].astype(BF16)


def join_kernel(place_ref, keep_ref, other_ref, *outs):
    wide = keep_ref.shape[2]
    core = place_ref[0] % 2

    def write(left, right):
        for s, out in enumerate(outs):
            out[:, :wide] = left[s]
            out[:, wide:] = right[s]

    @pl.when(core == 0)
    def _():
        write(keep_ref, other_ref)

    @pl.when(core == 1)
    def _():
        write(other_ref, keep_ref)


def column_output_kernel(steps, place_ref, w_ref, after_ref, *refs):
    ins, (keep_ref, send_ref, total_ref) = refs[:-3], refs[-3:]
    rows, local, _ = keep_ref.shape
    core, plane = place_ref[0] % 2, place_ref[0] // PLANE
    size = ins[0].shape[0]
    total = dot(jnp.concatenate([source[...] for source in ins], axis=0), w_ref[...])
    for i, s in enumerate(steps):
        start = pl.multiple_of(((plane + s) % len(ins)) * size, size)
        for p in range(total.shape[1] // 128):
            total_ref[p, pl.ds(start, size), :] = total[i * size : (i + 1) * size, 128 * p : 128 * p + 128]
    for p in range(total.shape[1] // 128):
        lanes = slice(128 * p, 128 * p + 128)
        total_ref[p] = total_ref[p] + after_ref[:, lanes].astype(F32)
        for r in range(rows):
            for target, index in ((keep_ref, core), (send_ref, 1 - core)):
                row = total_ref[p, pl.ds(index * rows + r, local, stride=2 * rows), :]
                target[r, :, lanes] = row.astype(BF16)


def assemble_kernel(place_ref, mine_ref, other_ref, out_ref, sems):
    core = place_ref[0] % 2
    local = mine_ref.shape[1]
    quarter = local // 2
    copies = []
    for source, index in ((mine_ref, core), (other_ref, 1 - core)):
        for y in range(2):
            start = pl.multiple_of(y * local + index * quarter, quarter)
            copies.append(
                pltpu.make_async_copy(
                    source.at[:, y * quarter : (y + 1) * quarter, :],
                    out_ref.at[:, pl.ds(start, quarter), :],
                    sems.at[len(copies)],
                )
            )
    for copy in copies:
        copy.start()
    for copy in copies:
        copy.wait()


def hbm(array):
    return pltpu.with_memory_space_constraint(array, pltpu.HBM)


def swap(array, offset):
    devices = lax.axis_size("seq")
    return lax.ppermute(array, "seq", [(i, i ^ offset) for i in range(devices)])


def spin_pairs(step):
    planes = lax.axis_size("seq") // PLANE
    pairs = []
    for z in range(planes):
        for y in range(2):
            for k in range(2):
                pairs.append((z * PLANE + 2 * y + k, (z + step) % planes * PLANE + 2 * k + y))
    return pairs


def far_first(planes):
    return sorted(range(planes), key=lambda s: (-min(s, planes - s), s))


def shift(array, step):
    devices = lax.axis_size("seq")
    if step == 0:
        return array
    return lax.ppermute(array, "seq", [(i, (i + PLANE * step) % devices) for i in range(devices)])


def spin(array, step):
    return lax.ppermute(array, "seq", spin_pairs(step))


def spin_back(array, step):
    return lax.ppermute(array, "seq", [(b, a) for a, b in spin_pairs(step)])


def per_device(
    alignment,
    protein_id,
    row_depth,
    row_gain,
    row_query,
    row_key,
    row_value,
    row_output,
    column_gain,
    column_query,
    column_key,
    column_value,
    column_output,
):
    rows, columns, width = alignment.shape
    devices = lax.axis_size("seq")
    place = lax.axis_index("seq").astype(jnp.int32)[None]
    total_rows = rows * devices
    head_size = width // H
    tokens = rows * columns
    planes, local = devices // PLANE, columns // 2
    size = tokens // planes
    sum_steps = back_steps = share_steps = far_first(planes)
    move_steps = [s for s in (1, 0) if s < planes] + [s for s in back_steps if s > 1]
    x = alignment.reshape(tokens, width)
    shape = jax.ShapeDtypeStruct
    square = 2 * tokens * width * width

    part = shape((local // planes, width), F32)
    matrix = shape((width, width), BF16)
    sibling = swap(x, 1)
    normed, query, key, row_query, row_key, same, seen = call(
        functools.partial(row_own_kernel, columns),
        (shape((tokens, width), BF16), shape((tokens // 2, width), BF16), shape((tokens, width), BF16), matrix, matrix)
        + (shape((columns, columns), F32),) * 2,
        "shhhhhh",
        "v" * 7,
        [
            pltpu.VMEM((tokens, width), BF16),
            pltpu.VMEM((width,), F32),
            pltpu.SMEM(row_depth.shape, jnp.int32),
            pltpu.VMEM((columns,), jnp.int32),
            pltpu.SemaphoreType.DMA((4 + 2 * (width // 256),)),
        ],
        (3 * square // 2, 4 * width * width, tokens),
        "row_own",
    )(place, hbm(x), hbm(row_gain), hbm(row_query), hbm(row_key), hbm(row_depth), hbm(protein_id))
    *pieces, normed_other = call(
        row_scores_kernel,
        (part,) * planes + (shape((tokens, width), BF16),),
        "s" + "v" * 8,
        "v" * (planes + 1),
        [pltpu.VMEM((planes, local // planes, width), F32)],
        (3 * square // 2, 4 * width * width, tokens),
        "row_scores",
    )(place, sibling, row_gain, row_query, row_key, query, key, same, seen)
    column_query, column_key, column_value, late, normed = lax.optimization_barrier(
        (column_query, column_key, column_value, x, normed)
    )
    (total,) = call(
        add_kernel, (part,), "v" * planes, "v", [], (columns * width, 2 * columns * width, 0), "add"
    )(*[shift(pieces[s], s) for s in sum_steps])
    value, value_other, spread = call(
        functools.partial(row_value_kernel, columns),
        (shape((tokens, width), BF16),) * 2 + (shape((width // 128, tokens, 128), F32),),
        "svvvvv",
        "vvv",
        [],
        (2 * square, 2 * width * width, 0),
        "row_value",
    )(place, normed, normed_other, row_value, late, sibling)
    (weights,) = call(
        functools.partial(row_softmax_kernel, 1.0 / (math.sqrt(head_size) * math.sqrt(total_rows))),
        (shape((local // planes, width), BF16),),
        "svvv",
        "v",
        [pltpu.VMEM((columns * planes // local, local // planes, columns), F32)],
        (columns * width, 2 * columns * width, columns * width // 8),
        "row_softmax",
    )(place, total, swap(total, 2), same)
    shared = [shift(weights, s) for s in share_steps]
    after, *blocks = call(
        functools.partial(row_output_kernel, share_steps),
        (shape((tokens, width), BF16),) + (shape((size, width), BF16),) * planes,
        "s" + "v" * (6 + planes),
        "v" * (1 + planes),
        [
            pltpu.VMEM((width // 128, tokens, 128), F32),
            pltpu.VMEM((planes, local // planes, width), F32),
            pltpu.VMEM((tokens, width), F32),
        ],
        (square, 2 * width * width, tokens),
        "row_output",
    )(place, same, value, value_other, spread, row_output, column_gain[None], *shared)
    moved = [spin(blocks[s], s) for s in move_steps]
    wide = width // 2
    (packed,) = call(
        pack_kernel,
        (shape((planes, size, width), BF16),),
        "v" * planes,
        "v",
        [],
        (tokens * width, 4 * tokens * width, 0),
        "pack",
    )(*moved)
    block = block_of(local // planes)
    chunk = 2 * planes * block * 2 * rows
    scale = 1.0 / math.sqrt(head_size)
    ours = call(
        functools.partial(column_project_kernel, scale, move_steps, columns),
        (shape((local // planes // block, 2 * planes, 8, 2 * chunk), F32),) + (shape((tokens, wide), BF16),) * 4,
        "sssvvv" + "v" * planes,
        "v" * 5,
        [pltpu.VMEM((tokens, width), BF16)],
        (3 * square // 2, 3 * width * width, 0),
        "column_project",
    )(row_depth, protein_id, place, column_query, column_key, column_value, *moved)
    halves = shape((planes, size, wide), BF16)
    keep, send = call(
        functools.partial(column_kernel, scale, columns),
        (halves, halves),
        "s" + "v" * 9,
        "vv",
        [pltpu.VMEM((tokens, width), BF16), pltpu.VMEM((wide, 2 * tokens), BF16)],
        (4 * square, 6 * width * width, H * tokens * tokens // 4),
        "column_attention",
    )(place, column_query, column_key, column_value, *ours, swap(packed, 1))
    joined = call(
        join_kernel,
        (shape((size, width), BF16),) * planes,
        "svv",
        "v" * planes,
        [],
        (tokens * width, 4 * tokens * width, 0),
        "join",
    )(place, keep, swap(send, 1))
    returned = [spin_back(joined[move_steps.index(s)], s) for s in back_steps]
    half = shape((rows, local, width), BF16)
    keep, send = call(
        functools.partial(column_output_kernel, back_steps),
        (half, half),
        "svv" + "v" * planes,
        "vv",
        [pltpu.VMEM((width // 128, tokens, 128), F32)],
        (square, 2 * width * width, 0),
        "column_output",
    )(place, column_output, after, *returned)
    (out,) = call(
        assemble_kernel,
        (shape((rows, columns, width), BF16),),
        "svv",
        "a",
        [pltpu.SemaphoreType.DMA((4,))],
        (tokens * width, 4 * tokens * width, 0),
        "assemble",
    )(place, keep, swap(send, 1))
    return out


def solution(mesh):
    return jax.shard_map(
        per_device,
        mesh=mesh,
        in_specs=(P(("grp", "seq"), None, None), P("grp"), P("grp")) + (P(),) * 10,
        out_specs=P(("grp", "seq"), None, None),
        check_vma=False,
    )
```

```python
import functools
import math

import jax
import jax.numpy as jnp
from jax import lax
from jax.experimental import pallas as pl
from jax.experimental.pallas import tpu as pltpu
from jax.sharding import PartitionSpec as P

H = 12
EPS = 1e-05
NEG = -1000000000.0
F32 = jnp.float32
BF16 = jnp.bfloat16
LIMIT = 20 << 20
PLANE = 4


def call(kernel, out_shape, ins, outs, scratch, cost, name):
    spaces = {"v": pltpu.VMEM, "s": pltpu.SMEM, "h": pltpu.HBM, "a": pl.ANY}
    return pl.pallas_call(
        kernel,
        out_shape=out_shape,
        in_specs=[pl.BlockSpec(memory_space=spaces[c]) for c in ins],
        out_specs=[pl.BlockSpec(memory_space=spaces[c]) for c in outs],
        scratch_shapes=scratch,
        compiler_params=pltpu.CompilerParams(vmem_limit_bytes=LIMIT),
        cost_estimate=pl.CostEstimate(flops=cost[0], bytes_accessed=cost[1], transcendentals=cost[2]),
        name=name,
    )


def norm(full, gain):
    middle = jnp.mean(full, axis=-1, keepdims=True)
    spread = jnp.mean((full - middle) ** 2, axis=-1, keepdims=True)
    return (full - middle) * lax.rsqrt(spread + EPS) * gain


def dot(a, b):
    return jnp.dot(a, b, preferred_element_type=F32)


def dot_t(a, b):
    return lax.dot_general(a, b, (((1,), (1,)), ((), ())), preferred_element_type=F32)


def iota(shape, dim):
    return lax.broadcasted_iota(jnp.int32, shape, dim)


def flat(ref):
    return jnp.concatenate([ref[p] for p in range(ref.shape[0])], axis=1)


def to_column(row, size):
    eye = iota((size, size), 0) == iota((size, size), 1)
    return jnp.sum(jnp.where(eye, jnp.broadcast_to(row, (size, size)), 0.0), axis=1, keepdims=True)


def half_masks(width):
    low = (iota((1, width), 1) % 128) < 64
    return jnp.where(low, 1.0, 0.0), jnp.where(low, 0.0, 1.0)


def own_columns(array, core, quarter):
    pieces = []
    for y in range(PLANE // 2):
        left, right = (array[(2 * y + k) * quarter : (2 * y + k + 1) * quarter] for k in range(2))
        pieces.append(jnp.where(core, left, right))
    return jnp.concatenate(pieces, axis=0)


def query_tokens(normed_ref, place_ref, columns):
    quarter = columns // PLANE
    core = place_ref[0] % 2
    pieces = []
    for start in range(0, normed_ref.shape[0], columns // 2):
        pieces.append(normed_ref[pl.ds(pl.multiple_of(start + core * quarter, quarter), quarter), :])
    return jnp.concatenate(pieces, axis=0)


def row_own_kernel(
    columns,
    place_ref,
    x_hbm,
    gain_hbm,
    wq_hbm,
    wk_hbm,
    depth_hbm,
    prot_hbm,
    normed_ref,
    query_ref,
    key_ref,
    wq_ref,
    wk_ref,
    same_ref,
    seen_ref,
    live_ref,
    x_ref,
    gain_ref,
    depth_ref,
    prot_ref,
    mask_ref,
    sems,
):
    tokens, width = x_ref.shape
    pairs = [(x_hbm, x_ref), (gain_hbm, gain_ref), (depth_hbm, depth_ref), (prot_hbm, prot_ref)]
    for n in range(width // 256):
        for source, target in ((wq_hbm, wq_ref), (wk_hbm, wk_ref)):
            pairs.append((source.at[256 * n : 256 * n + 256], target.at[256 * n : 256 * n + 256]))
    copies = [pltpu.make_async_copy(a, b, sems.at[i]) for i, (a, b) in enumerate(pairs)]
    for copy in copies:
        copy.start()
    for copy in copies[:2]:
        copy.wait()
    normed_ref[...] = norm(x_ref[...].astype(F32), gain_ref[...].reshape(1, width)).astype(BF16)
    for copy in copies[2:4]:
        copy.wait()
    prot = prot_ref[...].reshape(1, columns).astype(F32)
    depth = jnp.zeros((1, columns), F32)
    for p in range(depth_ref.shape[0]):
        depth = jnp.where(prot == float(p), depth_ref[p].astype(F32), depth)
    square = (columns, columns)
    same = jnp.broadcast_to(to_column(prot, columns), square) == jnp.broadcast_to(prot, square)
    same = jnp.where(same, 1.0, 0.0)
    core, quarter = place_ref[0] % 2, columns // PLANE
    same = own_columns(same, core == 0, quarter)
    same_ref[...] = same
    mask = jnp.maximum(same, pltpu.roll(same, 64, 1))
    own = live_ref.shape[0]
    for i in range(mask_ref.shape[0]):
        mask_ref[i] = mask[i * own : (i + 1) * own]
    live_ref[...] = mask_ref[place_ref[0] // PLANE]
    seen_ref[...] = jnp.broadcast_to(to_column(depth, columns), square)
    for copy in copies[4:]:
        copy.wait()
    query_ref[...] = dot(query_tokens(normed_ref, place_ref, columns), wq_ref[...]).astype(BF16)
    key_ref[...] = dot(normed_ref[...], wk_ref[...]).astype(BF16)


def row_scores_kernel(
    place_ref,
    x_ref,
    gain_ref,
    wq_ref,
    wk_ref,
    query_ref,
    key_ref,
    same_ref,
    seen_ref,
    *refs,
):
    outs, (normed_ref, part_ref) = refs[:-2], refs[-2:]
    columns = same_ref.shape[1]
    tokens, width = x_ref.shape
    rows, local, quarter = tokens // columns, columns // 2, columns // PLANE
    planes, own = part_ref.shape[:2]
    place = place_ref[0]
    core = (place % 2) == 0
    normed_ref[...] = norm(x_ref[...].astype(F32), gain_ref[...].reshape(1, width)).astype(BF16)
    same_l = same_ref[...]
    seen = seen_ref[...]
    depth_l = own_columns(seen, core, quarter)
    low = iota((local, columns), 1) < 64
    first = jnp.where(low, same_l, pltpu.roll(same_l, 64, 1)) > 0.5
    even, odd = half_masks(256)
    other = place + 1 - 2 * (place % 2)
    ids = [place * rows + r for r in range(rows)] + [other * rows + r for r in range(rows)]
    seen_q = [jnp.where(i.astype(F32) < depth_l, 1.0, 0.0) for i in ids]
    seen_k = [jnp.where(i.astype(F32) < seen, 1.0, 0.0) for i in ids]
    seen_q, seen_k = ([jnp.concatenate([m, m], axis=1) for m in masks] for masks in (seen_q, seen_k))
    tokens_q = query_tokens(normed_ref, place_ref, columns)
    for n in range(width // 256):
        cols = slice(256 * n, 256 * n + 256)
        queries = (query_ref[:, cols].astype(F32), dot(tokens_q, wq_ref[:, cols]).astype(BF16).astype(F32))
        keys = (key_ref[:, cols].astype(F32), dot(normed_ref[...], wk_ref[:, cols]))
        query, key = [], []
        for i in range(2 * rows):
            r = i % rows
            query.append(queries[i // rows][r * local : (r + 1) * local] * seen_q[i])
            key.append((keys[i // rows][r * columns : (r + 1) * columns] * seen_k[i]).astype(BF16))
        query_sides = [[(q * side).astype(BF16) for q in query] for side in (even, odd)]
        for q in range(2):
            lanes = slice(128 * q, 128 * q + 128)
            both = [jnp.concatenate([a[:, lanes] for a in side], axis=1) for side in query_sides]
            both = jnp.concatenate(both, axis=0)
            logits = dot_t(both, jnp.concatenate([a[:, lanes] for a in key], axis=1))
            one, two = logits[:local], logits[local:]
            folded = jnp.where(
                low,
                jnp.where(first, one, pltpu.roll(one, 64, 1)),
                jnp.where(first, pltpu.roll(two, 64, 1), two),
            )
            out = slice(256 * n + 128 * q, 256 * n + 128 * q + 128)
            for i in range(planes):
                part_ref[i, :, out] = folded[i * own : (i + 1) * own]
    plane = place // PLANE
    for s, target in enumerate(outs):
        target[...] = part_ref[(plane + s) % planes]


def add_kernel(*refs):
    parts = [ref[...] for ref in refs[:-1]]
    while len(parts) > 1:
        parts = [a + b for a, b in zip(parts[::2], parts[1::2])]
    refs[-1][...] = parts[0]


def row_value_kernel(
    columns, place_ref, x_ref, y_ref, w_ref, mine_ref, other_ref, out_ref, next_ref, spread_ref
):
    core = place_ref[0] % 2
    out_ref[...] = dot(x_ref[...], w_ref[...]).astype(BF16)
    next_ref[...] = dot(y_ref[...], w_ref[...]).astype(BF16)
    rows = x_ref.shape[0] // columns
    quarter = columns // PLANE
    for source, index in ((mine_ref, core), (other_ref, 1 - core)):
        for r in range(rows):
            for y in range(2):
                start = pl.multiple_of(r * columns + y * columns // 2 + quarter * core, quarter)
                piece = source[pl.ds(start, quarter), :].astype(F32)
                target = pl.ds(2 * rows * quarter * y + index * rows + r, quarter, stride=2 * rows)
                for p in range(piece.shape[1] // 128):
                    spread_ref[p, target, :] = piece[:, 128 * p : 128 * p + 128]


def row_softmax_kernel(scale, mine_ref, other_ref, live_ref, out_ref):
    own, width = out_ref.shape
    live = live_ref[...] > 0.5
    low = iota((own, 128), 1) < 64
    for p in range(width // 128):
        lanes = slice(128 * p, 128 * p + 128)
        tied = jnp.where(live, (mine_ref[:, lanes] + other_ref[:, lanes]) * scale, NEG)
        top_low = jnp.max(jnp.where(low, tied, 2 * NEG), axis=1, keepdims=True)
        top_high = jnp.max(jnp.where(low, 2 * NEG, tied), axis=1, keepdims=True)
        value = jnp.exp(tied - jnp.where(low, top_low, top_high))
        sum_low = jnp.sum(jnp.where(low, value, 0.0), axis=1, keepdims=True)
        sum_high = jnp.sum(jnp.where(low, 0.0, value), axis=1, keepdims=True)
        out_ref[:, lanes] = (value / jnp.where(low, sum_low, sum_high)).astype(BF16)


def row_output_kernel(
    steps,
    place_ref,
    same_ref,
    value_ref,
    other_ref,
    x_ref,
    w_ref,
    gain_ref,
    *refs,
):
    planes = (len(refs) - 4) // 2
    pieces, after_ref, outs = refs[:planes], refs[planes], refs[planes + 1 : -3]
    mixed_ref, folded_ref, normed_ref = refs[-3:]
    columns = same_ref.shape[1]
    tokens, width = after_ref.shape
    rows = tokens // columns
    quarter, local = columns // PLANE, columns // 2
    place = place_ref[0]
    core, plane = place % 2, place // PLANE
    own = local // planes
    for s, piece in zip(steps, pieces):
        folded_ref[(plane + planes - s) % planes] = piece[...].astype(F32)
    same = same_ref[...] > 0.5
    low = iota((local, columns), 1) < 64
    even, odd = half_masks(256 * rows)
    even, odd = even.astype(BF16), odd.astype(BF16)
    spots = [core * rows + r for r in range(rows)] + [(1 - core) * rows + r for r in range(rows)]
    for p in range(width // 128):
        lanes = slice(128 * p, 128 * p + 128)
        piece = folded_ref[:, :, lanes].reshape(local, 128)
        turned = pltpu.roll(piece, 64, 1)
        one = jnp.where(same, jnp.where(low, piece, turned), 0.0)
        two = jnp.where(same, jnp.where(low, turned, piece), 0.0)
        weights = jnp.concatenate([one, two], axis=1).astype(BF16)
        value = jnp.concatenate(
            [
                source[r * columns : (r + 1) * columns, lanes]
                for source in (value_ref, other_ref)
                for r in range(rows)
            ],
            axis=1,
        )
        value = jnp.concatenate([value * even, value * odd], axis=0)
        mixed = dot(weights, value)
        for i, spot in enumerate(spots):
            mixed_ref[p, pl.ds(spot, local, stride=2 * rows), :] = mixed[:, 128 * i : 128 * i + 128]
    after = (flat(x_ref) + dot(flat(mixed_ref).astype(BF16), w_ref[...])).astype(BF16)
    after_ref[...] = after
    normed_ref[...] = norm(after.astype(F32), gain_ref[...])
    size = tokens // len(outs)
    for s, out in enumerate(outs):
        start = pl.multiple_of(((plane + s) % len(outs)) * size, size)
        out[...] = normed_ref[pl.ds(start, size), :].astype(BF16)


def pack_kernel(*refs):
    for i, source in enumerate(refs[:-1]):
        refs[-1][i] = source[...]


def block_of(own):
    return 4 if own % 4 == 0 else own


def heads_of(place_ref, wide):
    return pl.ds(pl.multiple_of(place_ref[0] % 2 * wide, 128), wide)


def column_project_kernel(scale, steps, columns, depth_ref, prot_ref, place_ref, wq_ref, wk_ref, wv_ref, *refs):
    planes = len(steps)
    ins, (live_ref, even_ref, odd_ref, key_ref, value_ref, all_ref) = refs[:planes], refs[planes:]
    gather_tokens(ins, columns, all_ref)
    wide = key_ref.shape[1]
    heads = heads_of(place_ref, wide)
    query = dot(all_ref[...], wq_ref[:, heads]).astype(BF16).astype(F32) * scale
    for side, out in zip(half_masks(wide), (even_ref, odd_ref)):
        out[...] = (query * side).astype(BF16)
    for w_ref, out in ((wk_ref, key_ref), (wv_ref, value_ref)):
        out[...] = dot(all_ref[...], w_ref[:, heads]).astype(BF16)
    slots, local = 2 * planes, columns // 2
    own = local // planes
    rows = ins[0].shape[0] // own
    block = block_of(own)
    piece = block * rows
    chunk = slots * piece
    pair = 8 // rows
    place = place_ref[0]
    core, line, plane = place % 2, (place // 2) % 2, place // PLANE
    lane = (iota((8, 2 * chunk), 1) % piece) // rows
    level = iota((8, 2 * chunk), 0)
    fits = level // rows == lane % pair
    for g in range(own // block):
        depth = jnp.zeros((8, 2 * chunk), jnp.int32)
        for c in range(block):
            index = plane * own + g * block + c
            column = index % (local // 2) + (local // 2) * line + local * (index // (local // 2))
            depth = jnp.where(lane == c, depth_ref[prot_ref[column]], depth)
        for i in range(slots):
            away = ((plane + planes - steps[i % planes]) % planes) * 2 + (core if i < planes else 1 - core)
            live_ref[g, i] = jnp.where(fits & (level % rows + away * rows < depth), 1.0, 0.0)


def gather_tokens(sources, columns, all_ref):
    planes = len(sources)
    own = columns // 2 // planes
    piece = block_of(own) * sources[0].shape[0] // own
    for g in range(own // block_of(own)):
        for i, source in enumerate(sources):
            start = (g * planes + i) * piece
            all_ref[start : start + piece, :] = source[g * piece : (g + 1) * piece, :]


def column_kernel(
    scale,
    columns,
    place_ref,
    wq_ref,
    wk_ref,
    wv_ref,
    live_ref,
    even_ref,
    odd_ref,
    key_ref,
    value_ref,
    other_ref,
    keep_ref,
    send_ref,
    all_ref,
    mixed_ref,
):
    planes, size, width = other_ref.shape
    wide = width // 2
    slots, local = 2 * planes, columns // 2
    own = local // planes
    rows = size // own
    block = block_of(own)
    piece = block * rows
    chunk = slots * piece
    chunks = own // block
    fold = piece // 8
    pair = 8 // rows
    gather_tokens([other_ref.at[i] for i in range(planes)], columns, all_ref)
    heads = heads_of(place_ref, wide)
    half = chunk // 2

    def woven(mine, other):
        parts = []
        for start in range(0, planes * size, half):
            parts += [mine[start : start + half], other[start : start + half]]
        return jnp.concatenate(parts, axis=0)

    query = dot(all_ref[...], wq_ref[:, heads]).astype(BF16).astype(F32) * scale
    sides = [
        woven(mine_ref[...], (query * side).astype(BF16))
        for mine_ref, side in zip((even_ref, odd_ref), half_masks(wide))
    ]
    key = woven(key_ref[...], dot(all_ref[...], wk_ref[:, heads]).astype(BF16))
    value = woven(value_ref[...], dot(all_ref[...], wv_ref[:, heads]).astype(BF16))
    unit = jnp.where(iota((128, 128), 0) == iota((128, 128), 1), 1.0, 0.0).astype(BF16)
    lane = (iota((8, 2 * chunk), 1) % piece) // rows
    mine = [jnp.where(lane // pair == v, 1.0, 0.0)[None] for v in range(fold)]
    lives = [live_ref[g] > 0.5 for g in range(chunks)]
    packs, values = [], []
    for q in range(wide // 128):
        lanes = slice(128 * q, 128 * q + 128)
        for g in range(chunks):
            part = slice(g * chunk, g * chunk + chunk)
            both = jnp.concatenate([side[part, lanes] for side in sides], axis=0)
            scores = dot_t(key[part, lanes], both).reshape(slots, fold, 8, 2 * chunk)
            packed = scores[:, 0]
            for v in range(1, fold):
                packed = jnp.where(mine[v] > 0.5, scores[:, v], packed)
            packs.append(jnp.where(lives[g], packed, NEG))
        values.append(dot_t(unit, value[:, lanes]).astype(BF16))
    packs = [jnp.exp(packed - jnp.max(packed, axis=(0, 1), keepdims=True)) for packed in packs]
    packs = [packed * (1.0 / jnp.sum(packed, axis=(0, 1), keepdims=True)) for packed in packs]
    for q, value in enumerate(values):
        for g in range(chunks):
            part = slice(g * chunk, g * chunk + chunk)
            weight = packs[q * chunks + g]
            spread = jnp.stack([weight * m for m in mine], axis=1).reshape(chunk, 2 * chunk).astype(BF16)
            for s in range(2):
                mixed = dot(value[64 * s : 64 * s + 64, part], spread[:, s * chunk : (s + 1) * chunk])
                mixed_ref[128 * q + 64 * s : 128 * q + 64 * s + 64, part] = mixed.astype(BF16)
    turn = jnp.where(iota((chunk, chunk), 0) == iota((chunk, chunk), 1), 1.0, 0.0).astype(BF16)
    for g in range(chunks):
        mixed = dot_t(turn, mixed_ref[:, g * chunk : (g + 1) * chunk])
        for i in range(slots):
            target = keep_ref if i < planes else send_ref
            target[i % planes, g * piece : (g + 1) * piece, :] = mixed[i * piece : (i + 1) * piece].astype(BF16)


def join_kernel(place_ref, keep_ref, other_ref, *outs):
    wide = keep_ref.shape[2]
    core = place_ref[0] % 2

    def write(left, right):
        for s, out in enumerate(outs):
            out[:, :wide] = left[s]
            out[:, wide:] = right[s]

    @pl.when(core == 0)
    def _():
        write(keep_ref, other_ref)

    @pl.when(core == 1)
    def _():
        write(other_ref, keep_ref)


def column_output_kernel(steps, place_ref, w_ref, after_ref, *refs):
    ins, (keep_ref, send_ref, total_ref) = refs[:-3], refs[-3:]
    rows, local, _ = keep_ref.shape
    core, plane = place_ref[0] % 2, place_ref[0] // PLANE
    size = ins[0].shape[0]
    total = dot(jnp.concatenate([source[...] for source in ins], axis=0), w_ref[...])
    for i, s in enumerate(steps):
        start = pl.multiple_of(((plane + s) % len(ins)) * size, size)
        for p in range(total.shape[1] // 128):
            total_ref[p, pl.ds(start, size), :] = total[i * size : (i + 1) * size, 128 * p : 128 * p + 128]
    for p in range(total.shape[1] // 128):
        lanes = slice(128 * p, 128 * p + 128)
        total_ref[p] = total_ref[p] + after_ref[:, lanes].astype(F32)
        for r in range(rows):
            for target, index in ((keep_ref, core), (send_ref, 1 - core)):
                row = total_ref[p, pl.ds(index * rows + r, local, stride=2 * rows), :]
                target[r, :, lanes] = row.astype(BF16)


def assemble_kernel(place_ref, mine_ref, other_ref, out_ref, sems):
    core = place_ref[0] % 2
    local = mine_ref.shape[1]
    quarter = local // 2
    copies = []
    for source, index in ((mine_ref, core), (other_ref, 1 - core)):
        for y in range(2):
            start = pl.multiple_of(y * local + index * quarter, quarter)
            copies.append(
                pltpu.make_async_copy(
                    source.at[:, y * quarter : (y + 1) * quarter, :],
                    out_ref.at[:, pl.ds(start, quarter), :],
                    sems.at[len(copies)],
                )
            )
    for copy in copies:
        copy.start()
    for copy in copies:
        copy.wait()


def hbm(array):
    return pltpu.with_memory_space_constraint(array, pltpu.HBM)


def swap(array, offset):
    devices = lax.axis_size("seq")
    return lax.ppermute(array, "seq", [(i, i ^ offset) for i in range(devices)])


def spin_pairs(step):
    planes = lax.axis_size("seq") // PLANE
    pairs = []
    for z in range(planes):
        for y in range(2):
            for k in range(2):
                pairs.append((z * PLANE + 2 * y + k, (z + step) % planes * PLANE + 2 * k + y))
    return pairs


def far_first(planes):
    return sorted(range(planes), key=lambda s: (-min(s, planes - s), s))


def shift(array, step):
    devices = lax.axis_size("seq")
    if step == 0:
        return array
    return lax.ppermute(array, "seq", [(i, (i + PLANE * step) % devices) for i in range(devices)])


def spin(array, step):
    return lax.ppermute(array, "seq", spin_pairs(step))


def spin_back(array, step):
    return lax.ppermute(array, "seq", [(b, a) for a, b in spin_pairs(step)])


def per_device(
    alignment,
    protein_id,
    row_depth,
    row_gain,
    row_query,
    row_key,
    row_value,
    row_output,
    column_gain,
    column_query,
    column_key,
    column_value,
    column_output,
):
    rows, columns, width = alignment.shape
    devices = lax.axis_size("seq")
    place = lax.axis_index("seq").astype(jnp.int32)[None]
    total_rows = rows * devices
    head_size = width // H
    tokens = rows * columns
    planes, local = devices // PLANE, columns // 2
    size = tokens // planes
    sum_steps = back_steps = share_steps = far_first(planes)
    move_steps = [s for s in (1, 0) if s < planes] + [s for s in back_steps if s > 1]
    x = alignment.reshape(tokens, width)
    shape = jax.ShapeDtypeStruct
    square = 2 * tokens * width * width

    part = shape((local // planes, width), F32)
    matrix = shape((width, width), BF16)
    sibling = swap(x, 1)
    normed, query, key, row_query, row_key, same, seen, live = call(
        functools.partial(row_own_kernel, columns),
        (shape((tokens, width), BF16), shape((tokens // 2, width), BF16), shape((tokens, width), BF16), matrix, matrix)
        + (shape((local, columns), F32), shape((columns, columns), F32), shape((local // planes, columns), F32)),
        "shhhhhh",
        "v" * 8,
        [
            pltpu.VMEM((tokens, width), BF16),
            pltpu.VMEM((width,), F32),
            pltpu.SMEM(row_depth.shape, jnp.int32),
            pltpu.VMEM((columns,), jnp.int32),
            pltpu.VMEM((planes, local // planes, columns), F32),
            pltpu.SemaphoreType.DMA((4 + 2 * (width // 256),)),
        ],
        (3 * square // 2, 4 * width * width, tokens),
        "row_own",
    )(place, hbm(x), hbm(row_gain), hbm(row_query), hbm(row_key), hbm(row_depth), hbm(protein_id))
    *pieces, normed_other = call(
        row_scores_kernel,
        (part,) * planes + (shape((tokens, width), BF16),),
        "s" + "v" * 8,
        "v" * (planes + 1),
        [pltpu.VMEM((planes, local // planes, width), F32)],
        (3 * square // 2, 4 * width * width, tokens),
        "row_scores",
    )(place, sibling, row_gain, row_query, row_key, query, key, same, seen)
    column_query, column_key, column_value, late, normed = lax.optimization_barrier(
        (column_query, column_key, column_value, x, normed)
    )
    (total,) = call(
        add_kernel, (part,), "v" * planes, "v", [], (columns * width, 2 * columns * width, 0), "add"
    )(*[shift(pieces[s], s) for s in sum_steps])
    other_total = swap(total, 2)
    normed, _ = lax.optimization_barrier((normed, total))
    value, value_other, spread = call(
        functools.partial(row_value_kernel, columns),
        (shape((tokens, width), BF16),) * 2 + (shape((width // 128, tokens, 128), F32),),
        "svvvvv",
        "vvv",
        [],
        (2 * square, 2 * width * width, 0),
        "row_value",
    )(place, normed, normed_other, row_value, late, sibling)
    live, value = lax.optimization_barrier((live, value))
    (weights,) = call(
        functools.partial(row_softmax_kernel, 1.0 / (math.sqrt(head_size) * math.sqrt(total_rows))),
        (shape((local // planes, width), BF16),),
        "vvv",
        "v",
        [],
        (columns * width, 2 * columns * width, columns * width // 8),
        "row_softmax",
    )(total, other_total, live)
    shared = [shift(weights, s) for s in share_steps]
    after, *blocks = call(
        functools.partial(row_output_kernel, share_steps),
        (shape((tokens, width), BF16),) + (shape((size, width), BF16),) * planes,
        "s" + "v" * (6 + planes),
        "v" * (1 + planes),
        [
            pltpu.VMEM((width // 128, tokens, 128), F32),
            pltpu.VMEM((planes, local // planes, width), F32),
            pltpu.VMEM((tokens, width), F32),
        ],
        (square, 2 * width * width, tokens),
        "row_output",
    )(place, same, value, value_other, spread, row_output, column_gain[None], *shared)
    moved = [spin(blocks[s], s) for s in move_steps]
    wide = width // 2
    (packed,) = call(
        pack_kernel,
        (shape((planes, size, width), BF16),),
        "v" * planes,
        "v",
        [],
        (tokens * width, 4 * tokens * width, 0),
        "pack",
    )(*moved)
    block = block_of(local // planes)
    chunk = 2 * planes * block * 2 * rows
    scale = 1.0 / math.sqrt(head_size)
    ours = call(
        functools.partial(column_project_kernel, scale, move_steps, columns),
        (shape((local // planes // block, 2 * planes, 8, 2 * chunk), F32),) + (shape((tokens, wide), BF16),) * 4,
        "sssvvv" + "v" * planes,
        "v" * 5,
        [pltpu.VMEM((tokens, width), BF16)],
        (3 * square // 2, 3 * width * width, 0),
        "column_project",
    )(row_depth, protein_id, place, column_query, column_key, column_value, *moved)
    halves = shape((planes, size, wide), BF16)
    keep, send = call(
        functools.partial(column_kernel, scale, columns),
        (halves, halves),
        "s" + "v" * 9,
        "vv",
        [pltpu.VMEM((tokens, width), BF16), pltpu.VMEM((wide, 2 * tokens), BF16)],
        (4 * square, 6 * width * width, H * tokens * tokens // 4),
        "column_attention",
    )(place, column_query, column_key, column_value, *ours, swap(packed, 1))
    joined = call(
        join_kernel,
        (shape((size, width), BF16),) * planes,
        "svv",
        "v" * planes,
        [],
        (tokens * width, 4 * tokens * width, 0),
        "join",
    )(place, keep, swap(send, 1))
    returned = [spin_back(joined[move_steps.index(s)], s) for s in back_steps]
    half = shape((rows, local, width), BF16)
    keep, send = call(
        functools.partial(column_output_kernel, back_steps),
        (half, half),
        "svv" + "v" * planes,
        "vv",
        [pltpu.VMEM((width // 128, tokens, 128), F32)],
        (square, 2 * width * width, 0),
        "column_output",
    )(place, column_output, after, *returned)
    (out,) = call(
        assemble_kernel,
        (shape((rows, columns, width), BF16),),
        "svv",
        "a",
        [pltpu.SemaphoreType.DMA((4,))],
        (tokens * width, 4 * tokens * width, 0),
        "assemble",
    )(place, keep, swap(send, 1))
    return out


def solution(mesh):
    return jax.shard_map(
        per_device,
        mesh=mesh,
        in_specs=(P(("grp", "seq"), None, None), P("grp"), P("grp")) + (P(),) * 10,
        out_specs=P(("grp", "seq"), None, None),
        check_vma=False,
    )
```

```python
import functools
import math

import jax
import jax.numpy as jnp
from jax import lax
from jax.experimental import pallas as pl
from jax.experimental.pallas import tpu as pltpu
from jax.sharding import PartitionSpec as P

H = 12
EPS = 1e-05
NEG = -1000000000.0
F32 = jnp.float32
BF16 = jnp.bfloat16
LIMIT = 20 << 20
PLANE = 4


def call(kernel, out_shape, ins, outs, scratch, cost, name, aliases=None):
    spaces = {"v": pltpu.VMEM, "s": pltpu.SMEM, "h": pltpu.HBM}
    return pl.pallas_call(
        kernel,
        out_shape=out_shape,
        in_specs=[pl.BlockSpec(memory_space=spaces[c]) for c in ins],
        out_specs=[pl.BlockSpec(memory_space=spaces[c]) for c in outs],
        scratch_shapes=scratch,
        input_output_aliases=aliases or {},
        compiler_params=pltpu.CompilerParams(vmem_limit_bytes=LIMIT),
        cost_estimate=pl.CostEstimate(flops=cost[0], bytes_accessed=cost[1], transcendentals=cost[2]),
        name=name,
    )


def norm(full, gain):
    middle = jnp.mean(full, axis=-1, keepdims=True)
    spread = jnp.mean((full - middle) ** 2, axis=-1, keepdims=True)
    return (full - middle) * lax.rsqrt(spread + EPS) * gain


def dot(a, b):
    return jnp.dot(a, b, preferred_element_type=F32)


def dot_t(a, b):
    return lax.dot_general(a, b, (((1,), (1,)), ((), ())), preferred_element_type=F32)


def iota(shape, dim):
    return lax.broadcasted_iota(jnp.int32, shape, dim)


def flat(ref):
    return jnp.concatenate([ref[p] for p in range(ref.shape[0])], axis=1)


def to_column(row, size):
    eye = iota((size, size), 0) == iota((size, size), 1)
    return jnp.sum(jnp.where(eye, jnp.broadcast_to(row, (size, size)), 0.0), axis=1, keepdims=True)


def half_masks(width):
    low = (iota((1, width), 1) % 128) < 64
    return jnp.where(low, 1.0, 0.0), jnp.where(low, 0.0, 1.0)


def own_columns(array, core, quarter):
    pieces = []
    for y in range(PLANE // 2):
        left, right = (array[(2 * y + k) * quarter : (2 * y + k + 1) * quarter] for k in range(2))
        pieces.append(jnp.where(core, left, right))
    return jnp.concatenate(pieces, axis=0)


def query_tokens(normed_ref, place_ref, columns):
    quarter = columns // PLANE
    core = place_ref[0] % 2
    pieces = []
    for start in range(0, normed_ref.shape[0], columns // 2):
        pieces.append(normed_ref[pl.ds(pl.multiple_of(start + core * quarter, quarter), quarter), :])
    return jnp.concatenate(pieces, axis=0)


def row_own_kernel(
    columns,
    place_ref,
    x_hbm,
    gain_hbm,
    wq_hbm,
    wk_hbm,
    depth_hbm,
    prot_hbm,
    normed_ref,
    query_ref,
    key_ref,
    wq_ref,
    wk_ref,
    same_ref,
    seen_ref,
    live_ref,
    x_ref,
    gain_ref,
    depth_ref,
    prot_ref,
    mask_ref,
    sems,
):
    tokens, width = x_ref.shape
    pairs = [(x_hbm, x_ref), (gain_hbm, gain_ref), (depth_hbm, depth_ref), (prot_hbm, prot_ref)]
    for n in range(width // 256):
        for source, target in ((wq_hbm, wq_ref), (wk_hbm, wk_ref)):
            pairs.append((source.at[256 * n : 256 * n + 256], target.at[256 * n : 256 * n + 256]))
    copies = [pltpu.make_async_copy(a, b, sems.at[i]) for i, (a, b) in enumerate(pairs)]
    for copy in copies:
        copy.start()
    for copy in copies[:2]:
        copy.wait()
    normed_ref[...] = norm(x_ref[...].astype(F32), gain_ref[...].reshape(1, width)).astype(BF16)
    for copy in copies[2:4]:
        copy.wait()
    prot = prot_ref[...].reshape(1, columns).astype(F32)
    depth = jnp.zeros((1, columns), F32)
    for p in range(depth_ref.shape[0]):
        depth = jnp.where(prot == float(p), depth_ref[p].astype(F32), depth)
    square = (columns, columns)
    same = jnp.broadcast_to(to_column(prot, columns), square) == jnp.broadcast_to(prot, square)
    same = jnp.where(same, 1.0, 0.0)
    core, quarter = place_ref[0] % 2, columns // PLANE
    same = own_columns(same, core == 0, quarter)
    same_ref[...] = same
    mask = jnp.maximum(same, pltpu.roll(same, 64, 1))
    own = live_ref.shape[0]
    for i in range(mask_ref.shape[0]):
        mask_ref[i] = mask[i * own : (i + 1) * own]
    live_ref[...] = mask_ref[place_ref[0] // PLANE]
    seen_ref[...] = jnp.broadcast_to(to_column(depth, columns), square)
    for copy in copies[4:]:
        copy.wait()
    query_ref[...] = dot(query_tokens(normed_ref, place_ref, columns), wq_ref[...]).astype(BF16)
    key_ref[...] = dot(normed_ref[...], wk_ref[...]).astype(BF16)


def row_scores_kernel(
    place_ref,
    x_ref,
    gain_ref,
    wq_ref,
    wk_ref,
    query_ref,
    key_ref,
    same_ref,
    seen_ref,
    *refs,
):
    outs, (normed_ref, part_ref) = refs[:-2], refs[-2:]
    columns = same_ref.shape[1]
    tokens, width = x_ref.shape
    rows, local, quarter = tokens // columns, columns // 2, columns // PLANE
    planes, own = part_ref.shape[:2]
    place = place_ref[0]
    core = (place % 2) == 0
    normed_ref[...] = norm(x_ref[...].astype(F32), gain_ref[...].reshape(1, width)).astype(BF16)
    same_l = same_ref[...]
    seen = seen_ref[...]
    depth_l = own_columns(seen, core, quarter)
    low = iota((local, columns), 1) < 64
    first = jnp.where(low, same_l, pltpu.roll(same_l, 64, 1)) > 0.5
    even, odd = half_masks(256)
    other = place + 1 - 2 * (place % 2)
    ids = [place * rows + r for r in range(rows)] + [other * rows + r for r in range(rows)]
    seen_q = [jnp.where(i.astype(F32) < depth_l, 1.0, 0.0) for i in ids]
    seen_k = [jnp.where(i.astype(F32) < seen, 1.0, 0.0) for i in ids]
    seen_q, seen_k = ([jnp.concatenate([m, m], axis=1) for m in masks] for masks in (seen_q, seen_k))
    tokens_q = query_tokens(normed_ref, place_ref, columns)
    for n in range(width // 256):
        cols = slice(256 * n, 256 * n + 256)
        queries = (query_ref[:, cols].astype(F32), dot(tokens_q, wq_ref[:, cols]).astype(BF16).astype(F32))
        keys = (key_ref[:, cols].astype(F32), dot(normed_ref[...], wk_ref[:, cols]))
        query, key = [], []
        for i in range(2 * rows):
            r = i % rows
            query.append(queries[i // rows][r * local : (r + 1) * local] * seen_q[i])
            key.append((keys[i // rows][r * columns : (r + 1) * columns] * seen_k[i]).astype(BF16))
        query_sides = [[(q * side).astype(BF16) for q in query] for side in (even, odd)]
        for q in range(2):
            lanes = slice(128 * q, 128 * q + 128)
            both = [jnp.concatenate([a[:, lanes] for a in side], axis=1) for side in query_sides]
            both = jnp.concatenate(both, axis=0)
            logits = dot_t(both, jnp.concatenate([a[:, lanes] for a in key], axis=1))
            one, two = logits[:local], logits[local:]
            folded = jnp.where(
                low,
                jnp.where(first, one, pltpu.roll(one, 64, 1)),
                jnp.where(first, pltpu.roll(two, 64, 1), two),
            )
            out = slice(256 * n + 128 * q, 256 * n + 128 * q + 128)
            for i in range(planes):
                part_ref[i, :, out] = folded[i * own : (i + 1) * own]
    plane = place // PLANE
    for s, target in enumerate(outs):
        target[...] = part_ref[(plane + s) % planes]


def add_kernel(*refs):
    parts = [ref[...] for ref in refs[:-1]]
    while len(parts) > 1:
        parts = [a + b for a, b in zip(parts[::2], parts[1::2])]
    refs[-1][...] = parts[0]


def row_value_kernel(
    columns, place_ref, x_ref, y_ref, w_ref, mine_ref, other_ref, out_ref, next_ref, spread_ref
):
    core = place_ref[0] % 2
    out_ref[...] = dot(x_ref[...], w_ref[...]).astype(BF16)
    next_ref[...] = dot(y_ref[...], w_ref[...]).astype(BF16)
    rows = x_ref.shape[0] // columns
    quarter = columns // PLANE
    for source, index in ((mine_ref, core), (other_ref, 1 - core)):
        for r in range(rows):
            for y in range(2):
                start = pl.multiple_of(r * columns + y * columns // 2 + quarter * core, quarter)
                piece = source[pl.ds(start, quarter), :].astype(F32)
                target = pl.ds(2 * rows * quarter * y + index * rows + r, quarter, stride=2 * rows)
                for p in range(piece.shape[1] // 128):
                    spread_ref[p, target, :] = piece[:, 128 * p : 128 * p + 128]


def row_softmax_kernel(scale, mine_ref, other_ref, live_ref, out_ref):
    own, width = out_ref.shape
    live = live_ref[...] > 0.5
    low = iota((own, 128), 1) < 64
    for p in range(width // 128):
        lanes = slice(128 * p, 128 * p + 128)
        tied = jnp.where(live, (mine_ref[:, lanes] + other_ref[:, lanes]) * scale, NEG)
        top_low = jnp.max(jnp.where(low, tied, 2 * NEG), axis=1, keepdims=True)
        top_high = jnp.max(jnp.where(low, 2 * NEG, tied), axis=1, keepdims=True)
        value = jnp.exp(tied - jnp.where(low, top_low, top_high))
        sum_low = jnp.sum(jnp.where(low, value, 0.0), axis=1, keepdims=True)
        sum_high = jnp.sum(jnp.where(low, 0.0, value), axis=1, keepdims=True)
        out_ref[:, lanes] = (value / jnp.where(low, sum_low, sum_high)).astype(BF16)


def row_output_kernel(
    steps,
    place_ref,
    same_ref,
    value_ref,
    other_ref,
    x_ref,
    w_ref,
    gain_ref,
    *refs,
):
    planes = (len(refs) - 4) // 2
    pieces, after_ref, outs = refs[:planes], refs[planes], refs[planes + 1 : -3]
    mixed_ref, folded_ref, normed_ref = refs[-3:]
    columns = same_ref.shape[1]
    tokens, width = after_ref.shape
    rows = tokens // columns
    quarter, local = columns // PLANE, columns // 2
    place = place_ref[0]
    core, plane = place % 2, place // PLANE
    own = local // planes
    for s, piece in zip(steps, pieces):
        folded_ref[(plane + planes - s) % planes] = piece[...].astype(F32)
    same = same_ref[...] > 0.5
    low = iota((local, columns), 1) < 64
    even, odd = half_masks(256 * rows)
    even, odd = even.astype(BF16), odd.astype(BF16)
    spots = [core * rows + r for r in range(rows)] + [(1 - core) * rows + r for r in range(rows)]
    for p in range(width // 128):
        lanes = slice(128 * p, 128 * p + 128)
        piece = folded_ref[:, :, lanes].reshape(local, 128)
        turned = pltpu.roll(piece, 64, 1)
        one = jnp.where(same, jnp.where(low, piece, turned), 0.0)
        two = jnp.where(same, jnp.where(low, turned, piece), 0.0)
        weights = jnp.concatenate([one, two], axis=1).astype(BF16)
        value = jnp.concatenate(
            [
                source[r * columns : (r + 1) * columns, lanes]
                for source in (value_ref, other_ref)
                for r in range(rows)
            ],
            axis=1,
        )
        value = jnp.concatenate([value * even, value * odd], axis=0)
        mixed = dot(weights, value)
        for i, spot in enumerate(spots):
            mixed_ref[p, pl.ds(spot, local, stride=2 * rows), :] = mixed[:, 128 * i : 128 * i + 128]
    after = (flat(x_ref) + dot(flat(mixed_ref).astype(BF16), w_ref[...])).astype(BF16)
    after_ref[...] = after
    normed_ref[...] = norm(after.astype(F32), gain_ref[...])
    size = tokens // len(outs)
    for s, out in enumerate(outs):
        start = pl.multiple_of(((plane + s) % len(outs)) * size, size)
        out[...] = normed_ref[pl.ds(start, size), :].astype(BF16)


def pack_kernel(*refs):
    for i, source in enumerate(refs[:-1]):
        refs[-1][i] = source[...]


def block_of(own):
    return 4 if own % 4 == 0 else own


def heads_of(place_ref, wide):
    return pl.ds(pl.multiple_of(place_ref[0] % 2 * wide, 128), wide)


def column_project_kernel(scale, steps, columns, depth_ref, prot_ref, place_ref, wq_ref, wk_ref, wv_ref, *refs):
    planes = len(steps)
    ins, (live_ref, even_ref, odd_ref, key_ref, value_ref, all_ref) = refs[:planes], refs[planes:]
    gather_tokens(ins, columns, all_ref)
    wide = key_ref.shape[1]
    heads = heads_of(place_ref, wide)
    query = dot(all_ref[...], wq_ref[:, heads]).astype(BF16).astype(F32) * scale
    for side, out in zip(half_masks(wide), (even_ref, odd_ref)):
        out[...] = (query * side).astype(BF16)
    for w_ref, out in ((wk_ref, key_ref), (wv_ref, value_ref)):
        out[...] = dot(all_ref[...], w_ref[:, heads]).astype(BF16)
    slots, local = 2 * planes, columns // 2
    own = local // planes
    rows = ins[0].shape[0] // own
    block = block_of(own)
    piece = block * rows
    chunk = slots * piece
    pair = 8 // rows
    place = place_ref[0]
    core, line, plane = place % 2, (place // 2) % 2, place // PLANE
    lane = (iota((8, 2 * chunk), 1) % piece) // rows
    level = iota((8, 2 * chunk), 0)
    fits = level // rows == lane % pair
    for g in range(own // block):
        depth = jnp.zeros((8, 2 * chunk), jnp.int32)
        for c in range(block):
            index = plane * own + g * block + c
            column = index % (local // 2) + (local // 2) * line + local * (index // (local // 2))
            depth = jnp.where(lane == c, depth_ref[prot_ref[column]], depth)
        for i in range(slots):
            away = ((plane + planes - steps[i % planes]) % planes) * 2 + (core if i < planes else 1 - core)
            live_ref[g, i] = jnp.where(fits & (level % rows + away * rows < depth), 1.0, 0.0)


def gather_tokens(sources, columns, all_ref):
    planes = len(sources)
    own = columns // 2 // planes
    piece = block_of(own) * sources[0].shape[0] // own
    for g in range(own // block_of(own)):
        for i, source in enumerate(sources):
            start = (g * planes + i) * piece
            all_ref[start : start + piece, :] = source[g * piece : (g + 1) * piece, :]


def column_kernel(
    scale,
    columns,
    place_ref,
    wq_ref,
    wk_ref,
    wv_ref,
    live_ref,
    even_ref,
    odd_ref,
    key_ref,
    value_ref,
    other_ref,
    keep_ref,
    send_ref,
    all_ref,
    mixed_ref,
):
    planes, size, width = other_ref.shape
    wide = width // 2
    slots, local = 2 * planes, columns // 2
    own = local // planes
    rows = size // own
    block = block_of(own)
    piece = block * rows
    chunk = slots * piece
    chunks = own // block
    fold = piece // 8
    pair = 8 // rows
    gather_tokens([other_ref.at[i] for i in range(planes)], columns, all_ref)
    heads = heads_of(place_ref, wide)
    half = chunk // 2

    def woven(mine, other):
        parts = []
        for start in range(0, planes * size, half):
            parts += [mine[start : start + half], other[start : start + half]]
        return jnp.concatenate(parts, axis=0)

    query = dot(all_ref[...], wq_ref[:, heads]).astype(BF16).astype(F32) * scale
    sides = [
        woven(mine_ref[...], (query * side).astype(BF16))
        for mine_ref, side in zip((even_ref, odd_ref), half_masks(wide))
    ]
    key = woven(key_ref[...], dot(all_ref[...], wk_ref[:, heads]).astype(BF16))
    value = woven(value_ref[...], dot(all_ref[...], wv_ref[:, heads]).astype(BF16))
    unit = jnp.where(iota((128, 128), 0) == iota((128, 128), 1), 1.0, 0.0).astype(BF16)
    lane = (iota((8, 2 * chunk), 1) % piece) // rows
    mine = [jnp.where(lane // pair == v, 1.0, 0.0)[None] for v in range(fold)]
    lives = [live_ref[g] > 0.5 for g in range(chunks)]
    packs, values = [], []
    for q in range(wide // 128):
        lanes = slice(128 * q, 128 * q + 128)
        for g in range(chunks):
            part = slice(g * chunk, g * chunk + chunk)
            both = jnp.concatenate([side[part, lanes] for side in sides], axis=0)
            scores = dot_t(key[part, lanes], both).reshape(slots, fold, 8, 2 * chunk)
            packed = scores[:, 0]
            for v in range(1, fold):
                packed = jnp.where(mine[v] > 0.5, scores[:, v], packed)
            packs.append(jnp.where(lives[g], packed, NEG))
        values.append(dot_t(unit, value[:, lanes]).astype(BF16))
    packs = [jnp.exp(packed - jnp.max(packed, axis=(0, 1), keepdims=True)) for packed in packs]
    packs = [packed * (1.0 / jnp.sum(packed, axis=(0, 1), keepdims=True)) for packed in packs]
    for q, value in enumerate(values):
        for g in range(chunks):
            part = slice(g * chunk, g * chunk + chunk)
            weight = packs[q * chunks + g]
            spread = jnp.stack([weight * m for m in mine], axis=1).reshape(chunk, 2 * chunk).astype(BF16)
            for s in range(2):
                mixed = dot(value[64 * s : 64 * s + 64, part], spread[:, s * chunk : (s + 1) * chunk])
                mixed_ref[128 * q + 64 * s : 128 * q + 64 * s + 64, part] = mixed.astype(BF16)
    turn = jnp.where(iota((chunk, chunk), 0) == iota((chunk, chunk), 1), 1.0, 0.0).astype(BF16)
    for g in range(chunks):
        mixed = dot_t(turn, mixed_ref[:, g * chunk : (g + 1) * chunk])
        for i in range(slots):
            target = keep_ref if i < planes else send_ref
            target[i % planes, g * piece : (g + 1) * piece, :] = mixed[i * piece : (i + 1) * piece].astype(BF16)


def join_kernel(place_ref, keep_ref, other_ref, *outs):
    wide = keep_ref.shape[2]
    core = place_ref[0] % 2

    def write(left, right):
        for s, out in enumerate(outs):
            out[:, :wide] = left[s]
            out[:, wide:] = right[s]

    @pl.when(core == 0)
    def _():
        write(keep_ref, other_ref)

    @pl.when(core == 1)
    def _():
        write(other_ref, keep_ref)


def column_output_kernel(steps, place_ref, w_ref, after_ref, *refs):
    ins, (keep_ref, send_ref, total_ref) = refs[:-3], refs[-3:]
    rows, local, _ = keep_ref.shape
    core, plane = place_ref[0] % 2, place_ref[0] // PLANE
    size = ins[0].shape[0]
    total = dot(jnp.concatenate([source[...] for source in ins], axis=0), w_ref[...])
    for i, s in enumerate(steps):
        start = pl.multiple_of(((plane + s) % len(ins)) * size, size)
        for p in range(total.shape[1] // 128):
            total_ref[p, pl.ds(start, size), :] = total[i * size : (i + 1) * size, 128 * p : 128 * p + 128]
    for p in range(total.shape[1] // 128):
        lanes = slice(128 * p, 128 * p + 128)
        total_ref[p] = total_ref[p] + after_ref[:, lanes].astype(F32)
        for r in range(rows):
            for target, index in ((keep_ref, core), (send_ref, 1 - core)):
                row = total_ref[p, pl.ds(index * rows + r, local, stride=2 * rows), :]
                target[r, :, lanes] = row.astype(BF16)


def place_half(source, out_ref, index, sems):
    quarter = source.shape[1] // 2
    copies = []
    for y in range(2):
        start = pl.multiple_of(y * 2 * quarter + index * quarter, quarter)
        copies.append(
            pltpu.make_async_copy(
                source.at[:, y * quarter : (y + 1) * quarter, :],
                out_ref.at[:, pl.ds(start, quarter), :],
                sems.at[y],
            )
        )
    for copy in copies:
        copy.start()
    for copy in copies:
        copy.wait()


def own_half_kernel(place_ref, mine_ref, out_ref, sems):
    place_half(mine_ref, out_ref, place_ref[0] % 2, sems)


def assemble_kernel(place_ref, other_ref, half_ref, out_ref, sems):
    place_half(other_ref, out_ref, 1 - place_ref[0] % 2, sems)


def hbm(array):
    return pltpu.with_memory_space_constraint(array, pltpu.HBM)


def swap(array, offset):
    devices = lax.axis_size("seq")
    return lax.ppermute(array, "seq", [(i, i ^ offset) for i in range(devices)])


def spin_pairs(step):
    planes = lax.axis_size("seq") // PLANE
    pairs = []
    for z in range(planes):
        for y in range(2):
            for k in range(2):
                pairs.append((z * PLANE + 2 * y + k, (z + step) % planes * PLANE + 2 * k + y))
    return pairs


def far_first(planes):
    return sorted(range(planes), key=lambda s: (-min(s, planes - s), s))


def shift(array, step):
    devices = lax.axis_size("seq")
    if step == 0:
        return array
    return lax.ppermute(array, "seq", [(i, (i + PLANE * step) % devices) for i in range(devices)])


def spin(array, step):
    return lax.ppermute(array, "seq", spin_pairs(step))


def spin_back(array, step):
    return lax.ppermute(array, "seq", [(b, a) for a, b in spin_pairs(step)])


def per_device(
    alignment,
    protein_id,
    row_depth,
    row_gain,
    row_query,
    row_key,
    row_value,
    row_output,
    column_gain,
    column_query,
    column_key,
    column_value,
    column_output,
):
    rows, columns, width = alignment.shape
    devices = lax.axis_size("seq")
    place = lax.axis_index("seq").astype(jnp.int32)[None]
    total_rows = rows * devices
    head_size = width // H
    tokens = rows * columns
    planes, local = devices // PLANE, columns // 2
    size = tokens // planes
    sum_steps = back_steps = share_steps = far_first(planes)
    move_steps = [s for s in (1, 0) if s < planes] + [s for s in back_steps if s > 1]
    x = alignment.reshape(tokens, width)
    shape = jax.ShapeDtypeStruct
    square = 2 * tokens * width * width

    part = shape((local // planes, width), F32)
    matrix = shape((width, width), BF16)
    sibling = swap(x, 1)
    normed, query, key, row_query, row_key, same, seen, live = call(
        functools.partial(row_own_kernel, columns),
        (shape((tokens, width), BF16), shape((tokens // 2, width), BF16), shape((tokens, width), BF16), matrix, matrix)
        + (shape((local, columns), F32), shape((columns, columns), F32), shape((local // planes, columns), F32)),
        "shhhhhh",
        "v" * 8,
        [
            pltpu.VMEM((tokens, width), BF16),
            pltpu.VMEM((width,), F32),
            pltpu.SMEM(row_depth.shape, jnp.int32),
            pltpu.VMEM((columns,), jnp.int32),
            pltpu.VMEM((planes, local // planes, columns), F32),
            pltpu.SemaphoreType.DMA((4 + 2 * (width // 256),)),
        ],
        (3 * square // 2, 4 * width * width, tokens),
        "row_own",
    )(place, hbm(x), hbm(row_gain), hbm(row_query), hbm(row_key), hbm(row_depth), hbm(protein_id))
    *pieces, normed_other = call(
        row_scores_kernel,
        (part,) * planes + (shape((tokens, width), BF16),),
        "s" + "v" * 8,
        "v" * (planes + 1),
        [pltpu.VMEM((planes, local // planes, width), F32)],
        (3 * square // 2, 4 * width * width, tokens),
        "row_scores",
    )(place, sibling, row_gain, row_query, row_key, query, key, same, seen)
    column_query, column_key, column_value, late, normed = lax.optimization_barrier(
        (column_query, column_key, column_value, x, normed)
    )
    (total,) = call(
        add_kernel, (part,), "v" * planes, "v", [], (columns * width, 2 * columns * width, 0), "add"
    )(*[shift(pieces[s], s) for s in sum_steps])
    other_total = swap(total, 2)
    normed, _ = lax.optimization_barrier((normed, total))
    value, value_other, spread = call(
        functools.partial(row_value_kernel, columns),
        (shape((tokens, width), BF16),) * 2 + (shape((width // 128, tokens, 128), F32),),
        "svvvvv",
        "vvv",
        [],
        (2 * square, 2 * width * width, 0),
        "row_value",
    )(place, normed, normed_other, row_value, late, sibling)
    live, value = lax.optimization_barrier((live, value))
    (weights,) = call(
        functools.partial(row_softmax_kernel, 1.0 / (math.sqrt(head_size) * math.sqrt(total_rows))),
        (shape((local // planes, width), BF16),),
        "vvv",
        "v",
        [],
        (columns * width, 2 * columns * width, columns * width // 8),
        "row_softmax",
    )(total, other_total, live)
    shared = [shift(weights, s) for s in share_steps]
    after, *blocks = call(
        functools.partial(row_output_kernel, share_steps),
        (shape((tokens, width), BF16),) + (shape((size, width), BF16),) * planes,
        "s" + "v" * (6 + planes),
        "v" * (1 + planes),
        [
            pltpu.VMEM((width // 128, tokens, 128), F32),
            pltpu.VMEM((planes, local // planes, width), F32),
            pltpu.VMEM((tokens, width), F32),
        ],
        (square, 2 * width * width, tokens),
        "row_output",
    )(place, same, value, value_other, spread, row_output, column_gain[None], *shared)
    moved = [spin(blocks[s], s) for s in move_steps]
    wide = width // 2
    (packed,) = call(
        pack_kernel,
        (shape((planes, size, width), BF16),),
        "v" * planes,
        "v",
        [],
        (tokens * width, 4 * tokens * width, 0),
        "pack",
    )(*moved)
    block = block_of(local // planes)
    chunk = 2 * planes * block * 2 * rows
    scale = 1.0 / math.sqrt(head_size)
    ours = call(
        functools.partial(column_project_kernel, scale, move_steps, columns),
        (shape((local // planes // block, 2 * planes, 8, 2 * chunk), F32),) + (shape((tokens, wide), BF16),) * 4,
        "sssvvv" + "v" * planes,
        "v" * 5,
        [pltpu.VMEM((tokens, width), BF16)],
        (3 * square // 2, 3 * width * width, 0),
        "column_project",
    )(row_depth, protein_id, place, column_query, column_key, column_value, *moved)
    halves = shape((planes, size, wide), BF16)
    keep, send = call(
        functools.partial(column_kernel, scale, columns),
        (halves, halves),
        "s" + "v" * 9,
        "vv",
        [pltpu.VMEM((tokens, width), BF16), pltpu.VMEM((wide, 2 * tokens), BF16)],
        (4 * square, 6 * width * width, H * tokens * tokens // 4),
        "column_attention",
    )(place, column_query, column_key, column_value, *ours, swap(packed, 1))
    joined = call(
        join_kernel,
        (shape((size, width), BF16),) * planes,
        "svv",
        "v" * planes,
        [],
        (tokens * width, 4 * tokens * width, 0),
        "join",
    )(place, keep, swap(send, 1))
    returned = [spin_back(joined[move_steps.index(s)], s) for s in back_steps]
    half = shape((rows, local, width), BF16)
    keep, send = call(
        functools.partial(column_output_kernel, back_steps),
        (half, half),
        "svv" + "v" * planes,
        "vv",
        [pltpu.VMEM((width // 128, tokens, 128), F32)],
        (square, 2 * width * width, 0),
        "column_output",
    )(place, column_output, after, *returned)
    whole = shape((rows, columns, width), BF16)
    cost = (tokens * width, 2 * tokens * width, 0)
    two = [pltpu.SemaphoreType.DMA((2,))]
    (begun,) = call(own_half_kernel, (whole,), "sv", "h", two, cost, "own_half")(place, keep)
    (out,) = call(assemble_kernel, (whole,), "svh", "h", two, cost, "assemble", {2: 0})(
        place, swap(send, 1), begun
    )
    return out


def solution(mesh):
    return jax.shard_map(
        per_device,
        mesh=mesh,
        in_specs=(P(("grp", "seq"), None, None), P("grp"), P("grp")) + (P(),) * 10,
        out_specs=P(("grp", "seq"), None, None),
        check_vma=False,
    )
```
